256 devices in a mesh: cuts: 16 (over z_lo, y, core), col: 16 (over z_hi, x).
Axes of the slice: x: 4, y: 4, z: 8 (z_hi: 4, z_lo: 2; z = z_hi * 2 + z_lo), core: 2. Of those that a mesh axis runs over, the one named last changes fastest.
Arguments:
- data: bfloat16 [16, 64, 64, 1024], P('cuts', None, 'col'), may hold values from -12 to 12
- weights: float32 [16, 64], replicated, may hold values from 0.5 to 2
- mixing: float32 [64, 64], replicated, may hold values from -0.4 to 2.9
Outputs:
- factor: float32 [64, 64, 1024], P(None, 'col')
- updated: float32 [16, 64], P('cuts')
The draws below stay inside these ranges and needn't reach their ends.
All inputs are finite; a program needn't handle non-finite values.
Results may differ from the reference program's by a relative error of at most 0.0029.
Values sent between devices are 32-bit elements; how exact they have to be, the bound alone decides.
A program may use at most 64 MiB of HBM per device.

```python
import math
import jax
import jax.numpy as jnp
from jax import lax

R = 64
GRID = 32
PLANE = 1024
ITERS = 3
NZ = 64
SCANS = 16


def draw_mixing(key, part):
    folded = jax.random.fold_in(key, 11)
    first_key, second_key = jax.random.split(folded)
    diagonal = jax.random.uniform(first_key, (R,), jnp.float32, 1.5, 2.5)
    offdiag = jax.random.normal(second_key, (R, R), jnp.float32) * (0.6 / math.sqrt(R))
    offdiag = jnp.clip(offdiag, -0.4, 0.4) * (1.0 - jnp.eye(R, dtype=jnp.float32))
    return offdiag + jnp.diag(diagonal)


def with_spikes(drawn, key, source, target, parts, factor):
    def block_of(dim):
        return (jnp.arange(drawn.shape[dim]) // (drawn.shape[dim] // parts)).reshape((-1,) + (1,) * (drawn.ndim - 1 - dim))

    first = jax.random.permutation(key, parts)[block_of(target)]
    far = (block_of(target) + parts // 2) % parts
    return jnp.where((block_of(source) == first) | (block_of(source) == far), factor * drawn, drawn)


def block_scale(rng, shape, pieces, low, top_value):
    gain, own = 1.0, jax.random.fold_in(rng, 6)
    for position, parts in pieces:
        draws = jnp.exp(jax.random.uniform(jax.random.fold_in(own, position), (parts,), jnp.float32, low / len(pieces), top_value / len(pieces)))
        gain = gain * jnp.repeat(draws, shape[position] // parts).reshape([-1 if axis == position else 1 for axis in range(len(shape))])
    return gain


def noise_with(key, dims, scale, reach, cuts, heavy, held_as=jnp.bfloat16):
    result = scale * jax.random.normal(key, dims, jnp.float32)
    if cuts:
        result = result * block_scale(key, dims, cuts, -0.22, 0.18)
    return jnp.clip(with_spikes(result, jax.random.fold_in(key, 3), *heavy), -reach, reach).astype(held_as)


def setup_inputs(seed: int = 0) -> dict:
    splits = jax.random.split(jax.random.key(seed), 4)
    return {
        "data": noise_with(splits[0], (SCANS, R, NZ, PLANE), 2.0, 12.0, ((0, 16), (2, 16)), (0, 1, 16, 2.0)),
        "weights": jnp.clip(jnp.exp(jax.random.uniform(splits[1], (SCANS, R), jnp.float32, math.log(0.5), math.log(2.0))), 0.5, 2.0),
        "mixing": draw_mixing(jax.random.fold_in(splits[3], 71), 0),
    }


strength = 0.5
highest = lax.Precision.HIGHEST
low_edge = 1.0
high_edge = 1.0 + 12.0 * strength
centre = (high_edge + low_edge) / 2.0
spread = (high_edge - low_edge) / 2.0

def operate(extended):
    channels, depth, cells = extended.shape
    edge = cells // GRID * 0 + GRID
    interior = extended[:, 1:-1]
    column = jnp.arange(cells, dtype=jnp.int32) % edge
    has_left = (column > 0).astype(jnp.float32)
    has_right = (column < edge - 1).astype(jnp.float32)
    left_part = jnp.pad(interior, ((0, 0), (0, 0), (1, 0)))[:, :, :-1] * has_left
    right_part = jnp.pad(interior, ((0, 0), (0, 0), (0, 1)))[:, :, 1:] * has_right
    upper_part = jnp.pad(interior, ((0, 0), (0, 0), (edge, 0)))[:, :, :-edge]
    lower_part = jnp.pad(interior, ((0, 0), (0, 0), (0, edge)))[:, :, edge:]
    neighbours = extended[:, 2:] + extended[:, :-2]
    neighbours = neighbours + left_part + right_part + upper_part + lower_part
    return interior + strength * (6.0 * interior - neighbours)

def reference(data, weights, mixing):
    scan_count = data.shape[0]
    mix_gram = jnp.dot(mixing.T, mixing, precision=highest)
    weight_gram = jnp.dot(weights.T, weights, precision=highest)
    lower_factor = jnp.linalg.cholesky(mix_gram * weight_gram)
    scaled = (mixing[None, :, :] * weights[:, None, :]).reshape(scan_count * R, R)
    coefficients = jax.scipy.linalg.cho_solve((lower_factor, True), scaled.T).T.astype(jnp.bfloat16)
    stacked = data.reshape(scan_count * R, NZ * PLANE)
    source = lax.dot_general(coefficients.astype(jnp.float32), stacked.astype(jnp.float32), (((0,), (0,)), ((), ())), preferred_element_type=jnp.float32)
    source = source.reshape(R, NZ, PLANE)
    solution = jnp.zeros_like(source)
    residual = source
    direction = source / centre
    ratio = spread / centre
    for iteration in range(ITERS):
        solution = solution + direction
        extended = jnp.pad(direction, ((0, 0), (1, 1), (0, 0)))
        residual = residual - operate(extended)
        ratio_next = 1.0 / (2.0 * centre / spread - ratio)
        direction = ratio_next * ratio * direction + 2.0 * ratio_next / spread * residual
        ratio = ratio_next
    factor = solution + direction
    factor_flat = factor.reshape(R, NZ * PLANE)
    factor_half = factor_flat.astype(jnp.bfloat16)
    factor_gram = jnp.dot(factor_flat, factor_flat.T, precision=highest)

    def project(single):
        return lax.dot_general(single.reshape(R, NZ * PLANE).astype(jnp.float32), factor_half.astype(jnp.float32), (((1,), (1,)), ((), ())), preferred_element_type=jnp.float32)
    products = lax.map(project, data)
    targets = jnp.sum(mixing[None, :, :] * products, axis=1)
    lower_next = jnp.linalg.cholesky(mix_gram * factor_gram)
    updated = jax.scipy.linalg.cho_solve((lower_next, True), targets.T).T
    return (factor, updated)
```

```python
import jax
import jax.numpy as jnp
from jax import lax
from jax.sharding import PartitionSpec as P

GRID = 32
ITERS = 3


strength = 0.5
highest = lax.Precision.HIGHEST
low_edge = 1.0
high_edge = 1.0 + 12.0 * strength
centre = (high_edge + low_edge) / 2.0
spread = (high_edge - low_edge) / 2.0


def extended_2(cells, sides, width):
    for axis, dim in sides:
        count = lax.axis_size(axis)
        ends = count - 1
        head = lax.slice_in_dim(cells, 0, width, axis=dim)
        tail = lax.slice_in_dim(cells, cells.shape[dim] - width, cells.shape[dim], axis=dim)
        cells = jnp.concatenate(
            [
                lax.ppermute(tail, axis, [(i, (i + 1) % count) for i in range(ends)]),
                cells,
                lax.ppermute(head, axis, [((i + 1) % count, i) for i in range(ends)]),
            ],
            axis=dim,
        )
    return cells


def split_up(shard, dim, devices):
    before, after = (shard.shape[:dim], shard.shape[dim + 1 :])
    return jnp.moveaxis(shard.reshape(*before, devices, -1, *after), dim, 0)


def sent_and_summed(shard, axis, dim):
    tiles = split_up(shard, dim, lax.axis_size(axis))
    arrived = lax.all_to_all(tiles, axis, split_axis=0, concat_axis=0, tiled=True)
    return arrived.sum(axis=0)


def joined_along(tiles, dim):
    dims = list(tiles.shape[1:])
    dims[dim] *= tiles.shape[0]
    return jnp.moveaxis(tiles, 0, dim).reshape(dims)


def from_everyone(shard, axis):
    devices = lax.axis_size(axis)
    return lax.all_to_all(
        jnp.broadcast_to(shard[None], (devices, *shard.shape)), axis, 0, 0, tiled=True
    )


def gather_directly(shard, axis, dim):
    return joined_along(from_everyone(shard, axis), dim)


def taken_together(shard, axis):
    return from_everyone(shard, axis).sum(axis=0)


def packed_total(arrays, axis):
    line, at, done = (jnp.concatenate([a.reshape(-1) for a in arrays]), 0, [])
    running = taken_together(line, axis)
    for a in arrays:
        done.append(running[at : at + a.size].reshape(a.shape))
        at += a.size
    return tuple(done)


def operate(extended):
    channels, depth, cells = extended.shape
    edge = GRID
    interior = extended[:, 1:-1]
    column = jnp.arange(cells, dtype=jnp.int32) % edge
    has_left = (column > 0).astype(jnp.float32)
    has_right = (column < edge - 1).astype(jnp.float32)
    left_part = jnp.pad(interior, ((0, 0), (0, 0), (1, 0)))[:, :, :-1] * has_left
    right_part = jnp.pad(interior, ((0, 0), (0, 0), (0, 1)))[:, :, 1:] * has_right
    upper_part = jnp.pad(interior, ((0, 0), (0, 0), (edge, 0)))[:, :, :-edge]
    lower_part = jnp.pad(interior, ((0, 0), (0, 0), (0, edge)))[:, :, edge:]
    neighbours = extended[:, 2:] + extended[:, :-2]
    neighbours = neighbours + left_part + right_part + upper_part + lower_part
    return interior + strength * (6.0 * interior - neighbours)


def smooth_once(source):
    planes = source.shape[1]
    extended = extended_2(source, (("col", 1),), ITERS)
    first_plane = lax.axis_index("col") * planes - ITERS
    total_planes = planes * lax.axis_size("col")
    levels = first_plane + jnp.arange(planes + 2 * ITERS, dtype=jnp.int32)
    inside = ((levels >= 0) & (levels < total_planes)).astype(jnp.float32)[None, :, None]
    solution = jnp.zeros_like(source)
    residual = extended
    direction = extended / centre
    ratio = spread / centre
    for iteration in range(ITERS):
        margin = ITERS - iteration
        solution = solution + direction[:, margin : margin + planes]
        window = inside[:, iteration + 1 : iteration + 1 + planes + 2 * (margin - 1)]
        residual = (residual[:, 1:-1] - operate(direction)) * window
        ratio_next = 1.0 / (2.0 * centre / spread - ratio)
        direction = ratio_next * ratio * direction[:, 1:-1] + 2.0 * ratio_next / spread * residual
        ratio = ratio_next
    return solution + direction


def smooth(source):
    return smooth_once(source)


def per_device(data, weights, mixing):
    local_scans, ranks, planes, cells = data.shape
    mix_gram = jnp.dot(mixing.T, mixing, precision=highest)
    weight_gram = jnp.dot(weights.T, weights, precision=highest)
    lower_factor = jnp.linalg.cholesky(mix_gram * weight_gram)
    own_weights = lax.dynamic_slice_in_dim(
        weights, lax.axis_index("cuts") * local_scans, local_scans, 0
    )
    scaled = (mixing[None, :, :] * own_weights[:, None, :]).reshape(local_scans * ranks, ranks)
    coefficients = jax.scipy.linalg.cho_solve((lower_factor, True), scaled.T).T.astype(jnp.bfloat16)
    stacked = data.reshape(local_scans * ranks, planes * cells)
    portion = lax.psum_scatter(
        lax.dot_general(
            coefficients, stacked, (((0,), (0,)), ((), ())), preferred_element_type=jnp.float32
        ),
        "cuts",
        scatter_dimension=0,
        tiled=True,
    )
    smoothed = smooth(portion.reshape(-1, planes, cells))
    factor = lax.all_gather(smoothed, "cuts", axis=0, tiled=True)
    factor_flat = factor.reshape(ranks, planes * cells)
    factor_half = factor_flat.astype(jnp.bfloat16)
    factor_gram = jnp.dot(factor_flat, factor_flat.T, precision=highest)
    products = lax.dot_general(
        data.reshape(local_scans, ranks, planes * cells),
        factor_half,
        (((2,), (1,)), ((), ())),
        preferred_element_type=jnp.float32,
    )
    targets = jnp.sum(mixing[None, :, :] * products, axis=1)
    factor_gram, targets = lax.psum((factor_gram, targets), "col")
    lower_next = jnp.linalg.cholesky(mix_gram * factor_gram)
    updated = jax.scipy.linalg.cho_solve((lower_next, True), targets.T).T
    return (factor, updated)


def solution(mesh):
    return jax.shard_map(
        per_device,
        mesh=mesh,
        in_specs=(P("cuts", None, "col", None), P(), P()),
        out_specs=(P(None, "col", None), P("cuts", None)),
        check_vma=False,
    )
```

```python
import jax
import jax.numpy as jnp
from jax import lax
from jax.sharding import PartitionSpec as P

GRID = 32
ITERS = 3


strength = 0.5
highest = lax.Precision.HIGHEST
low_edge = 1.0
high_edge = 1.0 + 12.0 * strength
centre = (high_edge + low_edge) / 2.0
spread = (high_edge - low_edge) / 2.0


def extended_2(cells, sides, width):
    for axis, dim in sides:
        count = lax.axis_size(axis)
        ends = count - 1
        head = lax.slice_in_dim(cells, 0, width, axis=dim)
        tail = lax.slice_in_dim(cells, cells.shape[dim] - width, cells.shape[dim], axis=dim)
        cells = jnp.concatenate(
            [
                lax.ppermute(tail, axis, [(i, (i + 1) % count) for i in range(ends)]),
                cells,
                lax.ppermute(head, axis, [((i + 1) % count, i) for i in range(ends)]),
            ],
            axis=dim,
        )
    return cells


def split_up(shard, dim, devices):
    before, after = (shard.shape[:dim], shard.shape[dim + 1 :])
    return jnp.moveaxis(shard.reshape(*before, devices, -1, *after), dim, 0)


def sent_and_summed(shard, axis, dim):
    tiles = split_up(shard, dim, lax.axis_size(axis))
    arrived = lax.all_to_all(tiles, axis, split_axis=0, concat_axis=0, tiled=True)
    return arrived.sum(axis=0)


def joined_along(tiles, dim):
    dims = list(tiles.shape[1:])
    dims[dim] *= tiles.shape[0]
    return jnp.moveaxis(tiles, 0, dim).reshape(dims)


def from_everyone(shard, axis):
    devices = lax.axis_size(axis)
    return lax.all_to_all(
        jnp.broadcast_to(shard[None], (devices, *shard.shape)), axis, 0, 0, tiled=True
    )


def gather_directly(shard, axis, dim):
    return joined_along(from_everyone(shard, axis), dim)


def taken_together(shard, axis):
    return from_everyone(shard, axis).sum(axis=0)


def packed_total(arrays, axis):
    line, at, done = (jnp.concatenate([a.reshape(-1) for a in arrays]), 0, [])
    running = taken_together(line, axis)
    for a in arrays:
        done.append(running[at : at + a.size].reshape(a.shape))
        at += a.size
    return tuple(done)


def operate(extended):
    channels, depth, cells = extended.shape
    edge = GRID
    interior = extended[:, 1:-1]
    column = jnp.arange(cells, dtype=jnp.int32) % edge
    has_left = (column > 0).astype(jnp.float32)
    has_right = (column < edge - 1).astype(jnp.float32)
    left_part = jnp.pad(interior, ((0, 0), (0, 0), (1, 0)))[:, :, :-1] * has_left
    right_part = jnp.pad(interior, ((0, 0), (0, 0), (0, 1)))[:, :, 1:] * has_right
    upper_part = jnp.pad(interior, ((0, 0), (0, 0), (edge, 0)))[:, :, :-edge]
    lower_part = jnp.pad(interior, ((0, 0), (0, 0), (0, edge)))[:, :, edge:]
    neighbours = extended[:, 2:] + extended[:, :-2]
    neighbours = neighbours + left_part + right_part + upper_part + lower_part
    return interior + strength * (6.0 * interior - neighbours)


def smooth_once(source):
    planes = source.shape[1]
    extended = extended_2(source, (("col", 1),), ITERS)
    first_plane = lax.axis_index("col") * planes - ITERS
    total_planes = planes * lax.axis_size("col")
    levels = first_plane + jnp.arange(planes + 2 * ITERS, dtype=jnp.int32)
    inside = ((levels >= 0) & (levels < total_planes)).astype(jnp.float32)[None, :, None]
    solution = jnp.zeros_like(source)
    residual = extended
    direction = extended / centre
    ratio = spread / centre
    for iteration in range(ITERS):
        margin = ITERS - iteration
        solution = solution + direction[:, margin : margin + planes]
        window = inside[:, iteration + 1 : iteration + 1 + planes + 2 * (margin - 1)]
        residual = (residual[:, 1:-1] - operate(direction)) * window
        ratio_next = 1.0 / (2.0 * centre / spread - ratio)
        direction = ratio_next * ratio * direction[:, 1:-1] + 2.0 * ratio_next / spread * residual
        ratio = ratio_next
    return solution + direction


def smooth(source):
    return smooth_once(source)


def per_device(data, weights, mixing):
    local_scans, ranks, planes, cells = data.shape
    mix_gram = jnp.dot(mixing.T, mixing, precision=highest)
    weight_gram = jnp.dot(weights.T, weights, precision=highest)
    lower_factor = jnp.linalg.cholesky(mix_gram * weight_gram)
    own_weights = lax.dynamic_slice_in_dim(
        weights, lax.axis_index("cuts") * local_scans, local_scans, 0
    )
    scaled = (mixing[None, :, :] * own_weights[:, None, :]).reshape(local_scans * ranks, ranks)
    coefficients = jax.scipy.linalg.cho_solve((lower_factor, True), scaled.T).T.astype(jnp.bfloat16)
    stacked = data.reshape(local_scans * ranks, planes * cells)
    portion = sent_and_summed(
        lax.dot_general(
            coefficients, stacked, (((0,), (0,)), ((), ())), preferred_element_type=jnp.float32
        ),
        "cuts",
        0,
    )
    smoothed = smooth(portion.reshape(-1, planes, cells))
    factor = gather_directly(smoothed, "cuts", 0)
    factor_flat = factor.reshape(ranks, planes * cells)
    factor_half = factor_flat.astype(jnp.bfloat16)
    factor_gram = jnp.dot(factor_flat, factor_flat.T, precision=highest)
    products = lax.dot_general(
        data.reshape(local_scans, ranks, planes * cells),
        factor_half,
        (((2,), (1,)), ((), ())),
        preferred_element_type=jnp.float32,
    )
    targets = jnp.sum(mixing[None, :, :] * products, axis=1)
    half = ranks // 2
    row = lax.broadcasted_iota(jnp.int32, (half, half), 0)
    col = lax.broadcasted_iota(jnp.int32, (half, half), 1)
    top, off, low = (factor_gram[:half, :half], factor_gram[:half, half:], factor_gram[half:, half:])
    folded = jnp.where(row >= col, top, low)
    folded, off, low_diag, targets = packed_total(
        (folded, off, jnp.sum(jnp.where(row == col, low, 0.0), axis=1), targets), "col"
    )
    top = jnp.where(row >= col, folded, folded.T)
    low = jnp.where(row < col, folded, jnp.where(row > col, folded.T, low_diag[:, None]))
    factor_gram = jnp.concatenate(
        [jnp.concatenate([top, off], axis=1), jnp.concatenate([off.T, low], axis=1)], axis=0
    )
    lower_next = jnp.linalg.cholesky(mix_gram * factor_gram)
    updated = jax.scipy.linalg.cho_solve((lower_next, True), targets.T).T
    return (factor, updated)


def solution(mesh):
    return jax.shard_map(
        per_device,
        mesh=mesh,
        in_specs=(P("cuts", None, "col", None), P(), P()),
        out_specs=(P(None, "col", None), P("cuts", None)),
        check_vma=False,
    )
```

```python
import jax
import jax.numpy as jnp
from jax import lax
from jax.sharding import PartitionSpec as P
from jax.experimental import pallas as pl

GRID = 32
ITERS = 3


strength = 0.5
highest = lax.Precision.HIGHEST
low_edge = 1.0
high_edge = 1.0 + 12.0 * strength
centre = (high_edge + low_edge) / 2.0
spread = (high_edge - low_edge) / 2.0


def extended_2(cells, sides, width):
    for axis, dim in sides:
        count = lax.axis_size(axis)
        ends = count - 1
        head = lax.slice_in_dim(cells, 0, width, axis=dim)
        tail = lax.slice_in_dim(cells, cells.shape[dim] - width, cells.shape[dim], axis=dim)
        cells = jnp.concatenate(
            [
                lax.ppermute(tail, axis, [(i, (i + 1) % count) for i in range(ends)]),
                cells,
                lax.ppermute(head, axis, [((i + 1) % count, i) for i in range(ends)]),
            ],
            axis=dim,
        )
    return cells


def split_up(shard, dim, devices):
    before, after = (shard.shape[:dim], shard.shape[dim + 1 :])
    return jnp.moveaxis(shard.reshape(*before, devices, -1, *after), dim, 0)


def sent_and_summed(shard, axis, dim):
    tiles = split_up(shard, dim, lax.axis_size(axis))
    arrived = lax.all_to_all(tiles, axis, split_axis=0, concat_axis=0, tiled=True)
    return arrived.sum(axis=0)


def joined_along(tiles, dim):
    dims = list(tiles.shape[1:])
    dims[dim] *= tiles.shape[0]
    return jnp.moveaxis(tiles, 0, dim).reshape(dims)


def from_everyone(shard, axis):
    devices = lax.axis_size(axis)
    return lax.all_to_all(
        jnp.broadcast_to(shard[None], (devices, *shard.shape)), axis, 0, 0, tiled=True
    )


def gather_directly(shard, axis, dim):
    return joined_along(from_everyone(shard, axis), dim)


def taken_together(shard, axis):
    return from_everyone(shard, axis).sum(axis=0)


def packed_total(arrays, axis):
    line, at, done = (jnp.concatenate([a.reshape(-1) for a in arrays]), 0, [])
    running = taken_together(line, axis)
    for a in arrays:
        done.append(running[at : at + a.size].reshape(a.shape))
        at += a.size
    return tuple(done)


def operate(extended):
    channels, depth, cells = extended.shape
    edge = GRID
    interior = extended[:, 1:-1]
    column = jnp.arange(cells, dtype=jnp.int32) % edge
    has_left = (column > 0).astype(jnp.float32)
    has_right = (column < edge - 1).astype(jnp.float32)
    left_part = jnp.pad(interior, ((0, 0), (0, 0), (1, 0)))[:, :, :-1] * has_left
    right_part = jnp.pad(interior, ((0, 0), (0, 0), (0, 1)))[:, :, 1:] * has_right
    upper_part = jnp.pad(interior, ((0, 0), (0, 0), (edge, 0)))[:, :, :-edge]
    lower_part = jnp.pad(interior, ((0, 0), (0, 0), (0, edge)))[:, :, edge:]
    neighbours = extended[:, 2:] + extended[:, :-2]
    neighbours = neighbours + left_part + right_part + upper_part + lower_part
    return interior + strength * (6.0 * interior - neighbours)


def smooth_once(source):
    planes = source.shape[1]
    extended = extended_2(source, (("col", 1),), ITERS)
    first_plane = lax.axis_index("col") * planes - ITERS
    total_planes = planes * lax.axis_size("col")
    levels = first_plane + jnp.arange(planes + 2 * ITERS, dtype=jnp.int32)
    inside = ((levels >= 0) & (levels < total_planes)).astype(jnp.float32)[None, :, None]
    solution = jnp.zeros_like(source)
    residual = extended
    direction = extended / centre
    ratio = spread / centre
    for iteration in range(ITERS):
        margin = ITERS - iteration
        solution = solution + direction[:, margin : margin + planes]
        window = inside[:, iteration + 1 : iteration + 1 + planes + 2 * (margin - 1)]
        residual = (residual[:, 1:-1] - operate(direction)) * window
        ratio_next = 1.0 / (2.0 * centre / spread - ratio)
        direction = ratio_next * ratio * direction[:, 1:-1] + 2.0 * ratio_next / spread * residual
        ratio = ratio_next
    return solution + direction


def smooth(source):
    return smooth_once(source)


def _eliminate(a_ref, o_ref):
    a = a_ref[...]
    n, w = a.shape
    ri = lax.broadcasted_iota(jnp.int32, (n, w), 0)
    ci = lax.broadcasted_iota(jnp.int32, (n, w), 1)
    rc = lax.broadcasted_iota(jnp.int32, (n, 1), 0)

    def step(j, a):
        rowj = jnp.sum(jnp.where(ri == j, a, 0.0), axis=0, keepdims=True)
        colj = jnp.sum(jnp.where(ci == j, a, 0.0), axis=1, keepdims=True)
        pivot = jnp.sum(jnp.where(rc == j, colj, 0.0), axis=0, keepdims=True)
        rown = rowj / pivot
        return jnp.where(ri == j, rown, a - colj * rown)

    o_ref[...] = lax.fori_loop(0, n, step, a)


def spd_solve(m, b):
    n, k = b.shape
    width = max(128, (n + k + 127) // 128 * 128)
    a = jnp.concatenate([m, b, jnp.zeros((n, width - n - k), m.dtype)], axis=1)
    out = pl.pallas_call(_eliminate, out_shape=jax.ShapeDtypeStruct(a.shape, a.dtype))(a)
    return out[:, n : n + k]


def per_device(data, weights, mixing):
    local_scans, ranks, planes, cells = data.shape
    mix_gram = jnp.dot(mixing.T, mixing, precision=highest)
    weight_gram = jnp.dot(weights.T, weights, precision=highest)
    own_weights = lax.dynamic_slice_in_dim(
        weights, lax.axis_index("cuts") * local_scans, local_scans, 0
    )
    scaled = (mixing[None, :, :] * own_weights[:, None, :]).reshape(local_scans * ranks, ranks)
    coefficients = spd_solve(mix_gram * weight_gram, scaled.T).T.astype(jnp.bfloat16)
    stacked = data.reshape(local_scans * ranks, planes * cells)
    portion = sent_and_summed(
        lax.dot_general(
            coefficients, stacked, (((0,), (0,)), ((), ())), preferred_element_type=jnp.float32
        ),
        "cuts",
        0,
    )
    smoothed = smooth(portion.reshape(-1, planes, cells))
    factor = gather_directly(smoothed, "cuts", 0)
    factor_flat = factor.reshape(ranks, planes * cells)
    factor_half = factor_flat.astype(jnp.bfloat16)
    factor_gram = jnp.dot(factor_flat, factor_flat.T, precision=highest)
    products = lax.dot_general(
        data.reshape(local_scans, ranks, planes * cells),
        factor_half,
        (((2,), (1,)), ((), ())),
        preferred_element_type=jnp.float32,
    )
    targets = jnp.sum(mixing[None, :, :] * products, axis=1)
    half = ranks // 2
    row = lax.broadcasted_iota(jnp.int32, (half, half), 0)
    col = lax.broadcasted_iota(jnp.int32, (half, half), 1)
    top, off, low = (factor_gram[:half, :half], factor_gram[:half, half:], factor_gram[half:, half:])
    folded = jnp.where(row >= col, top, low)
    folded, off, low_diag, targets = packed_total(
        (folded, off, jnp.sum(jnp.where(row == col, low, 0.0), axis=1), targets), "col"
    )
    top = jnp.where(row >= col, folded, folded.T)
    low = jnp.where(row < col, folded, jnp.where(row > col, folded.T, low_diag[:, None]))
    factor_gram = jnp.concatenate(
        [jnp.concatenate([top, off], axis=1), jnp.concatenate([off.T, low], axis=1)], axis=0
    )
    updated = spd_solve(mix_gram * factor_gram, targets.T).T
    return (factor, updated)


def solution(mesh):
    return jax.shard_map(
        per_device,
        mesh=mesh,
        in_specs=(P("cuts", None, "col", None), P(), P()),
        out_specs=(P(None, "col", None), P("cuts", None)),
        check_vma=False,
    )
```

```python
import jax
import jax.numpy as jnp
from jax import lax
from jax.sharding import PartitionSpec as P
from jax.experimental import pallas as pl

GRID = 32
ITERS = 3


strength = 0.5
highest = lax.Precision.HIGHEST
low_edge = 1.0
high_edge = 1.0 + 12.0 * strength
centre = (high_edge + low_edge) / 2.0
spread = (high_edge - low_edge) / 2.0


def extended_2(cells, sides, width):
    for axis, dim in sides:
        count = lax.axis_size(axis)
        ends = count - 1
        head = lax.slice_in_dim(cells, 0, width, axis=dim)
        tail = lax.slice_in_dim(cells, cells.shape[dim] - width, cells.shape[dim], axis=dim)
        cells = jnp.concatenate(
            [
                lax.ppermute(tail, axis, [(i, (i + 1) % count) for i in range(ends)]),
                cells,
                lax.ppermute(head, axis, [((i + 1) % count, i) for i in range(ends)]),
            ],
            axis=dim,
        )
    return cells


def split_up(shard, dim, devices):
    before, after = (shard.shape[:dim], shard.shape[dim + 1 :])
    return jnp.moveaxis(shard.reshape(*before, devices, -1, *after), dim, 0)


def sent_and_summed(shard, axis, dim):
    tiles = split_up(shard, dim, lax.axis_size(axis))
    arrived = lax.all_to_all(tiles, axis, split_axis=0, concat_axis=0, tiled=True)
    return arrived.sum(axis=0)


def joined_along(tiles, dim):
    dims = list(tiles.shape[1:])
    dims[dim] *= tiles.shape[0]
    return jnp.moveaxis(tiles, 0, dim).reshape(dims)


def from_everyone(shard, axis):
    devices = lax.axis_size(axis)
    return lax.all_to_all(
        jnp.broadcast_to(shard[None], (devices, *shard.shape)), axis, 0, 0, tiled=True
    )


def gather_directly(shard, axis, dim):
    return joined_along(from_everyone(shard, axis), dim)


def taken_together(shard, axis):
    return from_everyone(shard, axis).sum(axis=0)


def packed_total(arrays, axis):
    line, at, done = (jnp.concatenate([a.reshape(-1) for a in arrays]), 0, [])
    running = taken_together(line, axis)
    for a in arrays:
        done.append(running[at : at + a.size].reshape(a.shape))
        at += a.size
    return tuple(done)


def operate(extended):
    channels, depth, cells = extended.shape
    edge = GRID
    interior = extended[:, 1:-1]
    column = jnp.arange(cells, dtype=jnp.int32) % edge
    has_left = (column > 0).astype(jnp.float32)
    has_right = (column < edge - 1).astype(jnp.float32)
    left_part = jnp.pad(interior, ((0, 0), (0, 0), (1, 0)))[:, :, :-1] * has_left
    right_part = jnp.pad(interior, ((0, 0), (0, 0), (0, 1)))[:, :, 1:] * has_right
    upper_part = jnp.pad(interior, ((0, 0), (0, 0), (edge, 0)))[:, :, :-edge]
    lower_part = jnp.pad(interior, ((0, 0), (0, 0), (0, edge)))[:, :, edge:]
    neighbours = extended[:, 2:] + extended[:, :-2]
    neighbours = neighbours + left_part + right_part + upper_part + lower_part
    return interior + strength * (6.0 * interior - neighbours)


def smooth_once(source):
    planes = source.shape[1]
    extended = extended_2(source, (("col", 1),), ITERS)
    first_plane = lax.axis_index("col") * planes - ITERS
    total_planes = planes * lax.axis_size("col")
    levels = first_plane + jnp.arange(planes + 2 * ITERS, dtype=jnp.int32)
    inside = ((levels >= 0) & (levels < total_planes)).astype(jnp.float32)[None, :, None]
    solution = jnp.zeros_like(source)
    residual = extended
    direction = extended / centre
    ratio = spread / centre
    for iteration in range(ITERS):
        margin = ITERS - iteration
        solution = solution + direction[:, margin : margin + planes]
        window = inside[:, iteration + 1 : iteration + 1 + planes + 2 * (margin - 1)]
        residual = (residual[:, 1:-1] - operate(direction)) * window
        ratio_next = 1.0 / (2.0 * centre / spread - ratio)
        direction = ratio_next * ratio * direction[:, 1:-1] + 2.0 * ratio_next / spread * residual
        ratio = ratio_next
    return solution + direction


def smooth(source):
    return smooth_once(source)


def _eliminate(m_ref, b_ref, o_ref):
    m = m_ref[...]
    b = b_ref[...]
    n = m.shape[0]
    ri = lax.broadcasted_iota(jnp.int32, m.shape, 0)
    ci = lax.broadcasted_iota(jnp.int32, m.shape, 1)
    rb = lax.broadcasted_iota(jnp.int32, b.shape, 0)

    def step(j, carry):
        m, b = carry
        colj = jnp.sum(jnp.where(ci == j, m, 0.0), axis=1, keepdims=True)
        pivot = jnp.sum(jnp.where(ri[:, :1] == j, colj, 0.0), axis=0, keepdims=True)
        rowm = jnp.sum(jnp.where(ri == j, m, 0.0), axis=0, keepdims=True) / pivot
        rowb = jnp.sum(jnp.where(rb == j, b, 0.0), axis=0, keepdims=True) / pivot
        m = jnp.where(ri == j, rowm, m - colj * rowm)
        b = jnp.where(rb == j, rowb, b - colj * rowb)
        return m, b

    o_ref[...] = lax.fori_loop(0, n, step, (m, b), unroll=8)[1]


def spd_solve(m, b):
    return pl.pallas_call(_eliminate, out_shape=jax.ShapeDtypeStruct(b.shape, b.dtype))(m, b)


def per_device(data, weights, mixing):
    local_scans, ranks, planes, cells = data.shape
    mix_gram = jnp.dot(mixing.T, mixing, precision=highest)
    weight_gram = jnp.dot(weights.T, weights, precision=highest)
    own_weights = lax.dynamic_slice_in_dim(
        weights, lax.axis_index("cuts") * local_scans, local_scans, 0
    )
    scaled = (mixing.T[None, :, :] * own_weights[:, :, None]).transpose(1, 0, 2)
    coefficients = spd_solve(mix_gram * weight_gram, scaled.reshape(ranks, local_scans * ranks))
    coefficients = coefficients.astype(jnp.bfloat16)
    stacked = data.reshape(local_scans * ranks, planes * cells)
    portion = sent_and_summed(
        lax.dot_general(
            coefficients, stacked, (((1,), (0,)), ((), ())), preferred_element_type=jnp.float32
        ),
        "cuts",
        0,
    )
    smoothed = smooth(portion.reshape(-1, planes, cells))
    factor = gather_directly(smoothed, "cuts", 0)
    factor_flat = factor.reshape(ranks, planes * cells)
    factor_half = factor_flat.astype(jnp.bfloat16)
    factor_gram = jnp.dot(factor_flat, factor_flat.T, precision=highest)
    products = lax.dot_general(
        data.reshape(local_scans, ranks, planes * cells),
        factor_half,
        (((2,), (1,)), ((), ())),
        preferred_element_type=jnp.float32,
    )
    targets = jnp.sum(mixing[None, :, :] * products, axis=1)
    half = ranks // 2
    row = lax.broadcasted_iota(jnp.int32, (half, half), 0)
    col = lax.broadcasted_iota(jnp.int32, (half, half), 1)
    top, off, low = (factor_gram[:half, :half], factor_gram[:half, half:], factor_gram[half:, half:])
    folded = jnp.where(row >= col, top, low)
    folded, off, low_diag, targets = packed_total(
        (folded, off, jnp.sum(jnp.where(row == col, low, 0.0), axis=1), targets), "col"
    )
    top = jnp.where(row >= col, folded, folded.T)
    low = jnp.where(row < col, folded, jnp.where(row > col, folded.T, low_diag[:, None]))
    factor_gram = jnp.concatenate(
        [jnp.concatenate([top, off], axis=1), jnp.concatenate([off.T, low], axis=1)], axis=0
    )
    updated = spd_solve(mix_gram * factor_gram, targets.T).T
    return (factor, updated)


def solution(mesh):
    return jax.shard_map(
        per_device,
        mesh=mesh,
        in_specs=(P("cuts", None, "col", None), P(), P()),
        out_specs=(P(None, "col", None), P("cuts", None)),
        check_vma=False,
    )
```

```python
import functools
import jax
import jax.numpy as jnp
from jax import lax
from jax.sharding import PartitionSpec as P
from jax.experimental import pallas as pl
from jax.experimental.pallas import tpu as pltpu

MESH = pl.DeviceIdType.MESH

GRID = 32
ITERS = 3


strength = 0.5
highest = lax.Precision.HIGHEST
low_edge = 1.0
high_edge = 1.0 + 12.0 * strength
centre = (high_edge + low_edge) / 2.0
spread = (high_edge - low_edge) / 2.0


def extended_2(cells, sides, width):
    for axis, dim in sides:
        count = lax.axis_size(axis)
        ends = count - 1
        head = lax.slice_in_dim(cells, 0, width, axis=dim)
        tail = lax.slice_in_dim(cells, cells.shape[dim] - width, cells.shape[dim], axis=dim)
        cells = jnp.concatenate(
            [
                lax.ppermute(tail, axis, [(i, (i + 1) % count) for i in range(ends)]),
                cells,
                lax.ppermute(head, axis, [((i + 1) % count, i) for i in range(ends)]),
            ],
            axis=dim,
        )
    return cells


def _exchange_kernel(axis, other, n, whole, x_ref, o_ref, send_sem, recv_sem, own_sem):
    me = lax.axis_index(axis)
    fixed = lax.axis_index(other)

    def where(peer):
        return (peer, fixed) if axis == "cuts" else (fixed, peer)

    def part(peer):
        return x_ref if whole else x_ref.at[peer]

    barrier = pltpu.get_barrier_semaphore()
    for d in range(1, n):
        pl.semaphore_signal(
            barrier, inc=1, device_id=where(lax.rem(me + d, n)), device_id_type=MESH
        )
    pl.semaphore_wait(barrier, n - 1)
    own = pltpu.make_async_copy(part(me), o_ref.at[me], own_sem)
    own.start()
    copies = []
    for d in range(1, n):
        peer = lax.rem(me + d, n)
        copy = pltpu.make_async_remote_copy(
            src_ref=part(peer),
            dst_ref=o_ref.at[me],
            send_sem=send_sem.at[peer],
            recv_sem=recv_sem.at[me],
            device_id=where(peer),
            device_id_type=MESH,
        )
        copy.start()
        copies.append(copy)
    for copy in copies:
        copy.wait_send()
    for d in range(1, n):
        source = lax.rem(me + n - d, n)
        pltpu.make_async_remote_copy(
            src_ref=part(source),
            dst_ref=o_ref.at[source],
            send_sem=send_sem.at[source],
            recv_sem=recv_sem.at[source],
            device_id=where(source),
            device_id_type=MESH,
        ).wait_recv()
    own.wait()


def exchange(x, axis, key, whole=False):
    other = "col" if axis == "cuts" else "cuts"
    n = lax.axis_size(axis)
    shape = (n, *x.shape) if whole else x.shape
    return pl.pallas_call(
        functools.partial(_exchange_kernel, axis, other, n, whole),
        out_shape=jax.ShapeDtypeStruct(shape, x.dtype),
        in_specs=[pl.BlockSpec(memory_space=pltpu.VMEM)],
        out_specs=pl.BlockSpec(memory_space=pltpu.VMEM),
        scratch_shapes=[
            pltpu.SemaphoreType.DMA((n,)),
            pltpu.SemaphoreType.DMA((n,)),
            pltpu.SemaphoreType.DMA,
        ],
        compiler_params=pltpu.CompilerParams(collective_id=key, has_side_effects=True),
    )(x)


def split_up(shard, dim, devices):
    before, after = (shard.shape[:dim], shard.shape[dim + 1 :])
    return jnp.moveaxis(shard.reshape(*before, devices, -1, *after), dim, 0)


def sent_and_summed(shard, axis, dim):
    tiles = split_up(shard, dim, lax.axis_size(axis))
    arrived = exchange(tiles, axis, 0)
    return arrived.sum(axis=0)


def joined_along(tiles, dim):
    dims = list(tiles.shape[1:])
    dims[dim] *= tiles.shape[0]
    return jnp.moveaxis(tiles, 0, dim).reshape(dims)


def from_everyone(shard, axis):
    return exchange(shard, axis, 1 if axis == "cuts" else 2, whole=True)


def gather_directly(shard, axis, dim):
    return joined_along(from_everyone(shard, axis), dim)


def taken_together(shard, axis):
    return from_everyone(shard, axis).sum(axis=0)


def packed_total(arrays, axis):
    line, at, done = (jnp.concatenate([a.reshape(-1) for a in arrays]), 0, [])
    running = taken_together(line, axis)
    for a in arrays:
        done.append(running[at : at + a.size].reshape(a.shape))
        at += a.size
    return tuple(done)


def operate(extended):
    channels, depth, cells = extended.shape
    edge = GRID
    interior = extended[:, 1:-1]
    column = jnp.arange(cells, dtype=jnp.int32) % edge
    has_left = (column > 0).astype(jnp.float32)
    has_right = (column < edge - 1).astype(jnp.float32)
    left_part = jnp.pad(interior, ((0, 0), (0, 0), (1, 0)))[:, :, :-1] * has_left
    right_part = jnp.pad(interior, ((0, 0), (0, 0), (0, 1)))[:, :, 1:] * has_right
    upper_part = jnp.pad(interior, ((0, 0), (0, 0), (edge, 0)))[:, :, :-edge]
    lower_part = jnp.pad(interior, ((0, 0), (0, 0), (0, edge)))[:, :, edge:]
    neighbours = extended[:, 2:] + extended[:, :-2]
    neighbours = neighbours + left_part + right_part + upper_part + lower_part
    return interior + strength * (6.0 * interior - neighbours)


def smooth_once(source):
    planes = source.shape[1]
    extended = extended_2(source, (("col", 1),), ITERS)
    first_plane = lax.axis_index("col") * planes - ITERS
    total_planes = planes * lax.axis_size("col")
    levels = first_plane + jnp.arange(planes + 2 * ITERS, dtype=jnp.int32)
    inside = ((levels >= 0) & (levels < total_planes)).astype(jnp.float32)[None, :, None]
    solution = jnp.zeros_like(source)
    residual = extended
    direction = extended / centre
    ratio = spread / centre
    for iteration in range(ITERS):
        margin = ITERS - iteration
        solution = solution + direction[:, margin : margin + planes]
        window = inside[:, iteration + 1 : iteration + 1 + planes + 2 * (margin - 1)]
        residual = (residual[:, 1:-1] - operate(direction)) * window
        ratio_next = 1.0 / (2.0 * centre / spread - ratio)
        direction = ratio_next * ratio * direction[:, 1:-1] + 2.0 * ratio_next / spread * residual
        ratio = ratio_next
    return solution + direction


def smooth(source):
    return smooth_once(source)


def _eliminate(m_ref, b_ref, o_ref):
    m = m_ref[...]
    b = b_ref[...]
    n = m.shape[0]
    ri = lax.broadcasted_iota(jnp.int32, m.shape, 0)
    ci = lax.broadcasted_iota(jnp.int32, m.shape, 1)
    rb = lax.broadcasted_iota(jnp.int32, b.shape, 0)

    def step(j, carry):
        m, b = carry
        colj = jnp.sum(jnp.where(ci == j, m, 0.0), axis=1, keepdims=True)
        pivot = jnp.sum(jnp.where(ri[:, :1] == j, colj, 0.0), axis=0, keepdims=True)
        rowm = jnp.sum(jnp.where(ri == j, m, 0.0), axis=0, keepdims=True) / pivot
        rowb = jnp.sum(jnp.where(rb == j, b, 0.0), axis=0, keepdims=True) / pivot
        m = jnp.where(ri == j, rowm, m - colj * rowm)
        b = jnp.where(rb == j, rowb, b - colj * rowb)
        return m, b

    o_ref[...] = lax.fori_loop(0, n, step, (m, b), unroll=8)[1]


def spd_solve(m, b):
    return pl.pallas_call(_eliminate, out_shape=jax.ShapeDtypeStruct(b.shape, b.dtype))(m, b)


def per_device(data, weights, mixing):
    local_scans, ranks, planes, cells = data.shape
    mix_gram = jnp.dot(mixing.T, mixing, precision=highest)
    weight_gram = jnp.dot(weights.T, weights, precision=highest)
    own_weights = lax.dynamic_slice_in_dim(
        weights, lax.axis_index("cuts") * local_scans, local_scans, 0
    )
    scaled = (mixing.T[None, :, :] * own_weights[:, :, None]).transpose(1, 0, 2)
    coefficients = spd_solve(mix_gram * weight_gram, scaled.reshape(ranks, local_scans * ranks))
    coefficients = coefficients.astype(jnp.bfloat16)
    stacked = data.reshape(local_scans * ranks, planes * cells)
    portion = sent_and_summed(
        lax.dot_general(
            coefficients, stacked, (((1,), (0,)), ((), ())), preferred_element_type=jnp.float32
        ),
        "cuts",
        0,
    )
    smoothed = smooth(portion.reshape(-1, planes, cells))
    factor = gather_directly(smoothed, "cuts", 0)
    factor_flat = factor.reshape(ranks, planes * cells)
    factor_half = factor_flat.astype(jnp.bfloat16)
    factor_gram = jnp.dot(factor_flat, factor_flat.T, precision=highest)
    products = lax.dot_general(
        data.reshape(local_scans, ranks, planes * cells),
        factor_half,
        (((2,), (1,)), ((), ())),
        preferred_element_type=jnp.float32,
    )
    targets = jnp.sum(mixing[None, :, :] * products, axis=1)
    half = ranks // 2
    row = lax.broadcasted_iota(jnp.int32, (half, half), 0)
    col = lax.broadcasted_iota(jnp.int32, (half, half), 1)
    top, off, low = (factor_gram[:half, :half], factor_gram[:half, half:], factor_gram[half:, half:])
    folded = jnp.where(row >= col, top, low)
    folded, off, low_diag, targets = packed_total(
        (folded, off, jnp.sum(jnp.where(row == col, low, 0.0), axis=1), targets), "col"
    )
    top = jnp.where(row >= col, folded, folded.T)
    low = jnp.where(row < col, folded, jnp.where(row > col, folded.T, low_diag[:, None]))
    factor_gram = jnp.concatenate(
        [jnp.concatenate([top, off], axis=1), jnp.concatenate([off.T, low], axis=1)], axis=0
    )
    updated = spd_solve(mix_gram * factor_gram, targets.T).T
    return (factor, updated)


def solution(mesh):
    return jax.shard_map(
        per_device,
        mesh=mesh,
        in_specs=(P("cuts", None, "col", None), P(), P()),
        out_specs=(P(None, "col", None), P("cuts", None)),
        check_vma=False,
    )
```

```python
import functools
import jax
import jax.numpy as jnp
from jax import lax
from jax.sharding import PartitionSpec as P
from jax.experimental import pallas as pl
from jax.experimental.pallas import tpu as pltpu

MESH = pl.DeviceIdType.MESH

GRID = 32
ITERS = 3


strength = 0.5
highest = lax.Precision.HIGHEST
low_edge = 1.0
high_edge = 1.0 + 12.0 * strength
centre = (high_edge + low_edge) / 2.0
spread = (high_edge - low_edge) / 2.0


def extended_2(cells, sides, width):
    for axis, dim in sides:
        count = lax.axis_size(axis)
        ends = count - 1
        head = lax.slice_in_dim(cells, 0, width, axis=dim)
        tail = lax.slice_in_dim(cells, cells.shape[dim] - width, cells.shape[dim], axis=dim)
        cells = jnp.concatenate(
            [
                lax.ppermute(tail, axis, [(i, (i + 1) % count) for i in range(ends)]),
                cells,
                lax.ppermute(head, axis, [((i + 1) % count, i) for i in range(ends)]),
            ],
            axis=dim,
        )
    return cells


def _exchange_kernel(axis, other, n, whole, x_ref, o_ref, send_sem, recv_sem, own_sem):
    me = lax.axis_index(axis)
    fixed = lax.axis_index(other)

    def where(peer):
        return (peer, fixed) if axis == "cuts" else (fixed, peer)

    def part(peer):
        return x_ref if whole else x_ref.at[peer]

    barrier = pltpu.get_barrier_semaphore()
    for d in range(1, n):
        pl.semaphore_signal(
            barrier, inc=1, device_id=where(lax.rem(me + d, n)), device_id_type=MESH
        )
    pl.semaphore_wait(barrier, n - 1)
    own = pltpu.make_async_copy(part(me), o_ref.at[me], own_sem)
    own.start()
    copies = []
    for d in range(1, n):
        peer = lax.rem(me + d, n)
        copy = pltpu.make_async_remote_copy(
            src_ref=part(peer),
            dst_ref=o_ref.at[me],
            send_sem=send_sem.at[peer],
            recv_sem=recv_sem.at[me],
            device_id=where(peer),
            device_id_type=MESH,
        )
        copy.start()
        copies.append(copy)
    for copy in copies:
        copy.wait_send()
    for d in range(1, n):
        source = lax.rem(me + n - d, n)
        pltpu.make_async_remote_copy(
            src_ref=part(source),
            dst_ref=o_ref.at[source],
            send_sem=send_sem.at[source],
            recv_sem=recv_sem.at[source],
            device_id=where(source),
            device_id_type=MESH,
        ).wait_recv()
    own.wait()


def exchange(x, axis, key, whole=False):
    other = "col" if axis == "cuts" else "cuts"
    n = lax.axis_size(axis)
    shape = (n, *x.shape) if whole else x.shape
    return pl.pallas_call(
        functools.partial(_exchange_kernel, axis, other, n, whole),
        out_shape=jax.ShapeDtypeStruct(shape, x.dtype),
        in_specs=[pl.BlockSpec(memory_space=pltpu.VMEM)],
        out_specs=pl.BlockSpec(memory_space=pltpu.VMEM),
        scratch_shapes=[
            pltpu.SemaphoreType.DMA((n,)),
            pltpu.SemaphoreType.DMA((n,)),
            pltpu.SemaphoreType.DMA,
        ],
        compiler_params=pltpu.CompilerParams(collective_id=key, has_side_effects=True),
    )(x)


def split_up(shard, dim, devices):
    before, after = (shard.shape[:dim], shard.shape[dim + 1 :])
    return jnp.moveaxis(shard.reshape(*before, devices, -1, *after), dim, 0)


def sent_and_summed(shard, axis, dim):
    tiles = split_up(shard, dim, lax.axis_size(axis))
    arrived = exchange(tiles, axis, 0)
    return arrived.sum(axis=0)


def joined_along(tiles, dim):
    dims = list(tiles.shape[1:])
    dims[dim] *= tiles.shape[0]
    return jnp.moveaxis(tiles, 0, dim).reshape(dims)


def from_everyone(shard, axis):
    return exchange(shard, axis, 1 if axis == "cuts" else 2, whole=True)


def gather_directly(shard, axis, dim):
    return joined_along(from_everyone(shard, axis), dim)


def taken_together(shard, axis):
    return from_everyone(shard, axis).sum(axis=0)


def packed_total(arrays, axis):
    line, at, done = (jnp.concatenate([a.reshape(-1) for a in arrays]), 0, [])
    running = taken_together(line, axis)
    for a in arrays:
        done.append(running[at : at + a.size].reshape(a.shape))
        at += a.size
    return tuple(done)


def operate(extended):
    channels, depth, cells = extended.shape
    edge = GRID
    interior = extended[:, 1:-1]
    column = jnp.arange(cells, dtype=jnp.int32) % edge
    has_left = (column > 0).astype(jnp.float32)
    has_right = (column < edge - 1).astype(jnp.float32)
    left_part = jnp.pad(interior, ((0, 0), (0, 0), (1, 0)))[:, :, :-1] * has_left
    right_part = jnp.pad(interior, ((0, 0), (0, 0), (0, 1)))[:, :, 1:] * has_right
    upper_part = jnp.pad(interior, ((0, 0), (0, 0), (edge, 0)))[:, :, :-edge]
    lower_part = jnp.pad(interior, ((0, 0), (0, 0), (0, edge)))[:, :, edge:]
    neighbours = extended[:, 2:] + extended[:, :-2]
    neighbours = neighbours + left_part + right_part + upper_part + lower_part
    return interior + strength * (6.0 * interior - neighbours)


def smooth_once(source):
    planes = source.shape[1]
    extended = extended_2(source, (("col", 1),), ITERS)
    first_plane = lax.axis_index("col") * planes - ITERS
    total_planes = planes * lax.axis_size("col")
    levels = first_plane + jnp.arange(planes + 2 * ITERS, dtype=jnp.int32)
    inside = ((levels >= 0) & (levels < total_planes)).astype(jnp.float32)[None, :, None]
    solution = jnp.zeros_like(source)
    residual = extended
    direction = extended / centre
    ratio = spread / centre
    for iteration in range(ITERS):
        margin = ITERS - iteration
        solution = solution + direction[:, margin : margin + planes]
        window = inside[:, iteration + 1 : iteration + 1 + planes + 2 * (margin - 1)]
        residual = (residual[:, 1:-1] - operate(direction)) * window
        ratio_next = 1.0 / (2.0 * centre / spread - ratio)
        direction = ratio_next * ratio * direction[:, 1:-1] + 2.0 * ratio_next / spread * residual
        ratio = ratio_next
    return solution + direction


def smooth(source):
    return smooth_once(source)


def _eliminate(m_ref, b_ref, o_ref):
    m = m_ref[...]
    b = b_ref[...]
    n = m.shape[0]
    ri = lax.broadcasted_iota(jnp.int32, m.shape, 0)
    ci = lax.broadcasted_iota(jnp.int32, m.shape, 1)
    rb = lax.broadcasted_iota(jnp.int32, b.shape, 0)

    def pick_row(x, rows, p):
        return jnp.sum(jnp.where(rows == p, x, 0.0), axis=0, keepdims=True)

    def pick_col(x, p):
        return jnp.sum(jnp.where(ci[: x.shape[0]] == p, x, 0.0), axis=1, keepdims=True)

    def step(j, carry):
        m, b = carry
        p, q = 2 * j, 2 * j + 1
        c0, c1 = pick_col(m, p), pick_col(m, q)
        r0, r1 = pick_row(m, ri, p), pick_row(m, ri, q)
        s0, s1 = pick_row(b, rb, p), pick_row(b, rb, q)
        a, e = pick_col(r0, p), pick_col(r0, q)
        c, d = pick_col(r1, p), pick_col(r1, q)
        scale = 1.0 / (a * d - e * c)
        n0, n1 = (d * r0 - e * r1) * scale, (a * r1 - c * r0) * scale
        t0, t1 = (d * s0 - e * s1) * scale, (a * s1 - c * s0) * scale
        m = jnp.where(ri == p, n0, jnp.where(ri == q, n1, m - c0 * n0 - c1 * n1))
        b = jnp.where(rb == p, t0, jnp.where(rb == q, t1, b - c0 * t0 - c1 * t1))
        return m, b

    o_ref[...] = lax.fori_loop(0, n // 2, step, (m, b), unroll=4)[1]


def spd_solve(m, b):
    return pl.pallas_call(_eliminate, out_shape=jax.ShapeDtypeStruct(b.shape, b.dtype))(m, b)


def per_device(data, weights, mixing):
    local_scans, ranks, planes, cells = data.shape
    mix_gram = jnp.dot(mixing.T, mixing, precision=highest)
    weight_gram = jnp.dot(weights.T, weights, precision=highest)
    own_weights = lax.dynamic_slice_in_dim(
        weights, lax.axis_index("cuts") * local_scans, local_scans, 0
    )
    scaled = (mixing.T[None, :, :] * own_weights[:, :, None]).transpose(1, 0, 2)
    coefficients = spd_solve(mix_gram * weight_gram, scaled.reshape(ranks, local_scans * ranks))
    coefficients = coefficients.astype(jnp.bfloat16)
    stacked = data.reshape(local_scans * ranks, planes * cells)
    portion = sent_and_summed(
        lax.dot_general(
            coefficients, stacked, (((1,), (0,)), ((), ())), preferred_element_type=jnp.float32
        ),
        "cuts",
        0,
    )
    smoothed = smooth(portion.reshape(-1, planes, cells))
    factor = gather_directly(smoothed, "cuts", 0)
    factor_flat = factor.reshape(ranks, planes * cells)
    factor_half = factor_flat.astype(jnp.bfloat16)
    factor_gram = jnp.dot(factor_flat, factor_flat.T, precision=highest)
    products = lax.dot_general(
        data.reshape(local_scans, ranks, planes * cells),
        factor_half,
        (((2,), (1,)), ((), ())),
        preferred_element_type=jnp.float32,
    )
    targets = jnp.sum(mixing[None, :, :] * products, axis=1)
    half = ranks // 2
    row = lax.broadcasted_iota(jnp.int32, (half, half), 0)
    col = lax.broadcasted_iota(jnp.int32, (half, half), 1)
    top, off, low = (factor_gram[:half, :half], factor_gram[:half, half:], factor_gram[half:, half:])
    folded = jnp.where(row >= col, top, low)
    folded, off, low_diag, targets = packed_total(
        (folded, off, jnp.sum(jnp.where(row == col, low, 0.0), axis=1), targets), "col"
    )
    top = jnp.where(row >= col, folded, folded.T)
    low = jnp.where(row < col, folded, jnp.where(row > col, folded.T, low_diag[:, None]))
    factor_gram = jnp.concatenate(
        [jnp.concatenate([top, off], axis=1), jnp.concatenate([off.T, low], axis=1)], axis=0
    )
    updated = spd_solve(mix_gram * factor_gram, targets.T).T
    return (factor, updated)


def solution(mesh):
    return jax.shard_map(
        per_device,
        mesh=mesh,
        in_specs=(P("cuts", None, "col", None), P(), P()),
        out_specs=(P(None, "col", None), P("cuts", None)),
        check_vma=False,
    )
```

```python
import functools
import jax
import jax.numpy as jnp
from jax import lax
from jax.sharding import PartitionSpec as P
from jax.experimental import pallas as pl
from jax.experimental.pallas import tpu as pltpu

MESH = pl.DeviceIdType.MESH

GRID = 32
ITERS = 3


strength = 0.5
highest = lax.Precision.HIGHEST
low_edge = 1.0
high_edge = 1.0 + 12.0 * strength
centre = (high_edge + low_edge) / 2.0
spread = (high_edge - low_edge) / 2.0


def extended_2(cells, sides, width):
    for axis, dim in sides:
        count = lax.axis_size(axis)
        ends = count - 1
        head = lax.slice_in_dim(cells, 0, width, axis=dim)
        tail = lax.slice_in_dim(cells, cells.shape[dim] - width, cells.shape[dim], axis=dim)
        cells = jnp.concatenate(
            [
                lax.ppermute(tail, axis, [(i, (i + 1) % count) for i in range(ends)]),
                cells,
                lax.ppermute(head, axis, [((i + 1) % count, i) for i in range(ends)]),
            ],
            axis=dim,
        )
    return cells


def _exchange_kernel(axis, other, n, whole, x_ref, o_ref, send_sem, recv_sem, own_sem):
    me = lax.axis_index(axis)
    fixed = lax.axis_index(other)

    def where(peer):
        return (peer, fixed) if axis == "cuts" else (fixed, peer)

    def part(peer):
        return x_ref if whole else x_ref.at[peer]

    barrier = pltpu.get_barrier_semaphore()
    for d in range(1, n):
        pl.semaphore_signal(
            barrier, inc=1, device_id=where(lax.rem(me + d, n)), device_id_type=MESH
        )
    pl.semaphore_wait(barrier, n - 1)
    own = pltpu.make_async_copy(part(me), o_ref.at[me], own_sem)
    own.start()
    copies = []
    for d in range(1, n):
        peer = lax.rem(me + d, n)
        copy = pltpu.make_async_remote_copy(
            src_ref=part(peer),
            dst_ref=o_ref.at[me],
            send_sem=send_sem.at[peer],
            recv_sem=recv_sem.at[me],
            device_id=where(peer),
            device_id_type=MESH,
        )
        copy.start()
        copies.append(copy)
    for copy in copies:
        copy.wait_send()
    for d in range(1, n):
        source = lax.rem(me + n - d, n)
        pltpu.make_async_remote_copy(
            src_ref=part(source),
            dst_ref=o_ref.at[source],
            send_sem=send_sem.at[source],
            recv_sem=recv_sem.at[source],
            device_id=where(source),
            device_id_type=MESH,
        ).wait_recv()
    own.wait()


def exchange(x, axis, key, whole=False):
    other = "col" if axis == "cuts" else "cuts"
    n = lax.axis_size(axis)
    shape = (n, *x.shape) if whole else x.shape
    return pl.pallas_call(
        functools.partial(_exchange_kernel, axis, other, n, whole),
        out_shape=jax.ShapeDtypeStruct(shape, x.dtype),
        in_specs=[pl.BlockSpec(memory_space=pltpu.VMEM)],
        out_specs=pl.BlockSpec(memory_space=pltpu.VMEM),
        scratch_shapes=[
            pltpu.SemaphoreType.DMA((n,)),
            pltpu.SemaphoreType.DMA((n,)),
            pltpu.SemaphoreType.DMA,
        ],
        compiler_params=pltpu.CompilerParams(collective_id=key, has_side_effects=True),
    )(x)


def _halo_kernel(n, head_ref, tail_ref, below_ref, above_ref, send_sem, recv_sem):
    me = lax.axis_index("col")
    fixed = lax.axis_index("cuts")
    has_left = (me + n - 1) // n
    has_right = 1 - me // (n - 1)
    left, right = (fixed, me - has_left), (fixed, me + has_right)

    def to_left():
        return pltpu.make_async_remote_copy(
            src_ref=head_ref, dst_ref=above_ref, send_sem=send_sem.at[0],
            recv_sem=recv_sem.at[1], device_id=left, device_id_type=MESH,
        )

    def to_right():
        return pltpu.make_async_remote_copy(
            src_ref=tail_ref, dst_ref=below_ref, send_sem=send_sem.at[1],
            recv_sem=recv_sem.at[0], device_id=right, device_id_type=MESH,
        )

    barrier = pltpu.get_barrier_semaphore()

    @pl.when(me > 0)
    def _():
        pl.semaphore_signal(barrier, inc=1, device_id=left, device_id_type=MESH)

    @pl.when(me < n - 1)
    def _():
        pl.semaphore_signal(barrier, inc=1, device_id=right, device_id_type=MESH)

    pl.semaphore_wait(barrier, has_left + has_right)

    @pl.when(me == 0)
    def _():
        below_ref[...] = jnp.zeros_like(below_ref)

    @pl.when(me == n - 1)
    def _():
        above_ref[...] = jnp.zeros_like(above_ref)

    @pl.when(me > 0)
    def _():
        to_left().start()

    @pl.when(me < n - 1)
    def _():
        to_right().start()

    @pl.when(me > 0)
    def _():
        to_left().wait_send()
        pltpu.make_async_remote_copy(
            src_ref=tail_ref, dst_ref=below_ref, send_sem=send_sem.at[1],
            recv_sem=recv_sem.at[0], device_id=left, device_id_type=MESH,
        ).wait_recv()

    @pl.when(me < n - 1)
    def _():
        to_right().wait_send()
        pltpu.make_async_remote_copy(
            src_ref=head_ref, dst_ref=above_ref, send_sem=send_sem.at[0],
            recv_sem=recv_sem.at[1], device_id=right, device_id_type=MESH,
        ).wait_recv()


def with_halo(cells, width):
    n = lax.axis_size("col")
    head = lax.slice_in_dim(cells, 0, width, axis=1)
    tail = lax.slice_in_dim(cells, cells.shape[1] - width, cells.shape[1], axis=1)
    below, above = pl.pallas_call(
        functools.partial(_halo_kernel, n),
        out_shape=(jax.ShapeDtypeStruct(head.shape, head.dtype),) * 2,
        in_specs=[pl.BlockSpec(memory_space=pltpu.VMEM)] * 2,
        out_specs=(pl.BlockSpec(memory_space=pltpu.VMEM),) * 2,
        scratch_shapes=[pltpu.SemaphoreType.DMA((2,)), pltpu.SemaphoreType.DMA((2,))],
        compiler_params=pltpu.CompilerParams(collective_id=3, has_side_effects=True),
    )(head, tail)
    return jnp.concatenate([below, cells, above], axis=1)


def split_up(shard, dim, devices):
    before, after = (shard.shape[:dim], shard.shape[dim + 1 :])
    return jnp.moveaxis(shard.reshape(*before, devices, -1, *after), dim, 0)


def sent_and_summed(shard, axis, dim):
    tiles = split_up(shard, dim, lax.axis_size(axis))
    arrived = exchange(tiles, axis, 0)
    return arrived.sum(axis=0)


def joined_along(tiles, dim):
    dims = list(tiles.shape[1:])
    dims[dim] *= tiles.shape[0]
    return jnp.moveaxis(tiles, 0, dim).reshape(dims)


def from_everyone(shard, axis):
    return exchange(shard, axis, 1 if axis == "cuts" else 2, whole=True)


def gather_directly(shard, axis, dim):
    return joined_along(from_everyone(shard, axis), dim)


def taken_together(shard, axis):
    return from_everyone(shard, axis).sum(axis=0)


def packed_total(arrays, axis):
    line, at, done = (jnp.concatenate([a.reshape(-1) for a in arrays]), 0, [])
    running = taken_together(line, axis)
    for a in arrays:
        done.append(running[at : at + a.size].reshape(a.shape))
        at += a.size
    return tuple(done)


def operate(extended):
    channels, depth, cells = extended.shape
    edge = GRID
    interior = extended[:, 1:-1]
    column = jnp.arange(cells, dtype=jnp.int32) % edge
    has_left = (column > 0).astype(jnp.float32)
    has_right = (column < edge - 1).astype(jnp.float32)
    left_part = jnp.pad(interior, ((0, 0), (0, 0), (1, 0)))[:, :, :-1] * has_left
    right_part = jnp.pad(interior, ((0, 0), (0, 0), (0, 1)))[:, :, 1:] * has_right
    upper_part = jnp.pad(interior, ((0, 0), (0, 0), (edge, 0)))[:, :, :-edge]
    lower_part = jnp.pad(interior, ((0, 0), (0, 0), (0, edge)))[:, :, edge:]
    neighbours = extended[:, 2:] + extended[:, :-2]
    neighbours = neighbours + left_part + right_part + upper_part + lower_part
    return interior + strength * (6.0 * interior - neighbours)


def smooth_once(source):
    planes = source.shape[1]
    extended = with_halo(source, ITERS)
    first_plane = lax.axis_index("col") * planes - ITERS
    total_planes = planes * lax.axis_size("col")
    levels = first_plane + jnp.arange(planes + 2 * ITERS, dtype=jnp.int32)
    inside = ((levels >= 0) & (levels < total_planes)).astype(jnp.float32)[None, :, None]
    solution = jnp.zeros_like(source)
    residual = extended
    direction = extended / centre
    ratio = spread / centre
    for iteration in range(ITERS):
        margin = ITERS - iteration
        solution = solution + direction[:, margin : margin + planes]
        window = inside[:, iteration + 1 : iteration + 1 + planes + 2 * (margin - 1)]
        residual = (residual[:, 1:-1] - operate(direction)) * window
        ratio_next = 1.0 / (2.0 * centre / spread - ratio)
        direction = ratio_next * ratio * direction[:, 1:-1] + 2.0 * ratio_next / spread * residual
        ratio = ratio_next
    return solution + direction


def smooth(source):
    return smooth_once(source)


def _eliminate(m_ref, b_ref, o_ref):
    m = m_ref[...]
    b = b_ref[...]
    n = m.shape[0]
    ri = lax.broadcasted_iota(jnp.int32, m.shape, 0)
    ci = lax.broadcasted_iota(jnp.int32, m.shape, 1)
    rb = lax.broadcasted_iota(jnp.int32, b.shape, 0)

    def pick_row(x, rows, p):
        return jnp.sum(jnp.where(rows == p, x, 0.0), axis=0, keepdims=True)

    def pick_col(x, p):
        return jnp.sum(jnp.where(ci[: x.shape[0]] == p, x, 0.0), axis=1, keepdims=True)

    def step(j, carry):
        m, b = carry
        p, q = 2 * j, 2 * j + 1
        c0, c1 = pick_col(m, p), pick_col(m, q)
        r0, r1 = pick_row(m, ri, p), pick_row(m, ri, q)
        s0, s1 = pick_row(b, rb, p), pick_row(b, rb, q)
        a, e = pick_col(r0, p), pick_col(r0, q)
        c, d = pick_col(r1, p), pick_col(r1, q)
        scale = 1.0 / (a * d - e * c)
        n0, n1 = (d * r0 - e * r1) * scale, (a * r1 - c * r0) * scale
        t0, t1 = (d * s0 - e * s1) * scale, (a * s1 - c * s0) * scale
        m = jnp.where(ri == p, n0, jnp.where(ri == q, n1, m - c0 * n0 - c1 * n1))
        b = jnp.where(rb == p, t0, jnp.where(rb == q, t1, b - c0 * t0 - c1 * t1))
        return m, b

    o_ref[...] = lax.fori_loop(0, n // 2, step, (m, b), unroll=4)[1]


def spd_solve(m, b):
    return pl.pallas_call(_eliminate, out_shape=jax.ShapeDtypeStruct(b.shape, b.dtype))(m, b)


def per_device(data, weights, mixing):
    local_scans, ranks, planes, cells = data.shape
    mix_gram = jnp.dot(mixing.T, mixing, precision=highest)
    weight_gram = jnp.dot(weights.T, weights, precision=highest)
    own_weights = lax.dynamic_slice_in_dim(
        weights, lax.axis_index("cuts") * local_scans, local_scans, 0
    )
    scaled = (mixing.T[None, :, :] * own_weights[:, :, None]).transpose(1, 0, 2)
    coefficients = spd_solve(mix_gram * weight_gram, scaled.reshape(ranks, local_scans * ranks))
    coefficients = coefficients.astype(jnp.bfloat16)
    stacked = data.reshape(local_scans * ranks, planes * cells)
    portion = sent_and_summed(
        lax.dot_general(
            coefficients, stacked, (((1,), (0,)), ((), ())), preferred_element_type=jnp.float32
        ),
        "cuts",
        0,
    )
    smoothed = smooth(portion.reshape(-1, planes, cells))
    factor = gather_directly(smoothed, "cuts", 0)
    factor_flat = factor.reshape(ranks, planes * cells)
    factor_half = factor_flat.astype(jnp.bfloat16)
    factor_gram = jnp.dot(factor_flat, factor_flat.T, precision=highest)
    products = lax.dot_general(
        data.reshape(local_scans, ranks, planes * cells),
        factor_half,
        (((2,), (1,)), ((), ())),
        preferred_element_type=jnp.float32,
    )
    targets = jnp.sum(mixing[None, :, :] * products, axis=1)
    half = ranks // 2
    row = lax.broadcasted_iota(jnp.int32, (half, half), 0)
    col = lax.broadcasted_iota(jnp.int32, (half, half), 1)
    top, off, low = (factor_gram[:half, :half], factor_gram[:half, half:], factor_gram[half:, half:])
    folded = jnp.where(row >= col, top, low)
    folded, off, low_diag, targets = packed_total(
        (folded, off, jnp.sum(jnp.where(row == col, low, 0.0), axis=1), targets), "col"
    )
    top = jnp.where(row >= col, folded, folded.T)
    low = jnp.where(row < col, folded, jnp.where(row > col, folded.T, low_diag[:, None]))
    factor_gram = jnp.concatenate(
        [jnp.concatenate([top, off], axis=1), jnp.concatenate([off.T, low], axis=1)], axis=0
    )
    updated = spd_solve(mix_gram * factor_gram, targets.T).T
    return (factor, updated)


def solution(mesh):
    return jax.shard_map(
        per_device,
        mesh=mesh,
        in_specs=(P("cuts", None, "col", None), P(), P()),
        out_specs=(P(None, "col", None), P("cuts", None)),
        check_vma=False,
    )
```

```python
import functools
import jax
import jax.numpy as jnp
from jax import lax
from jax.sharding import PartitionSpec as P
from jax.experimental import pallas as pl
from jax.experimental.pallas import tpu as pltpu

MESH = pl.DeviceIdType.MESH

GRID = 32
ITERS = 3


strength = 0.5
highest = lax.Precision.HIGHEST
low_edge = 1.0
high_edge = 1.0 + 12.0 * strength
centre = (high_edge + low_edge) / 2.0
spread = (high_edge - low_edge) / 2.0


def extended_2(cells, sides, width):
    for axis, dim in sides:
        count = lax.axis_size(axis)
        ends = count - 1
        head = lax.slice_in_dim(cells, 0, width, axis=dim)
        tail = lax.slice_in_dim(cells, cells.shape[dim] - width, cells.shape[dim], axis=dim)
        cells = jnp.concatenate(
            [
                lax.ppermute(tail, axis, [(i, (i + 1) % count) for i in range(ends)]),
                cells,
                lax.ppermute(head, axis, [((i + 1) % count, i) for i in range(ends)]),
            ],
            axis=dim,
        )
    return cells


def _exchange_kernel(axis, other, size, stride, whole, x_ref, o_ref, send_sem, recv_sem, own_sem):
    me = lax.axis_index(axis)
    fixed = lax.axis_index(other)
    pos = (me // stride) % size
    base = me - pos * stride

    def where(peer_pos):
        peer = base + peer_pos * stride
        return (peer, fixed) if axis == "cuts" else (fixed, peer)

    def part(peer_pos):
        return x_ref if whole else x_ref.at[peer_pos]

    barrier = pltpu.get_barrier_semaphore()
    for d in range(1, size):
        pl.semaphore_signal(
            barrier, inc=1, device_id=where((pos + d) % size), device_id_type=MESH
        )
    pl.semaphore_wait(barrier, size - 1)
    own = pltpu.make_async_copy(part(pos), o_ref.at[pos], own_sem)
    own.start()
    copies = []
    for d in range(1, size):
        peer_pos = (pos + d) % size
        copy = pltpu.make_async_remote_copy(
            src_ref=part(peer_pos),
            dst_ref=o_ref.at[pos],
            send_sem=send_sem.at[peer_pos],
            recv_sem=recv_sem.at[pos],
            device_id=where(peer_pos),
            device_id_type=MESH,
        )
        copy.start()
        copies.append(copy)
    for copy in copies:
        copy.wait_send()
    for d in range(1, size):
        source = (pos + size - d) % size
        pltpu.make_async_remote_copy(
            src_ref=part(source),
            dst_ref=o_ref.at[source],
            send_sem=send_sem.at[source],
            recv_sem=recv_sem.at[source],
            device_id=where(source),
            device_id_type=MESH,
        ).wait_recv()
    own.wait()


def exchange(x, axis, key, whole=False, size=None, stride=1):
    other = "col" if axis == "cuts" else "cuts"
    size = size or lax.axis_size(axis)
    shape = (size, *x.shape) if whole else x.shape
    return pl.pallas_call(
        functools.partial(_exchange_kernel, axis, other, size, stride, whole),
        out_shape=jax.ShapeDtypeStruct(shape, x.dtype),
        in_specs=[pl.BlockSpec(memory_space=pltpu.VMEM)],
        out_specs=pl.BlockSpec(memory_space=pltpu.VMEM),
        scratch_shapes=[
            pltpu.SemaphoreType.DMA((size,)),
            pltpu.SemaphoreType.DMA((size,)),
            pltpu.SemaphoreType.DMA,
        ],
        compiler_params=pltpu.CompilerParams(collective_id=key, has_side_effects=True),
    )(x)


def _halo_kernel(n, head_ref, tail_ref, below_ref, above_ref, send_sem, recv_sem):
    me = lax.axis_index("col")
    fixed = lax.axis_index("cuts")
    has_left = (me + n - 1) // n
    has_right = 1 - me // (n - 1)
    left, right = (fixed, me - has_left), (fixed, me + has_right)

    def to_left():
        return pltpu.make_async_remote_copy(
            src_ref=head_ref, dst_ref=above_ref, send_sem=send_sem.at[0],
            recv_sem=recv_sem.at[1], device_id=left, device_id_type=MESH,
        )

    def to_right():
        return pltpu.make_async_remote_copy(
            src_ref=tail_ref, dst_ref=below_ref, send_sem=send_sem.at[1],
            recv_sem=recv_sem.at[0], device_id=right, device_id_type=MESH,
        )

    barrier = pltpu.get_barrier_semaphore()

    @pl.when(me > 0)
    def _():
        pl.semaphore_signal(barrier, inc=1, device_id=left, device_id_type=MESH)

    @pl.when(me < n - 1)
    def _():
        pl.semaphore_signal(barrier, inc=1, device_id=right, device_id_type=MESH)

    pl.semaphore_wait(barrier, has_left + has_right)

    @pl.when(me == 0)
    def _():
        below_ref[...] = jnp.zeros_like(below_ref)

    @pl.when(me == n - 1)
    def _():
        above_ref[...] = jnp.zeros_like(above_ref)

    @pl.when(me > 0)
    def _():
        to_left().start()

    @pl.when(me < n - 1)
    def _():
        to_right().start()

    @pl.when(me > 0)
    def _():
        to_left().wait_send()
        pltpu.make_async_remote_copy(
            src_ref=tail_ref, dst_ref=below_ref, send_sem=send_sem.at[1],
            recv_sem=recv_sem.at[0], device_id=left, device_id_type=MESH,
        ).wait_recv()

    @pl.when(me < n - 1)
    def _():
        to_right().wait_send()
        pltpu.make_async_remote_copy(
            src_ref=head_ref, dst_ref=above_ref, send_sem=send_sem.at[0],
            recv_sem=recv_sem.at[1], device_id=right, device_id_type=MESH,
        ).wait_recv()


def with_halo(cells, width):
    n = lax.axis_size("col")
    head = lax.slice_in_dim(cells, 0, width, axis=1)
    tail = lax.slice_in_dim(cells, cells.shape[1] - width, cells.shape[1], axis=1)
    below, above = pl.pallas_call(
        functools.partial(_halo_kernel, n),
        out_shape=(jax.ShapeDtypeStruct(head.shape, head.dtype),) * 2,
        in_specs=[pl.BlockSpec(memory_space=pltpu.VMEM)] * 2,
        out_specs=(pl.BlockSpec(memory_space=pltpu.VMEM),) * 2,
        scratch_shapes=[pltpu.SemaphoreType.DMA((2,)), pltpu.SemaphoreType.DMA((2,))],
        compiler_params=pltpu.CompilerParams(collective_id=3, has_side_effects=True),
    )(head, tail)
    return jnp.concatenate([below, cells, above], axis=1)


def split_up(shard, dim, devices):
    before, after = (shard.shape[:dim], shard.shape[dim + 1 :])
    return jnp.moveaxis(shard.reshape(*before, devices, -1, *after), dim, 0)


def sent_and_summed(shard, axis, dim):
    tiles = split_up(shard, dim, lax.axis_size(axis))
    arrived = exchange(tiles, axis, 0)
    return arrived.sum(axis=0)


def joined_along(tiles, dim):
    dims = list(tiles.shape[1:])
    dims[dim] *= tiles.shape[0]
    return jnp.moveaxis(tiles, 0, dim).reshape(dims)


def from_everyone(shard, axis):
    return exchange(shard, axis, 1 if axis == "cuts" else 2, whole=True)


def gather_directly(shard, axis, dim):
    return joined_along(from_everyone(shard, axis), dim)


def taken_together(shard, axis):
    return from_everyone(shard, axis).sum(axis=0)


def packed_total(arrays, axis):
    line, at, done = (jnp.concatenate([a.reshape(-1) for a in arrays]), 0, [])
    running = taken_together(line, axis)
    for a in arrays:
        done.append(running[at : at + a.size].reshape(a.shape))
        at += a.size
    return tuple(done)


def operate(extended):
    channels, depth, cells = extended.shape
    edge = GRID
    interior = extended[:, 1:-1]
    column = jnp.arange(cells, dtype=jnp.int32) % edge
    has_left = (column > 0).astype(jnp.float32)
    has_right = (column < edge - 1).astype(jnp.float32)
    left_part = jnp.pad(interior, ((0, 0), (0, 0), (1, 0)))[:, :, :-1] * has_left
    right_part = jnp.pad(interior, ((0, 0), (0, 0), (0, 1)))[:, :, 1:] * has_right
    upper_part = jnp.pad(interior, ((0, 0), (0, 0), (edge, 0)))[:, :, :-edge]
    lower_part = jnp.pad(interior, ((0, 0), (0, 0), (0, edge)))[:, :, edge:]
    neighbours = extended[:, 2:] + extended[:, :-2]
    neighbours = neighbours + left_part + right_part + upper_part + lower_part
    return interior + strength * (6.0 * interior - neighbours)


def smooth_once(source):
    planes = source.shape[1]
    extended = with_halo(source, ITERS)
    first_plane = lax.axis_index("col") * planes - ITERS
    total_planes = planes * lax.axis_size("col")
    levels = first_plane + jnp.arange(planes + 2 * ITERS, dtype=jnp.int32)
    inside = ((levels >= 0) & (levels < total_planes)).astype(jnp.float32)[None, :, None]
    solution = jnp.zeros_like(source)
    residual = extended
    direction = extended / centre
    ratio = spread / centre
    for iteration in range(ITERS):
        margin = ITERS - iteration
        solution = solution + direction[:, margin : margin + planes]
        window = inside[:, iteration + 1 : iteration + 1 + planes + 2 * (margin - 1)]
        residual = (residual[:, 1:-1] - operate(direction)) * window
        ratio_next = 1.0 / (2.0 * centre / spread - ratio)
        direction = ratio_next * ratio * direction[:, 1:-1] + 2.0 * ratio_next / spread * residual
        ratio = ratio_next
    return solution + direction


def smooth(source):
    return smooth_once(source)


def _eliminate(m_ref, b_ref, o_ref):
    m = m_ref[...]
    b = b_ref[...]
    n = m.shape[0]
    ri = lax.broadcasted_iota(jnp.int32, m.shape, 0)
    ci = lax.broadcasted_iota(jnp.int32, m.shape, 1)
    rb = lax.broadcasted_iota(jnp.int32, b.shape, 0)

    def pick_row(x, rows, p):
        return jnp.sum(jnp.where(rows == p, x, 0.0), axis=0, keepdims=True)

    def pick_col(x, p):
        return jnp.sum(jnp.where(ci[: x.shape[0]] == p, x, 0.0), axis=1, keepdims=True)

    def step(j, carry):
        m, b = carry
        p, q = 2 * j, 2 * j + 1
        c0, c1 = pick_col(m, p), pick_col(m, q)
        r0, r1 = pick_row(m, ri, p), pick_row(m, ri, q)
        s0, s1 = pick_row(b, rb, p), pick_row(b, rb, q)
        a, e = pick_col(r0, p), pick_col(r0, q)
        c, d = pick_col(r1, p), pick_col(r1, q)
        scale = 1.0 / (a * d - e * c)
        n0, n1 = (d * r0 - e * r1) * scale, (a * r1 - c * r0) * scale
        t0, t1 = (d * s0 - e * s1) * scale, (a * s1 - c * s0) * scale
        m = jnp.where(ri == p, n0, jnp.where(ri == q, n1, m - c0 * n0 - c1 * n1))
        b = jnp.where(rb == p, t0, jnp.where(rb == q, t1, b - c0 * t0 - c1 * t1))
        return m, b

    o_ref[...] = lax.fori_loop(0, n // 2, step, (m, b), unroll=4)[1]


def spd_solve(m, b):
    return pl.pallas_call(_eliminate, out_shape=jax.ShapeDtypeStruct(b.shape, b.dtype))(m, b)


def per_device(data, weights, mixing):
    local_scans, ranks, planes, cells = data.shape
    mix_gram = jnp.dot(mixing.T, mixing, precision=highest)
    weight_gram = jnp.dot(weights.T, weights, precision=highest)
    own_weights = lax.dynamic_slice_in_dim(
        weights, lax.axis_index("cuts") * local_scans, local_scans, 0
    )
    scaled = (mixing.T[None, :, :] * own_weights[:, :, None]).transpose(1, 0, 2)
    coefficients = spd_solve(mix_gram * weight_gram, scaled.reshape(ranks, local_scans * ranks))
    coefficients = coefficients.astype(jnp.bfloat16)
    stacked = data.reshape(local_scans * ranks, planes * cells)
    partial = lax.dot_general(
        coefficients, stacked, (((1,), (0,)), ((), ())), preferred_element_type=jnp.float32
    )
    cores = 2
    chips = lax.axis_size("cuts") // cores
    paired = exchange(partial.reshape(cores, chips, -1, planes * cells), "cuts", 0, size=cores)
    paired = paired.sum(axis=0)
    portion = exchange(paired, "cuts", 4, size=chips, stride=cores).sum(axis=0)
    smoothed = smooth(portion.reshape(-1, planes, cells))
    half_factor = exchange(smoothed, "cuts", 1, whole=True, size=chips, stride=cores)
    factor = exchange(half_factor, "cuts", 5, whole=True, size=cores)
    factor = factor.reshape(ranks, planes, cells)
    factor_flat = factor.reshape(ranks, planes * cells)
    factor_half = factor_flat.astype(jnp.bfloat16)
    factor_gram = jnp.dot(factor_flat, factor_flat.T, precision=highest)
    products = lax.dot_general(
        data.reshape(local_scans, ranks, planes * cells),
        factor_half,
        (((2,), (1,)), ((), ())),
        preferred_element_type=jnp.float32,
    )
    targets = jnp.sum(mixing[None, :, :] * products, axis=1)
    half = ranks // 2
    row = lax.broadcasted_iota(jnp.int32, (half, half), 0)
    col = lax.broadcasted_iota(jnp.int32, (half, half), 1)
    top, off, low = (factor_gram[:half, :half], factor_gram[:half, half:], factor_gram[half:, half:])
    folded = jnp.where(row >= col, top, low)
    folded, off, low_diag, targets = packed_total(
        (folded, off, jnp.sum(jnp.where(row == col, low, 0.0), axis=1), targets), "col"
    )
    top = jnp.where(row >= col, folded, folded.T)
    low = jnp.where(row < col, folded, jnp.where(row > col, folded.T, low_diag[:, None]))
    factor_gram = jnp.concatenate(
        [jnp.concatenate([top, off], axis=1), jnp.concatenate([off.T, low], axis=1)], axis=0
    )
    updated = spd_solve(mix_gram * factor_gram, targets.T).T
    return (factor, updated)


def solution(mesh):
    return jax.shard_map(
        per_device,
        mesh=mesh,
        in_specs=(P("cuts", None, "col", None), P(), P()),
        out_specs=(P(None, "col", None), P("cuts", None)),
        check_vma=False,
    )
```

```python
import functools
import jax
import jax.numpy as jnp
from jax import lax
from jax.sharding import PartitionSpec as P
from jax.experimental import pallas as pl
from jax.experimental.pallas import tpu as pltpu

MESH = pl.DeviceIdType.MESH

GRID = 32
ITERS = 3


strength = 0.5
highest = lax.Precision.HIGHEST
low_edge = 1.0
high_edge = 1.0 + 12.0 * strength
centre = (high_edge + low_edge) / 2.0
spread = (high_edge - low_edge) / 2.0


def extended_2(cells, sides, width):
    for axis, dim in sides:
        count = lax.axis_size(axis)
        ends = count - 1
        head = lax.slice_in_dim(cells, 0, width, axis=dim)
        tail = lax.slice_in_dim(cells, cells.shape[dim] - width, cells.shape[dim], axis=dim)
        cells = jnp.concatenate(
            [
                lax.ppermute(tail, axis, [(i, (i + 1) % count) for i in range(ends)]),
                cells,
                lax.ppermute(head, axis, [((i + 1) % count, i) for i in range(ends)]),
            ],
            axis=dim,
        )
    return cells


def _exchange_kernel(axis, other, size, stride, whole, summed, x_ref, o_ref, *scratch):
    if summed:
        send_sem, recv_sem, own_sem, got = scratch
    else:
        (send_sem, recv_sem, own_sem), got = scratch, o_ref
    me = lax.axis_index(axis)
    fixed = lax.axis_index(other)
    pos = (me // stride) % size
    base = me - pos * stride

    def where(peer_pos):
        peer = base + peer_pos * stride
        return (peer, fixed) if axis == "cuts" else (fixed, peer)

    def part(peer_pos):
        return x_ref if whole else x_ref.at[peer_pos]

    barrier = pltpu.get_barrier_semaphore()
    for d in range(1, size):
        pl.semaphore_signal(
            barrier, inc=1, device_id=where((pos + d) % size), device_id_type=MESH
        )
    pl.semaphore_wait(barrier, size - 1)
    own = pltpu.make_async_copy(part(pos), got.at[pos], own_sem)
    own.start()
    copies = []
    for d in range(1, size):
        peer_pos = (pos + d) % size
        copy = pltpu.make_async_remote_copy(
            src_ref=part(peer_pos),
            dst_ref=got.at[pos],
            send_sem=send_sem.at[peer_pos],
            recv_sem=recv_sem.at[pos],
            device_id=where(peer_pos),
            device_id_type=MESH,
        )
        copy.start()
        copies.append(copy)
    for copy in copies:
        copy.wait_send()
    for d in range(1, size):
        source = (pos + size - d) % size
        pltpu.make_async_remote_copy(
            src_ref=part(source),
            dst_ref=got.at[source],
            send_sem=send_sem.at[source],
            recv_sem=recv_sem.at[source],
            device_id=where(source),
            device_id_type=MESH,
        ).wait_recv()
    own.wait()
    if summed:
        total = got[0]
        for slot in range(1, size):
            total = total + got[slot]
        o_ref[...] = total


def exchange(x, axis, key, whole=False, size=None, stride=1, summed=False):
    other = "col" if axis == "cuts" else "cuts"
    size = size or lax.axis_size(axis)
    shape = (size, *x.shape) if whole else x.shape
    scratch = [
        pltpu.SemaphoreType.DMA((size,)),
        pltpu.SemaphoreType.DMA((size,)),
        pltpu.SemaphoreType.DMA,
    ]
    if summed:
        scratch.append(pltpu.VMEM(shape, x.dtype))
        shape = shape[1:]
    return pl.pallas_call(
        functools.partial(_exchange_kernel, axis, other, size, stride, whole, summed),
        out_shape=jax.ShapeDtypeStruct(shape, x.dtype),
        in_specs=[pl.BlockSpec(memory_space=pltpu.VMEM)],
        out_specs=pl.BlockSpec(memory_space=pltpu.VMEM),
        scratch_shapes=scratch,
        compiler_params=pltpu.CompilerParams(collective_id=key, has_side_effects=True),
    )(x)


def _halo_kernel(n, head_ref, tail_ref, below_ref, above_ref, send_sem, recv_sem):
    me = lax.axis_index("col")
    fixed = lax.axis_index("cuts")
    has_left = (me + n - 1) // n
    has_right = 1 - me // (n - 1)
    left, right = (fixed, me - has_left), (fixed, me + has_right)

    def to_left():
        return pltpu.make_async_remote_copy(
            src_ref=head_ref, dst_ref=above_ref, send_sem=send_sem.at[0],
            recv_sem=recv_sem.at[1], device_id=left, device_id_type=MESH,
        )

    def to_right():
        return pltpu.make_async_remote_copy(
            src_ref=tail_ref, dst_ref=below_ref, send_sem=send_sem.at[1],
            recv_sem=recv_sem.at[0], device_id=right, device_id_type=MESH,
        )

    barrier = pltpu.get_barrier_semaphore()

    @pl.when(me > 0)
    def _():
        pl.semaphore_signal(barrier, inc=1, device_id=left, device_id_type=MESH)

    @pl.when(me < n - 1)
    def _():
        pl.semaphore_signal(barrier, inc=1, device_id=right, device_id_type=MESH)

    pl.semaphore_wait(barrier, has_left + has_right)

    @pl.when(me == 0)
    def _():
        below_ref[...] = jnp.zeros_like(below_ref)

    @pl.when(me == n - 1)
    def _():
        above_ref[...] = jnp.zeros_like(above_ref)

    @pl.when(me > 0)
    def _():
        to_left().start()

    @pl.when(me < n - 1)
    def _():
        to_right().start()

    @pl.when(me > 0)
    def _():
        to_left().wait_send()
        pltpu.make_async_remote_copy(
            src_ref=tail_ref, dst_ref=below_ref, send_sem=send_sem.at[1],
            recv_sem=recv_sem.at[0], device_id=left, device_id_type=MESH,
        ).wait_recv()

    @pl.when(me < n - 1)
    def _():
        to_right().wait_send()
        pltpu.make_async_remote_copy(
            src_ref=head_ref, dst_ref=above_ref, send_sem=send_sem.at[0],
            recv_sem=recv_sem.at[1], device_id=right, device_id_type=MESH,
        ).wait_recv()


def with_halo(cells, width):
    n = lax.axis_size("col")
    head = lax.slice_in_dim(cells, 0, width, axis=1)
    tail = lax.slice_in_dim(cells, cells.shape[1] - width, cells.shape[1], axis=1)
    below, above = pl.pallas_call(
        functools.partial(_halo_kernel, n),
        out_shape=(jax.ShapeDtypeStruct(head.shape, head.dtype),) * 2,
        in_specs=[pl.BlockSpec(memory_space=pltpu.VMEM)] * 2,
        out_specs=(pl.BlockSpec(memory_space=pltpu.VMEM),) * 2,
        scratch_shapes=[pltpu.SemaphoreType.DMA((2,)), pltpu.SemaphoreType.DMA((2,))],
        compiler_params=pltpu.CompilerParams(collective_id=3, has_side_effects=True),
    )(head, tail)
    return jnp.concatenate([below, cells, above], axis=1)


def split_up(shard, dim, devices):
    before, after = (shard.shape[:dim], shard.shape[dim + 1 :])
    return jnp.moveaxis(shard.reshape(*before, devices, -1, *after), dim, 0)


def sent_and_summed(shard, axis, dim):
    tiles = split_up(shard, dim, lax.axis_size(axis))
    arrived = exchange(tiles, axis, 0)
    return arrived.sum(axis=0)


def joined_along(tiles, dim):
    dims = list(tiles.shape[1:])
    dims[dim] *= tiles.shape[0]
    return jnp.moveaxis(tiles, 0, dim).reshape(dims)


def from_everyone(shard, axis):
    return exchange(shard, axis, 1 if axis == "cuts" else 2, whole=True)


def gather_directly(shard, axis, dim):
    return joined_along(from_everyone(shard, axis), dim)


def taken_together(shard, axis):
    return from_everyone(shard, axis).sum(axis=0)


def packed_total(arrays, axis):
    line, at, done = (jnp.concatenate([a.reshape(-1) for a in arrays]), 0, [])
    running = taken_together(line, axis)
    for a in arrays:
        done.append(running[at : at + a.size].reshape(a.shape))
        at += a.size
    return tuple(done)


def operate(extended):
    channels, depth, cells = extended.shape
    edge = GRID
    interior = extended[:, 1:-1]
    column = jnp.arange(cells, dtype=jnp.int32) % edge
    has_left = (column > 0).astype(jnp.float32)
    has_right = (column < edge - 1).astype(jnp.float32)
    left_part = jnp.pad(interior, ((0, 0), (0, 0), (1, 0)))[:, :, :-1] * has_left
    right_part = jnp.pad(interior, ((0, 0), (0, 0), (0, 1)))[:, :, 1:] * has_right
    upper_part = jnp.pad(interior, ((0, 0), (0, 0), (edge, 0)))[:, :, :-edge]
    lower_part = jnp.pad(interior, ((0, 0), (0, 0), (0, edge)))[:, :, edge:]
    neighbours = extended[:, 2:] + extended[:, :-2]
    neighbours = neighbours + left_part + right_part + upper_part + lower_part
    return interior + strength * (6.0 * interior - neighbours)


def smooth_once(source):
    planes = source.shape[1]
    extended = with_halo(source, ITERS)
    first_plane = lax.axis_index("col") * planes - ITERS
    total_planes = planes * lax.axis_size("col")
    levels = first_plane + jnp.arange(planes + 2 * ITERS, dtype=jnp.int32)
    inside = ((levels >= 0) & (levels < total_planes)).astype(jnp.float32)[None, :, None]
    solution = jnp.zeros_like(source)
    residual = extended
    direction = extended / centre
    ratio = spread / centre
    for iteration in range(ITERS):
        margin = ITERS - iteration
        solution = solution + direction[:, margin : margin + planes]
        window = inside[:, iteration + 1 : iteration + 1 + planes + 2 * (margin - 1)]
        residual = (residual[:, 1:-1] - operate(direction)) * window
        ratio_next = 1.0 / (2.0 * centre / spread - ratio)
        direction = ratio_next * ratio * direction[:, 1:-1] + 2.0 * ratio_next / spread * residual
        ratio = ratio_next
    return solution + direction


def smooth(source):
    return smooth_once(source)


def _eliminate(m_ref, b_ref, o_ref):
    m = m_ref[...]
    b = b_ref[...]
    n = m.shape[0]
    ri = lax.broadcasted_iota(jnp.int32, m.shape, 0)
    ci = lax.broadcasted_iota(jnp.int32, m.shape, 1)
    rb = lax.broadcasted_iota(jnp.int32, b.shape, 0)

    def pick_row(x, rows, p):
        return jnp.sum(jnp.where(rows == p, x, 0.0), axis=0, keepdims=True)

    def pick_col(x, p):
        return jnp.sum(jnp.where(ci[: x.shape[0]] == p, x, 0.0), axis=1, keepdims=True)

    def step(j, carry):
        m, b = carry
        p, q = 2 * j, 2 * j + 1
        c0, c1 = pick_col(m, p), pick_col(m, q)
        r0, r1 = pick_row(m, ri, p), pick_row(m, ri, q)
        s0, s1 = pick_row(b, rb, p), pick_row(b, rb, q)
        a, e = pick_col(r0, p), pick_col(r0, q)
        c, d = pick_col(r1, p), pick_col(r1, q)
        scale = 1.0 / (a * d - e * c)
        n0, n1 = (d * r0 - e * r1) * scale, (a * r1 - c * r0) * scale
        t0, t1 = (d * s0 - e * s1) * scale, (a * s1 - c * s0) * scale
        m = jnp.where(ri == p, n0, jnp.where(ri == q, n1, m - c0 * n0 - c1 * n1))
        b = jnp.where(rb == p, t0, jnp.where(rb == q, t1, b - c0 * t0 - c1 * t1))
        return m, b

    o_ref[...] = lax.fori_loop(0, n // 2, step, (m, b), unroll=4)[1]


def spd_solve(m, b):
    return pl.pallas_call(_eliminate, out_shape=jax.ShapeDtypeStruct(b.shape, b.dtype))(m, b)


def per_device(data, weights, mixing):
    local_scans, ranks, planes, cells = data.shape
    mix_gram = jnp.dot(mixing.T, mixing, precision=highest)
    weight_gram = jnp.dot(weights.T, weights, precision=highest)
    own_weights = lax.dynamic_slice_in_dim(
        weights, lax.axis_index("cuts") * local_scans, local_scans, 0
    )
    scaled = (mixing.T[None, :, :] * own_weights[:, :, None]).transpose(1, 0, 2)
    coefficients = spd_solve(mix_gram * weight_gram, scaled.reshape(ranks, local_scans * ranks))
    coefficients = coefficients.astype(jnp.bfloat16)
    partial = lax.dot_general(
        coefficients, data.reshape(-1, planes, cells), (((1,), (0,)), ((), ())), preferred_element_type=jnp.float32
    )
    cores = 2
    chips = lax.axis_size("cuts") // cores
    paired = exchange(
        partial.reshape(cores, chips, -1, planes, cells), "cuts", 0, size=cores, summed=True
    )
    portion = exchange(paired, "cuts", 4, size=chips, stride=cores, summed=True)
    smoothed = smooth(portion.reshape(-1, planes, cells))
    half_factor = exchange(smoothed, "cuts", 1, whole=True, size=chips, stride=cores)
    factor = exchange(half_factor, "cuts", 5, whole=True, size=cores)
    factor = factor.reshape(ranks, planes, cells)
    factor_half = factor.astype(jnp.bfloat16)
    factor_gram = lax.dot_general(
        factor, factor, (((1, 2), (1, 2)), ((), ())), precision=highest
    )
    products = lax.dot_general(
        data, factor_half, (((2, 3), (1, 2)), ((), ())), preferred_element_type=jnp.float32
    )
    targets = jnp.sum(mixing[None, :, :] * products, axis=1)
    half = ranks // 2
    row = lax.broadcasted_iota(jnp.int32, (half, half), 0)
    col = lax.broadcasted_iota(jnp.int32, (half, half), 1)
    top, off, low = (factor_gram[:half, :half], factor_gram[:half, half:], factor_gram[half:, half:])
    folded = jnp.where(row >= col, top, low)
    folded, off, low_diag, targets = packed_total(
        (folded, off, jnp.sum(jnp.where(row == col, low, 0.0), axis=1), targets), "col"
    )
    top = jnp.where(row >= col, folded, folded.T)
    low = jnp.where(row < col, folded, jnp.where(row > col, folded.T, low_diag[:, None]))
    factor_gram = jnp.concatenate(
        [jnp.concatenate([top, off], axis=1), jnp.concatenate([off.T, low], axis=1)], axis=0
    )
    updated = spd_solve(mix_gram * factor_gram, targets.T).T
    return (factor, updated)


def solution(mesh):
    return jax.shard_map(
        per_device,
        mesh=mesh,
        in_specs=(P("cuts", None, "col", None), P(), P()),
        out_specs=(P(None, "col", None), P("cuts", None)),
        check_vma=False,
    )
```

```python
import functools
import jax
import jax.numpy as jnp
from jax import lax
from jax.sharding import PartitionSpec as P
from jax.experimental import pallas as pl
from jax.experimental.pallas import tpu as pltpu

MESH = pl.DeviceIdType.MESH

GRID = 32
ITERS = 3


strength = 0.5
highest = lax.Precision.HIGHEST
low_edge = 1.0
high_edge = 1.0 + 12.0 * strength
centre = (high_edge + low_edge) / 2.0
spread = (high_edge - low_edge) / 2.0


def extended_2(cells, sides, width):
    for axis, dim in sides:
        count = lax.axis_size(axis)
        ends = count - 1
        head = lax.slice_in_dim(cells, 0, width, axis=dim)
        tail = lax.slice_in_dim(cells, cells.shape[dim] - width, cells.shape[dim], axis=dim)
        cells = jnp.concatenate(
            [
                lax.ppermute(tail, axis, [(i, (i + 1) % count) for i in range(ends)]),
                cells,
                lax.ppermute(head, axis, [((i + 1) % count, i) for i in range(ends)]),
            ],
            axis=dim,
        )
    return cells


def _exchange_kernel(axis, other, size, stride, whole, summed, x_ref, o_ref, *scratch):
    if summed:
        send_sem, recv_sem, own_sem, got = scratch
    else:
        (send_sem, recv_sem, own_sem), got = scratch, o_ref
    me = lax.axis_index(axis)
    fixed = lax.axis_index(other)
    pos = (me // stride) % size
    base = me - pos * stride

    def where(peer_pos):
        peer = base + peer_pos * stride
        return (peer, fixed) if axis == "cuts" else (fixed, peer)

    def part(peer_pos):
        return x_ref if whole else x_ref.at[peer_pos]

    barrier = pltpu.get_barrier_semaphore()
    for d in range(1, size):
        pl.semaphore_signal(
            barrier, inc=1, device_id=where((pos + d) % size), device_id_type=MESH
        )
    pl.semaphore_wait(barrier, size - 1)
    own = pltpu.make_async_copy(part(pos), got.at[pos], own_sem)
    own.start()
    copies = []
    for d in range(1, size):
        peer_pos = (pos + d) % size
        copy = pltpu.make_async_remote_copy(
            src_ref=part(peer_pos),
            dst_ref=got.at[pos],
            send_sem=send_sem.at[peer_pos],
            recv_sem=recv_sem.at[pos],
            device_id=where(peer_pos),
            device_id_type=MESH,
        )
        copy.start()
        copies.append(copy)
    for copy in copies:
        copy.wait_send()
    for d in range(1, size):
        source = (pos + size - d) % size
        pltpu.make_async_remote_copy(
            src_ref=part(source),
            dst_ref=got.at[source],
            send_sem=send_sem.at[source],
            recv_sem=recv_sem.at[source],
            device_id=where(source),
            device_id_type=MESH,
        ).wait_recv()
    own.wait()
    if summed:
        total = got[0]
        for slot in range(1, size):
            total = total + got[slot]
        o_ref[...] = total


def exchange(x, axis, key, whole=False, size=None, stride=1, summed=False, space=None):
    other = "col" if axis == "cuts" else "cuts"
    size = size or lax.axis_size(axis)
    shape = (size, *x.shape) if whole else x.shape
    scratch = [
        pltpu.SemaphoreType.DMA((size,)),
        pltpu.SemaphoreType.DMA((size,)),
        pltpu.SemaphoreType.DMA,
    ]
    if summed:
        scratch.append(pltpu.VMEM(shape, x.dtype))
        shape = shape[1:]
    return pl.pallas_call(
        functools.partial(_exchange_kernel, axis, other, size, stride, whole, summed),
        out_shape=jax.ShapeDtypeStruct(shape, x.dtype),
        in_specs=[pl.BlockSpec(memory_space=pltpu.VMEM)],
        out_specs=pl.BlockSpec(memory_space=space or pltpu.VMEM),
        scratch_shapes=scratch,
        compiler_params=pltpu.CompilerParams(collective_id=key, has_side_effects=True),
    )(x)


def _halo_kernel(n, head_ref, tail_ref, below_ref, above_ref, send_sem, recv_sem):
    me = lax.axis_index("col")
    fixed = lax.axis_index("cuts")
    has_left = (me + n - 1) // n
    has_right = 1 - me // (n - 1)
    left, right = (fixed, me - has_left), (fixed, me + has_right)

    def to_left():
        return pltpu.make_async_remote_copy(
            src_ref=head_ref, dst_ref=above_ref, send_sem=send_sem.at[0],
            recv_sem=recv_sem.at[1], device_id=left, device_id_type=MESH,
        )

    def to_right():
        return pltpu.make_async_remote_copy(
            src_ref=tail_ref, dst_ref=below_ref, send_sem=send_sem.at[1],
            recv_sem=recv_sem.at[0], device_id=right, device_id_type=MESH,
        )

    barrier = pltpu.get_barrier_semaphore()

    @pl.when(me > 0)
    def _():
        pl.semaphore_signal(barrier, inc=1, device_id=left, device_id_type=MESH)

    @pl.when(me < n - 1)
    def _():
        pl.semaphore_signal(barrier, inc=1, device_id=right, device_id_type=MESH)

    pl.semaphore_wait(barrier, has_left + has_right)

    @pl.when(me == 0)
    def _():
        below_ref[...] = jnp.zeros_like(below_ref)

    @pl.when(me == n - 1)
    def _():
        above_ref[...] = jnp.zeros_like(above_ref)

    @pl.when(me > 0)
    def _():
        to_left().start()

    @pl.when(me < n - 1)
    def _():
        to_right().start()

    @pl.when(me > 0)
    def _():
        to_left().wait_send()
        pltpu.make_async_remote_copy(
            src_ref=tail_ref, dst_ref=below_ref, send_sem=send_sem.at[1],
            recv_sem=recv_sem.at[0], device_id=left, device_id_type=MESH,
        ).wait_recv()

    @pl.when(me < n - 1)
    def _():
        to_right().wait_send()
        pltpu.make_async_remote_copy(
            src_ref=head_ref, dst_ref=above_ref, send_sem=send_sem.at[0],
            recv_sem=recv_sem.at[1], device_id=right, device_id_type=MESH,
        ).wait_recv()


def with_halo(cells, width):
    n = lax.axis_size("col")
    head = lax.slice_in_dim(cells, 0, width, axis=1)
    tail = lax.slice_in_dim(cells, cells.shape[1] - width, cells.shape[1], axis=1)
    below, above = pl.pallas_call(
        functools.partial(_halo_kernel, n),
        out_shape=(jax.ShapeDtypeStruct(head.shape, head.dtype),) * 2,
        in_specs=[pl.BlockSpec(memory_space=pltpu.VMEM)] * 2,
        out_specs=(pl.BlockSpec(memory_space=pltpu.VMEM),) * 2,
        scratch_shapes=[pltpu.SemaphoreType.DMA((2,)), pltpu.SemaphoreType.DMA((2,))],
        compiler_params=pltpu.CompilerParams(collective_id=3, has_side_effects=True),
    )(head, tail)
    return jnp.concatenate([below, cells, above], axis=1)


def split_up(shard, dim, devices):
    before, after = (shard.shape[:dim], shard.shape[dim + 1 :])
    return jnp.moveaxis(shard.reshape(*before, devices, -1, *after), dim, 0)


def sent_and_summed(shard, axis, dim):
    tiles = split_up(shard, dim, lax.axis_size(axis))
    arrived = exchange(tiles, axis, 0)
    return arrived.sum(axis=0)


def joined_along(tiles, dim):
    dims = list(tiles.shape[1:])
    dims[dim] *= tiles.shape[0]
    return jnp.moveaxis(tiles, 0, dim).reshape(dims)


def from_everyone(shard, axis):
    return exchange(shard, axis, 1 if axis == "cuts" else 2, whole=True)


def gather_directly(shard, axis, dim):
    return joined_along(from_everyone(shard, axis), dim)


def taken_together(shard, axis):
    return from_everyone(shard, axis).sum(axis=0)


def packed_total(arrays, axis):
    line, at, done = (jnp.concatenate([a.reshape(-1) for a in arrays]), 0, [])
    running = taken_together(line, axis)
    for a in arrays:
        done.append(running[at : at + a.size].reshape(a.shape))
        at += a.size
    return tuple(done)


def operate(extended):
    channels, depth, cells = extended.shape
    edge = GRID
    interior = extended[:, 1:-1]
    column = jnp.arange(cells, dtype=jnp.int32) % edge
    has_left = (column > 0).astype(jnp.float32)
    has_right = (column < edge - 1).astype(jnp.float32)
    left_part = jnp.pad(interior, ((0, 0), (0, 0), (1, 0)))[:, :, :-1] * has_left
    right_part = jnp.pad(interior, ((0, 0), (0, 0), (0, 1)))[:, :, 1:] * has_right
    upper_part = jnp.pad(interior, ((0, 0), (0, 0), (edge, 0)))[:, :, :-edge]
    lower_part = jnp.pad(interior, ((0, 0), (0, 0), (0, edge)))[:, :, edge:]
    neighbours = extended[:, 2:] + extended[:, :-2]
    neighbours = neighbours + left_part + right_part + upper_part + lower_part
    return interior + strength * (6.0 * interior - neighbours)


def smooth_once(source):
    planes = source.shape[1]
    extended = with_halo(source, ITERS)
    first_plane = lax.axis_index("col") * planes - ITERS
    total_planes = planes * lax.axis_size("col")
    levels = first_plane + jnp.arange(planes + 2 * ITERS, dtype=jnp.int32)
    inside = ((levels >= 0) & (levels < total_planes)).astype(jnp.float32)[None, :, None]
    solution = jnp.zeros_like(source)
    residual = extended
    direction = extended / centre
    ratio = spread / centre
    for iteration in range(ITERS):
        margin = ITERS - iteration
        solution = solution + direction[:, margin : margin + planes]
        window = inside[:, iteration + 1 : iteration + 1 + planes + 2 * (margin - 1)]
        residual = (residual[:, 1:-1] - operate(direction)) * window
        ratio_next = 1.0 / (2.0 * centre / spread - ratio)
        direction = ratio_next * ratio * direction[:, 1:-1] + 2.0 * ratio_next / spread * residual
        ratio = ratio_next
    return solution + direction


def smooth(source):
    return smooth_once(source)


def _eliminate(m_ref, b_ref, o_ref):
    m = m_ref[...]
    b = b_ref[...]
    n = m.shape[0]
    ri = lax.broadcasted_iota(jnp.int32, m.shape, 0)
    ci = lax.broadcasted_iota(jnp.int32, m.shape, 1)
    rb = lax.broadcasted_iota(jnp.int32, b.shape, 0)

    def pick_row(x, rows, p):
        return jnp.sum(jnp.where(rows == p, x, 0.0), axis=0, keepdims=True)

    def pick_col(x, p):
        return jnp.sum(jnp.where(ci[: x.shape[0]] == p, x, 0.0), axis=1, keepdims=True)

    def step(j, carry):
        m, b = carry
        p, q = 2 * j, 2 * j + 1
        c0, c1 = pick_col(m, p), pick_col(m, q)
        r0, r1 = pick_row(m, ri, p), pick_row(m, ri, q)
        s0, s1 = pick_row(b, rb, p), pick_row(b, rb, q)
        a, e = pick_col(r0, p), pick_col(r0, q)
        c, d = pick_col(r1, p), pick_col(r1, q)
        scale = 1.0 / (a * d - e * c)
        n0, n1 = (d * r0 - e * r1) * scale, (a * r1 - c * r0) * scale
        t0, t1 = (d * s0 - e * s1) * scale, (a * s1 - c * s0) * scale
        m = jnp.where(ri == p, n0, jnp.where(ri == q, n1, m - c0 * n0 - c1 * n1))
        b = jnp.where(rb == p, t0, jnp.where(rb == q, t1, b - c0 * t0 - c1 * t1))
        return m, b

    x = lax.fori_loop(0, n // 2, step, (m, b), unroll=4)[1]
    if o_ref.shape == b.shape:
        o_ref[...] = x
    else:
        o_ref[...] = jnp.sum(jnp.where(ri == ci, x, 0.0), axis=0, keepdims=True)


def spd_solve(m, b):
    shape = (1, b.shape[0]) if b.shape[1] == 1 else b.shape
    return pl.pallas_call(_eliminate, out_shape=jax.ShapeDtypeStruct(shape, b.dtype))(m, b)


def per_device(data, weights, mixing):
    local_scans, ranks, planes, cells = data.shape
    mix_gram = jnp.dot(mixing.T, mixing, precision=highest)
    weight_gram = jnp.dot(weights.T, weights, precision=highest)
    own_weights = lax.dynamic_slice_in_dim(
        weights, lax.axis_index("cuts") * local_scans, local_scans, 0
    )
    scaled = (mixing.T[None, :, :] * own_weights[:, :, None]).transpose(1, 0, 2)
    coefficients = spd_solve(mix_gram * weight_gram, scaled.reshape(ranks, local_scans * ranks))
    coefficients = coefficients.astype(jnp.bfloat16)
    partial = lax.dot_general(
        coefficients, data.reshape(-1, planes, cells), (((1,), (0,)), ((), ())), preferred_element_type=jnp.float32
    )
    cores = 2
    chips = lax.axis_size("cuts") // cores
    paired = exchange(
        partial.reshape(cores, chips, -1, planes, cells), "cuts", 0, size=cores, summed=True
    )
    portion = exchange(paired, "cuts", 4, size=chips, stride=cores, summed=True)
    smoothed = smooth(portion.reshape(-1, planes, cells))
    half_factor = exchange(smoothed, "cuts", 1, whole=True, size=chips, stride=cores)
    factor = exchange(half_factor, "cuts", 5, whole=True, size=cores, space=pl.ANY)
    factor = factor.reshape(ranks, planes, cells)
    factor_half = factor.astype(jnp.bfloat16)
    factor_gram = lax.dot_general(
        factor, factor, (((1, 2), (1, 2)), ((), ())), precision=highest
    )
    products = lax.dot_general(
        data, factor_half, (((2, 3), (1, 2)), ((), ())), preferred_element_type=jnp.float32
    )
    targets = jnp.sum(mixing[None, :, :] * products, axis=1)
    half = ranks // 2
    row = lax.broadcasted_iota(jnp.int32, (half, half), 0)
    col = lax.broadcasted_iota(jnp.int32, (half, half), 1)
    top, off, low = (factor_gram[:half, :half], factor_gram[:half, half:], factor_gram[half:, half:])
    folded = jnp.where(row >= col, top, low)
    folded, off, low_diag, targets = packed_total(
        (folded, off, jnp.sum(jnp.where(row == col, low, 0.0), axis=1), targets), "col"
    )
    top = jnp.where(row >= col, folded, folded.T)
    low = jnp.where(row < col, folded, jnp.where(row > col, folded.T, low_diag[:, None]))
    factor_gram = jnp.concatenate(
        [jnp.concatenate([top, off], axis=1), jnp.concatenate([off.T, low], axis=1)], axis=0
    )
    updated = spd_solve(mix_gram * factor_gram, targets.T)
    return (factor, updated)


def solution(mesh):
    return jax.shard_map(
        per_device,
        mesh=mesh,
        in_specs=(P("cuts", None, "col", None), P(), P()),
        out_specs=(P(None, "col", None), P("cuts", None)),
        check_vma=False,
    )
```

```python
import functools
import jax
import jax.numpy as jnp
from jax import lax
from jax.sharding import PartitionSpec as P
from jax.experimental import pallas as pl
from jax.experimental.pallas import tpu as pltpu

MESH = pl.DeviceIdType.MESH

GRID = 32
ITERS = 3


strength = 0.5
highest = lax.Precision.HIGHEST
low_edge = 1.0
high_edge = 1.0 + 12.0 * strength
centre = (high_edge + low_edge) / 2.0
spread = (high_edge - low_edge) / 2.0


def extended_2(cells, sides, width):
    for axis, dim in sides:
        count = lax.axis_size(axis)
        ends = count - 1
        head = lax.slice_in_dim(cells, 0, width, axis=dim)
        tail = lax.slice_in_dim(cells, cells.shape[dim] - width, cells.shape[dim], axis=dim)
        cells = jnp.concatenate(
            [
                lax.ppermute(tail, axis, [(i, (i + 1) % count) for i in range(ends)]),
                cells,
                lax.ppermute(head, axis, [((i + 1) % count, i) for i in range(ends)]),
            ],
            axis=dim,
        )
    return cells


def _exchange_kernel(axis, other, size, stride, whole, summed, x_ref, o_ref, *scratch):
    if summed:
        send_sem, recv_sem, own_sem, got = scratch
    else:
        (send_sem, recv_sem, own_sem), got = scratch, o_ref
    me = lax.axis_index(axis)
    fixed = lax.axis_index(other)
    pos = (me // stride) % size
    base = me - pos * stride

    def where(peer_pos):
        peer = base + peer_pos * stride
        return (peer, fixed) if axis == "cuts" else (fixed, peer)

    def part(peer_pos):
        return x_ref if whole else x_ref.at[peer_pos]

    barrier = pltpu.get_barrier_semaphore()
    for d in range(1, size):
        pl.semaphore_signal(
            barrier, inc=1, device_id=where((pos + d) % size), device_id_type=MESH
        )
    pl.semaphore_wait(barrier, size - 1)
    own = pltpu.make_async_copy(part(pos), got.at[pos], own_sem)
    own.start()
    copies = []
    for d in range(1, size):
        peer_pos = (pos + d) % size
        copy = pltpu.make_async_remote_copy(
            src_ref=part(peer_pos),
            dst_ref=got.at[pos],
            send_sem=send_sem.at[peer_pos],
            recv_sem=recv_sem.at[pos],
            device_id=where(peer_pos),
            device_id_type=MESH,
        )
        copy.start()
        copies.append(copy)
    for copy in copies:
        copy.wait_send()
    for d in range(1, size):
        source = (pos + size - d) % size
        pltpu.make_async_remote_copy(
            src_ref=part(source),
            dst_ref=got.at[source],
            send_sem=send_sem.at[source],
            recv_sem=recv_sem.at[source],
            device_id=where(source),
            device_id_type=MESH,
        ).wait_recv()
    own.wait()
    if summed:
        total = got[0]
        for slot in range(1, size):
            total = total + got[slot]
        o_ref[...] = total


def exchange(x, axis, key, whole=False, size=None, stride=1, summed=False, space=None):
    other = "col" if axis == "cuts" else "cuts"
    size = size or lax.axis_size(axis)
    shape = (size, *x.shape) if whole else x.shape
    scratch = [
        pltpu.SemaphoreType.DMA((size,)),
        pltpu.SemaphoreType.DMA((size,)),
        pltpu.SemaphoreType.DMA,
    ]
    if summed:
        scratch.append(pltpu.VMEM(shape, x.dtype))
        shape = shape[1:]
    return pl.pallas_call(
        functools.partial(_exchange_kernel, axis, other, size, stride, whole, summed),
        out_shape=jax.ShapeDtypeStruct(shape, x.dtype),
        in_specs=[pl.BlockSpec(memory_space=pltpu.VMEM)],
        out_specs=pl.BlockSpec(memory_space=space or pltpu.VMEM),
        scratch_shapes=scratch,
        compiler_params=pltpu.CompilerParams(collective_id=key, has_side_effects=True),
    )(x)


def _halo_kernel(n, head_ref, tail_ref, below_ref, above_ref, send_sem, recv_sem):
    me = lax.axis_index("col")
    fixed = lax.axis_index("cuts")
    has_left = (me + n - 1) // n
    has_right = 1 - me // (n - 1)
    left, right = (fixed, me - has_left), (fixed, me + has_right)

    def to_left():
        return pltpu.make_async_remote_copy(
            src_ref=head_ref, dst_ref=above_ref, send_sem=send_sem.at[0],
            recv_sem=recv_sem.at[1], device_id=left, device_id_type=MESH,
        )

    def to_right():
        return pltpu.make_async_remote_copy(
            src_ref=tail_ref, dst_ref=below_ref, send_sem=send_sem.at[1],
            recv_sem=recv_sem.at[0], device_id=right, device_id_type=MESH,
        )

    barrier = pltpu.get_barrier_semaphore()

    @pl.when(me > 0)
    def _():
        pl.semaphore_signal(barrier, inc=1, device_id=left, device_id_type=MESH)

    @pl.when(me < n - 1)
    def _():
        pl.semaphore_signal(barrier, inc=1, device_id=right, device_id_type=MESH)

    pl.semaphore_wait(barrier, has_left + has_right)

    @pl.when(me == 0)
    def _():
        below_ref[...] = jnp.zeros_like(below_ref)

    @pl.when(me == n - 1)
    def _():
        above_ref[...] = jnp.zeros_like(above_ref)

    @pl.when(me > 0)
    def _():
        to_left().start()

    @pl.when(me < n - 1)
    def _():
        to_right().start()

    @pl.when(me > 0)
    def _():
        to_left().wait_send()
        pltpu.make_async_remote_copy(
            src_ref=tail_ref, dst_ref=below_ref, send_sem=send_sem.at[1],
            recv_sem=recv_sem.at[0], device_id=left, device_id_type=MESH,
        ).wait_recv()

    @pl.when(me < n - 1)
    def _():
        to_right().wait_send()
        pltpu.make_async_remote_copy(
            src_ref=head_ref, dst_ref=above_ref, send_sem=send_sem.at[0],
            recv_sem=recv_sem.at[1], device_id=right, device_id_type=MESH,
        ).wait_recv()


def with_halo(cells, width):
    n = lax.axis_size("col")
    head = lax.slice_in_dim(cells, 0, width, axis=1)
    tail = lax.slice_in_dim(cells, cells.shape[1] - width, cells.shape[1], axis=1)
    below, above = pl.pallas_call(
        functools.partial(_halo_kernel, n),
        out_shape=(jax.ShapeDtypeStruct(head.shape, head.dtype),) * 2,
        in_specs=[pl.BlockSpec(memory_space=pltpu.VMEM)] * 2,
        out_specs=(pl.BlockSpec(memory_space=pltpu.VMEM),) * 2,
        scratch_shapes=[pltpu.SemaphoreType.DMA((2,)), pltpu.SemaphoreType.DMA((2,))],
        compiler_params=pltpu.CompilerParams(collective_id=3, has_side_effects=True),
    )(head, tail)
    return jnp.concatenate([below, cells, above], axis=1)


def split_up(shard, dim, devices):
    before, after = (shard.shape[:dim], shard.shape[dim + 1 :])
    return jnp.moveaxis(shard.reshape(*before, devices, -1, *after), dim, 0)


def sent_and_summed(shard, axis, dim):
    tiles = split_up(shard, dim, lax.axis_size(axis))
    arrived = exchange(tiles, axis, 0)
    return arrived.sum(axis=0)


def joined_along(tiles, dim):
    dims = list(tiles.shape[1:])
    dims[dim] *= tiles.shape[0]
    return jnp.moveaxis(tiles, 0, dim).reshape(dims)


def from_everyone(shard, axis):
    return exchange(shard, axis, 1 if axis == "cuts" else 2, whole=True)


def gather_directly(shard, axis, dim):
    return joined_along(from_everyone(shard, axis), dim)


def taken_together(shard, axis):
    return from_everyone(shard, axis).sum(axis=0)


def packed_total(arrays, axis):
    line, at, done = (jnp.concatenate([a.reshape(-1) for a in arrays]), 0, [])
    running = taken_together(line, axis)
    for a in arrays:
        done.append(running[at : at + a.size].reshape(a.shape))
        at += a.size
    return tuple(done)


def operate(extended):
    channels, depth, cells = extended.shape
    edge = GRID
    interior = extended[:, 1:-1]
    column = jnp.arange(cells, dtype=jnp.int32) % edge
    has_left = (column > 0).astype(jnp.float32)
    has_right = (column < edge - 1).astype(jnp.float32)
    left_part = jnp.pad(interior, ((0, 0), (0, 0), (1, 0)))[:, :, :-1] * has_left
    right_part = jnp.pad(interior, ((0, 0), (0, 0), (0, 1)))[:, :, 1:] * has_right
    upper_part = jnp.pad(interior, ((0, 0), (0, 0), (edge, 0)))[:, :, :-edge]
    lower_part = jnp.pad(interior, ((0, 0), (0, 0), (0, edge)))[:, :, edge:]
    neighbours = extended[:, 2:] + extended[:, :-2]
    neighbours = neighbours + left_part + right_part + upper_part + lower_part
    return interior + strength * (6.0 * interior - neighbours)


def smooth_once(source):
    planes = source.shape[1]
    extended = with_halo(source, ITERS)
    first_plane = lax.axis_index("col") * planes - ITERS
    total_planes = planes * lax.axis_size("col")
    levels = first_plane + jnp.arange(planes + 2 * ITERS, dtype=jnp.int32)
    inside = ((levels >= 0) & (levels < total_planes)).astype(jnp.float32)[None, :, None]
    solution = jnp.zeros_like(source)
    residual = extended
    direction = extended / centre
    ratio = spread / centre
    for iteration in range(ITERS):
        margin = ITERS - iteration
        solution = solution + direction[:, margin : margin + planes]
        window = inside[:, iteration + 1 : iteration + 1 + planes + 2 * (margin - 1)]
        residual = (residual[:, 1:-1] - operate(direction)) * window
        ratio_next = 1.0 / (2.0 * centre / spread - ratio)
        direction = ratio_next * ratio * direction[:, 1:-1] + 2.0 * ratio_next / spread * residual
        ratio = ratio_next
    return solution + direction


def smooth(source):
    return smooth_once(source)


def _eliminate(m_ref, b_ref, o_ref):
    m = m_ref[...]
    b = b_ref[...]
    n = m.shape[0]
    ri = lax.broadcasted_iota(jnp.int32, m.shape, 0)
    ci = lax.broadcasted_iota(jnp.int32, m.shape, 1)
    rb = lax.broadcasted_iota(jnp.int32, b.shape, 0)

    def pick_row(x, rows, p):
        return jnp.sum(jnp.where(rows == p, x, 0.0), axis=0, keepdims=True)

    def pick_col(x, p):
        return jnp.sum(jnp.where(ci[: x.shape[0]] == p, x, 0.0), axis=1, keepdims=True)

    def step(j, carry):
        m, b = carry
        p, q = 2 * j, 2 * j + 1
        c0, c1 = pick_col(m, p), pick_col(m, q)
        r0, r1 = pick_row(m, ri, p), pick_row(m, ri, q)
        s0, s1 = pick_row(b, rb, p), pick_row(b, rb, q)
        a, e = pick_col(r0, p), pick_col(r0, q)
        c, d = pick_col(r1, p), pick_col(r1, q)
        scale = 1.0 / (a * d - e * c)
        n0, n1 = (d * r0 - e * r1) * scale, (a * r1 - c * r0) * scale
        t0, t1 = (d * s0 - e * s1) * scale, (a * s1 - c * s0) * scale
        m = jnp.where(ri == p, n0, jnp.where(ri == q, n1, m - c0 * n0 - c1 * n1))
        b = jnp.where(rb == p, t0, jnp.where(rb == q, t1, b - c0 * t0 - c1 * t1))
        return m, b

    x = lax.fori_loop(0, n // 2, step, (m, b), unroll=4)[1]
    if o_ref.shape == b.shape:
        o_ref[...] = x.astype(o_ref.dtype)
    else:
        o_ref[...] = jnp.sum(jnp.where(ri == ci, x, 0.0), axis=0, keepdims=True)


def spd_solve(m, b, dtype=None):
    shape = (1, b.shape[0]) if b.shape[1] == 1 else b.shape
    return pl.pallas_call(
        _eliminate, out_shape=jax.ShapeDtypeStruct(shape, dtype or b.dtype)
    )(m, b)


def per_device(data, weights, mixing):
    local_scans, ranks, planes, cells = data.shape
    mix_gram = jnp.dot(mixing.T, mixing, precision=highest)
    weight_gram = jnp.dot(weights.T, weights, precision=highest)
    own_weights = lax.dynamic_slice_in_dim(
        weights, lax.axis_index("cuts") * local_scans, local_scans, 0
    )
    scaled = (mixing.T[None, :, :] * own_weights[:, :, None]).transpose(1, 0, 2)
    coefficients = spd_solve(
        mix_gram * weight_gram, scaled.reshape(ranks, local_scans * ranks), jnp.bfloat16
    )
    partial = lax.dot_general(
        coefficients, data.reshape(-1, planes, cells), (((1,), (0,)), ((), ())), preferred_element_type=jnp.float32
    )
    cores = 2
    chips = lax.axis_size("cuts") // cores
    paired = exchange(
        partial.reshape(cores, chips, -1, planes, cells), "cuts", 0, size=cores, summed=True
    )
    portion = exchange(paired, "cuts", 4, size=chips, stride=cores, summed=True)
    smoothed = smooth(portion.reshape(-1, planes, cells))
    half_factor = exchange(smoothed, "cuts", 1, whole=True, size=chips, stride=cores)
    factor = exchange(half_factor, "cuts", 5, whole=True, size=cores, space=pl.ANY)
    factor = factor.reshape(ranks, planes, cells)
    factor_half = factor.astype(jnp.bfloat16)
    factor_gram = lax.dot_general(
        factor, factor, (((1, 2), (1, 2)), ((), ())), precision=lax.Precision.HIGH
    )
    products = lax.dot_general(
        data, factor_half, (((2, 3), (1, 2)), ((), ())), preferred_element_type=jnp.float32
    )
    targets = jnp.sum(mixing[None, :, :] * products, axis=1)
    half = ranks // 2
    row = lax.broadcasted_iota(jnp.int32, (half, half), 0)
    col = lax.broadcasted_iota(jnp.int32, (half, half), 1)
    top, off, low = (factor_gram[:half, :half], factor_gram[:half, half:], factor_gram[half:, half:])
    folded = jnp.where(row >= col, top, low)
    folded, off, low_diag, targets = packed_total(
        (folded, off, jnp.sum(jnp.where(row == col, low, 0.0), axis=1), targets), "col"
    )
    top = jnp.where(row >= col, folded, folded.T)
    low = jnp.where(row < col, folded, jnp.where(row > col, folded.T, low_diag[:, None]))
    factor_gram = jnp.concatenate(
        [jnp.concatenate([top, off], axis=1), jnp.concatenate([off.T, low], axis=1)], axis=0
    )
    updated = spd_solve(mix_gram * factor_gram, targets.T)
    return (factor, updated)


def solution(mesh):
    return jax.shard_map(
        per_device,
        mesh=mesh,
        in_specs=(P("cuts", None, "col", None), P(), P()),
        out_specs=(P(None, "col", None), P("cuts", None)),
        check_vma=False,
    )
```

```python
import functools
import jax
import jax.numpy as jnp
from jax import lax
from jax.sharding import PartitionSpec as P
from jax.experimental import pallas as pl
from jax.experimental.pallas import tpu as pltpu

MESH = pl.DeviceIdType.MESH

GRID = 32
ITERS = 3


strength = 0.5
highest = lax.Precision.HIGHEST
low_edge = 1.0
high_edge = 1.0 + 12.0 * strength
centre = (high_edge + low_edge) / 2.0
spread = (high_edge - low_edge) / 2.0


def extended_2(cells, sides, width):
    for axis, dim in sides:
        count = lax.axis_size(axis)
        ends = count - 1
        head = lax.slice_in_dim(cells, 0, width, axis=dim)
        tail = lax.slice_in_dim(cells, cells.shape[dim] - width, cells.shape[dim], axis=dim)
        cells = jnp.concatenate(
            [
                lax.ppermute(tail, axis, [(i, (i + 1) % count) for i in range(ends)]),
                cells,
                lax.ppermute(head, axis, [((i + 1) % count, i) for i in range(ends)]),
            ],
            axis=dim,
        )
    return cells


def _exchange_kernel(axis, other, size, stride, whole, summed, x_ref, o_ref, *scratch):
    if summed:
        send_sem, recv_sem, own_sem, got = scratch
    else:
        (send_sem, recv_sem, own_sem), got = scratch, o_ref
    me = lax.axis_index(axis)
    fixed = lax.axis_index(other)
    pos = (me // stride) % size
    base = me - pos * stride

    def where(peer_pos):
        peer = base + peer_pos * stride
        return (peer, fixed) if axis == "cuts" else (fixed, peer)

    def part(peer_pos):
        return x_ref if whole else x_ref.at[peer_pos]

    barrier = pltpu.get_barrier_semaphore()
    for d in range(1, size):
        pl.semaphore_signal(
            barrier, inc=1, device_id=where((pos + d) % size), device_id_type=MESH
        )
    pl.semaphore_wait(barrier, size - 1)
    own = pltpu.make_async_copy(part(pos), got.at[pos], own_sem)
    own.start()
    copies = []
    for d in range(1, size):
        peer_pos = (pos + d) % size
        copy = pltpu.make_async_remote_copy(
            src_ref=part(peer_pos),
            dst_ref=got.at[pos],
            send_sem=send_sem.at[peer_pos],
            recv_sem=recv_sem.at[pos],
            device_id=where(peer_pos),
            device_id_type=MESH,
        )
        copy.start()
        copies.append(copy)
    for copy in copies:
        copy.wait_send()
    for d in range(1, size):
        source = (pos + size - d) % size
        pltpu.make_async_remote_copy(
            src_ref=part(source),
            dst_ref=got.at[source],
            send_sem=send_sem.at[source],
            recv_sem=recv_sem.at[source],
            device_id=where(source),
            device_id_type=MESH,
        ).wait_recv()
    own.wait()
    if summed:
        total = got[0]
        for slot in range(1, size):
            total = total + got[slot]
        o_ref[...] = total


def exchange(x, axis, key, whole=False, size=None, stride=1, summed=False, space=None):
    other = "col" if axis == "cuts" else "cuts"
    size = size or lax.axis_size(axis)
    shape = (size, *x.shape) if whole else x.shape
    scratch = [
        pltpu.SemaphoreType.DMA((size,)),
        pltpu.SemaphoreType.DMA((size,)),
        pltpu.SemaphoreType.DMA,
    ]
    if summed:
        scratch.append(pltpu.VMEM(shape, x.dtype))
        shape = shape[1:]
    return pl.pallas_call(
        functools.partial(_exchange_kernel, axis, other, size, stride, whole, summed),
        out_shape=jax.ShapeDtypeStruct(shape, x.dtype),
        in_specs=[pl.BlockSpec(memory_space=pltpu.VMEM)],
        out_specs=pl.BlockSpec(memory_space=space or pltpu.VMEM),
        scratch_shapes=scratch,
        compiler_params=pltpu.CompilerParams(collective_id=key, has_side_effects=True),
    )(x)


def _halo_kernel(n, head_ref, tail_ref, below_ref, above_ref, send_sem, recv_sem):
    me = lax.axis_index("col")
    fixed = lax.axis_index("cuts")
    has_left = (me + n - 1) // n
    has_right = 1 - me // (n - 1)
    left, right = (fixed, me - has_left), (fixed, me + has_right)

    def to_left():
        return pltpu.make_async_remote_copy(
            src_ref=head_ref, dst_ref=above_ref, send_sem=send_sem.at[0],
            recv_sem=recv_sem.at[1], device_id=left, device_id_type=MESH,
        )

    def to_right():
        return pltpu.make_async_remote_copy(
            src_ref=tail_ref, dst_ref=below_ref, send_sem=send_sem.at[1],
            recv_sem=recv_sem.at[0], device_id=right, device_id_type=MESH,
        )

    barrier = pltpu.get_barrier_semaphore()

    @pl.when(me > 0)
    def _():
        pl.semaphore_signal(barrier, inc=1, device_id=left, device_id_type=MESH)

    @pl.when(me < n - 1)
    def _():
        pl.semaphore_signal(barrier, inc=1, device_id=right, device_id_type=MESH)

    pl.semaphore_wait(barrier, has_left + has_right)

    @pl.when(me == 0)
    def _():
        below_ref[...] = jnp.zeros_like(below_ref)

    @pl.when(me == n - 1)
    def _():
        above_ref[...] = jnp.zeros_like(above_ref)

    @pl.when(me > 0)
    def _():
        to_left().start()

    @pl.when(me < n - 1)
    def _():
        to_right().start()

    @pl.when(me > 0)
    def _():
        to_left().wait_send()
        pltpu.make_async_remote_copy(
            src_ref=tail_ref, dst_ref=below_ref, send_sem=send_sem.at[1],
            recv_sem=recv_sem.at[0], device_id=left, device_id_type=MESH,
        ).wait_recv()

    @pl.when(me < n - 1)
    def _():
        to_right().wait_send()
        pltpu.make_async_remote_copy(
            src_ref=head_ref, dst_ref=above_ref, send_sem=send_sem.at[0],
            recv_sem=recv_sem.at[1], device_id=right, device_id_type=MESH,
        ).wait_recv()


def with_halo(cells, width):
    n = lax.axis_size("col")
    head = lax.slice_in_dim(cells, 0, width, axis=1)
    tail = lax.slice_in_dim(cells, cells.shape[1] - width, cells.shape[1], axis=1)
    below, above = pl.pallas_call(
        functools.partial(_halo_kernel, n),
        out_shape=(jax.ShapeDtypeStruct(head.shape, head.dtype),) * 2,
        in_specs=[pl.BlockSpec(memory_space=pltpu.VMEM)] * 2,
        out_specs=(pl.BlockSpec(memory_space=pltpu.VMEM),) * 2,
        scratch_shapes=[pltpu.SemaphoreType.DMA((2,)), pltpu.SemaphoreType.DMA((2,))],
        compiler_params=pltpu.CompilerParams(collective_id=3, has_side_effects=True),
    )(head, tail)
    return jnp.concatenate([below, cells, above], axis=1)


def split_up(shard, dim, devices):
    before, after = (shard.shape[:dim], shard.shape[dim + 1 :])
    return jnp.moveaxis(shard.reshape(*before, devices, -1, *after), dim, 0)


def sent_and_summed(shard, axis, dim):
    tiles = split_up(shard, dim, lax.axis_size(axis))
    arrived = exchange(tiles, axis, 0)
    return arrived.sum(axis=0)


def joined_along(tiles, dim):
    dims = list(tiles.shape[1:])
    dims[dim] *= tiles.shape[0]
    return jnp.moveaxis(tiles, 0, dim).reshape(dims)


def from_everyone(shard, axis):
    return exchange(shard, axis, 1 if axis == "cuts" else 2, whole=True)


def gather_directly(shard, axis, dim):
    return joined_along(from_everyone(shard, axis), dim)


def taken_together(shard, axis):
    return exchange(shard, axis, 2, whole=True, summed=True)


def packed_total(arrays, axis):
    line, at, done = (jnp.concatenate([a.reshape(-1) for a in arrays]), 0, [])
    running = taken_together(line, axis)
    for a in arrays:
        done.append(running[at : at + a.size].reshape(a.shape))
        at += a.size
    return tuple(done)


def operate(extended):
    channels, depth, cells = extended.shape
    edge = GRID
    interior = extended[:, 1:-1]
    column = jnp.arange(cells, dtype=jnp.int32) % edge
    has_left = (column > 0).astype(jnp.float32)
    has_right = (column < edge - 1).astype(jnp.float32)
    left_part = jnp.pad(interior, ((0, 0), (0, 0), (1, 0)))[:, :, :-1] * has_left
    right_part = jnp.pad(interior, ((0, 0), (0, 0), (0, 1)))[:, :, 1:] * has_right
    upper_part = jnp.pad(interior, ((0, 0), (0, 0), (edge, 0)))[:, :, :-edge]
    lower_part = jnp.pad(interior, ((0, 0), (0, 0), (0, edge)))[:, :, edge:]
    neighbours = extended[:, 2:] + extended[:, :-2]
    neighbours = neighbours + left_part + right_part + upper_part + lower_part
    return interior + strength * (6.0 * interior - neighbours)


def smooth_once(source):
    planes = source.shape[1]
    extended = with_halo(source, ITERS)
    first_plane = lax.axis_index("col") * planes - ITERS
    total_planes = planes * lax.axis_size("col")
    levels = first_plane + jnp.arange(planes + 2 * ITERS, dtype=jnp.int32)
    inside = ((levels >= 0) & (levels < total_planes)).astype(jnp.float32)[None, :, None]
    solution = jnp.zeros_like(source)
    residual = extended
    direction = extended / centre
    ratio = spread / centre
    for iteration in range(ITERS):
        margin = ITERS - iteration
        solution = solution + direction[:, margin : margin + planes]
        window = inside[:, iteration + 1 : iteration + 1 + planes + 2 * (margin - 1)]
        residual = (residual[:, 1:-1] - operate(direction)) * window
        ratio_next = 1.0 / (2.0 * centre / spread - ratio)
        direction = ratio_next * ratio * direction[:, 1:-1] + 2.0 * ratio_next / spread * residual
        ratio = ratio_next
    return solution + direction


def smooth(source):
    return smooth_once(source)


def _eliminate(m_ref, b_ref, o_ref):
    m = m_ref[...]
    b = b_ref[...]
    n = m.shape[0]
    ri = lax.broadcasted_iota(jnp.int32, m.shape, 0)
    ci = lax.broadcasted_iota(jnp.int32, m.shape, 1)
    rb = lax.broadcasted_iota(jnp.int32, b.shape, 0)

    def pick_row(x, rows, p):
        return jnp.sum(jnp.where(rows == p, x, 0.0), axis=0, keepdims=True)

    def pick_col(x, p):
        return jnp.sum(jnp.where(ci[: x.shape[0]] == p, x, 0.0), axis=1, keepdims=True)

    def step(j, carry):
        m, b = carry
        p, q = 2 * j, 2 * j + 1
        c0, c1 = pick_col(m, p), pick_col(m, q)
        r0, r1 = pick_row(m, ri, p), pick_row(m, ri, q)
        s0, s1 = pick_row(b, rb, p), pick_row(b, rb, q)
        a, e = pick_col(r0, p), pick_col(r0, q)
        c, d = pick_col(r1, p), pick_col(r1, q)
        scale = 1.0 / (a * d - e * c)
        n0, n1 = (d * r0 - e * r1) * scale, (a * r1 - c * r0) * scale
        t0, t1 = (d * s0 - e * s1) * scale, (a * s1 - c * s0) * scale
        m = jnp.where(ri == p, n0, jnp.where(ri == q, n1, m - c0 * n0 - c1 * n1))
        b = jnp.where(rb == p, t0, jnp.where(rb == q, t1, b - c0 * t0 - c1 * t1))
        return m, b

    x = lax.fori_loop(0, n // 2, step, (m, b), unroll=4)[1]
    if o_ref.shape == b.shape:
        o_ref[...] = x.astype(o_ref.dtype)
    else:
        o_ref[...] = jnp.sum(jnp.where(ri == ci, x, 0.0), axis=0, keepdims=True)


def spd_solve(m, b, dtype=None):
    shape = (1, b.shape[0]) if b.shape[1] == 1 else b.shape
    return pl.pallas_call(
        _eliminate, out_shape=jax.ShapeDtypeStruct(shape, dtype or b.dtype)
    )(m, b)


def per_device(data, weights, mixing):
    local_scans, ranks, planes, cells = data.shape
    mix_gram = jnp.dot(mixing.T, mixing, precision=highest)
    weight_gram = jnp.dot(weights.T, weights, precision=highest)
    own_weights = lax.dynamic_slice_in_dim(
        weights, lax.axis_index("cuts") * local_scans, local_scans, 0
    )
    scaled = (mixing.T[None, :, :] * own_weights[:, :, None]).transpose(1, 0, 2)
    coefficients = spd_solve(
        mix_gram * weight_gram, scaled.reshape(ranks, local_scans * ranks), jnp.bfloat16
    )
    partial = lax.dot_general(
        coefficients, data.reshape(-1, planes, cells), (((1,), (0,)), ((), ())), preferred_element_type=jnp.float32
    )
    cores = 2
    chips = lax.axis_size("cuts") // cores
    paired = exchange(
        partial.reshape(cores, chips, -1, planes, cells), "cuts", 0, size=cores, summed=True
    )
    portion = exchange(paired, "cuts", 4, size=chips, stride=cores, summed=True)
    smoothed = smooth(portion.reshape(-1, planes, cells))
    half_factor = exchange(smoothed, "cuts", 1, whole=True, size=chips, stride=cores)
    factor = exchange(half_factor, "cuts", 5, whole=True, size=cores, space=pl.ANY)
    factor = factor.reshape(ranks, planes, cells)
    factor_half = factor.astype(jnp.bfloat16)
    factor_gram = lax.dot_general(
        factor, factor, (((1, 2), (1, 2)), ((), ())), precision=lax.Precision.HIGH
    )
    products = lax.dot_general(
        data, factor_half, (((2, 3), (1, 2)), ((), ())), preferred_element_type=jnp.float32
    )
    targets = jnp.sum(mixing[None, :, :] * products, axis=1)
    half = ranks // 2
    row = lax.broadcasted_iota(jnp.int32, (half, half), 0)
    col = lax.broadcasted_iota(jnp.int32, (half, half), 1)
    top, off, low = (factor_gram[:half, :half], factor_gram[:half, half:], factor_gram[half:, half:])
    folded = jnp.where(row >= col, top, low)
    folded, off, low_diag, targets = packed_total(
        (folded, off, jnp.sum(jnp.where(row == col, low, 0.0), axis=1), targets), "col"
    )
    top = jnp.where(row >= col, folded, folded.T)
    low = jnp.where(row < col, folded, jnp.where(row > col, folded.T, low_diag[:, None]))
    factor_gram = jnp.concatenate(
        [jnp.concatenate([top, off], axis=1), jnp.concatenate([off.T, low], axis=1)], axis=0
    )
    updated = spd_solve(mix_gram * factor_gram, targets.T)
    return (factor, updated)


def solution(mesh):
    return jax.shard_map(
        per_device,
        mesh=mesh,
        in_specs=(P("cuts", None, "col", None), P(), P()),
        out_specs=(P(None, "col", None), P("cuts", None)),
        check_vma=False,
    )
```

```python
import functools
import jax
import jax.numpy as jnp
from jax import lax
from jax.sharding import PartitionSpec as P
from jax.experimental import pallas as pl
from jax.experimental.pallas import tpu as pltpu

MESH = pl.DeviceIdType.MESH

GRID = 32
ITERS = 3


strength = 0.5
highest = lax.Precision.HIGHEST
low_edge = 1.0
high_edge = 1.0 + 12.0 * strength
centre = (high_edge + low_edge) / 2.0
spread = (high_edge - low_edge) / 2.0


def extended_2(cells, sides, width):
    for axis, dim in sides:
        count = lax.axis_size(axis)
        ends = count - 1
        head = lax.slice_in_dim(cells, 0, width, axis=dim)
        tail = lax.slice_in_dim(cells, cells.shape[dim] - width, cells.shape[dim], axis=dim)
        cells = jnp.concatenate(
            [
                lax.ppermute(tail, axis, [(i, (i + 1) % count) for i in range(ends)]),
                cells,
                lax.ppermute(head, axis, [((i + 1) % count, i) for i in range(ends)]),
            ],
            axis=dim,
        )
    return cells


def _exchange_kernel(axis, other, size, stride, whole, summed, x_ref, o_ref, *scratch):
    if summed:
        send_sem, recv_sem, own_sem, got = scratch
    else:
        (send_sem, recv_sem, own_sem), got = scratch, o_ref
    me = lax.axis_index(axis)
    fixed = lax.axis_index(other)
    pos = (me // stride) % size
    base = me - pos * stride

    def where(peer_pos):
        peer = base + peer_pos * stride
        return (peer, fixed) if axis == "cuts" else (fixed, peer)

    def part(peer_pos):
        return x_ref if whole else x_ref.at[peer_pos]

    barrier = pltpu.get_barrier_semaphore()
    for d in range(1, size):
        pl.semaphore_signal(
            barrier, inc=1, device_id=where((pos + d) % size), device_id_type=MESH
        )
    pl.semaphore_wait(barrier, size - 1)
    own = pltpu.make_async_copy(part(pos), got.at[pos], own_sem)
    own.start()
    copies = []
    for d in range(1, size):
        peer_pos = (pos + d) % size
        copy = pltpu.make_async_remote_copy(
            src_ref=part(peer_pos),
            dst_ref=got.at[pos],
            send_sem=send_sem.at[peer_pos],
            recv_sem=recv_sem.at[pos],
            device_id=where(peer_pos),
            device_id_type=MESH,
        )
        copy.start()
        copies.append(copy)
    for copy in copies:
        copy.wait_send()
    for d in range(1, size):
        source = (pos + size - d) % size
        pltpu.make_async_remote_copy(
            src_ref=part(source),
            dst_ref=got.at[source],
            send_sem=send_sem.at[source],
            recv_sem=recv_sem.at[source],
            device_id=where(source),
            device_id_type=MESH,
        ).wait_recv()
    own.wait()
    if summed:
        total = got[0]
        for slot in range(1, size):
            total = total + got[slot]
        o_ref[...] = total


def exchange(x, axis, key, whole=False, size=None, stride=1, summed=False, space=None):
    other = "col" if axis == "cuts" else "cuts"
    size = size or lax.axis_size(axis)
    shape = (size, *x.shape) if whole else x.shape
    scratch = [
        pltpu.SemaphoreType.DMA((size,)),
        pltpu.SemaphoreType.DMA((size,)),
        pltpu.SemaphoreType.DMA,
    ]
    if summed:
        scratch.append(pltpu.VMEM(shape, x.dtype))
        shape = shape[1:]
    return pl.pallas_call(
        functools.partial(_exchange_kernel, axis, other, size, stride, whole, summed),
        out_shape=jax.ShapeDtypeStruct(shape, x.dtype),
        in_specs=[pl.BlockSpec(memory_space=pltpu.VMEM)],
        out_specs=pl.BlockSpec(memory_space=space or pltpu.VMEM),
        scratch_shapes=scratch,
        compiler_params=pltpu.CompilerParams(collective_id=key, has_side_effects=True),
    )(x)


def _halo_kernel(n, head_ref, tail_ref, below_ref, above_ref, send_sem, recv_sem):
    me = lax.axis_index("col")
    fixed = lax.axis_index("cuts")
    has_left = (me + n - 1) // n
    has_right = 1 - me // (n - 1)
    left, right = (fixed, me - has_left), (fixed, me + has_right)

    def to_left():
        return pltpu.make_async_remote_copy(
            src_ref=head_ref, dst_ref=above_ref, send_sem=send_sem.at[0],
            recv_sem=recv_sem.at[1], device_id=left, device_id_type=MESH,
        )

    def to_right():
        return pltpu.make_async_remote_copy(
            src_ref=tail_ref, dst_ref=below_ref, send_sem=send_sem.at[1],
            recv_sem=recv_sem.at[0], device_id=right, device_id_type=MESH,
        )

    barrier = pltpu.get_barrier_semaphore()

    @pl.when(me > 0)
    def _():
        pl.semaphore_signal(barrier, inc=1, device_id=left, device_id_type=MESH)

    @pl.when(me < n - 1)
    def _():
        pl.semaphore_signal(barrier, inc=1, device_id=right, device_id_type=MESH)

    pl.semaphore_wait(barrier, has_left + has_right)

    @pl.when(me == 0)
    def _():
        below_ref[...] = jnp.zeros_like(below_ref)

    @pl.when(me == n - 1)
    def _():
        above_ref[...] = jnp.zeros_like(above_ref)

    @pl.when(me > 0)
    def _():
        to_left().start()

    @pl.when(me < n - 1)
    def _():
        to_right().start()

    @pl.when(me > 0)
    def _():
        to_left().wait_send()
        pltpu.make_async_remote_copy(
            src_ref=tail_ref, dst_ref=below_ref, send_sem=send_sem.at[1],
            recv_sem=recv_sem.at[0], device_id=left, device_id_type=MESH,
        ).wait_recv()

    @pl.when(me < n - 1)
    def _():
        to_right().wait_send()
        pltpu.make_async_remote_copy(
            src_ref=head_ref, dst_ref=above_ref, send_sem=send_sem.at[0],
            recv_sem=recv_sem.at[1], device_id=right, device_id_type=MESH,
        ).wait_recv()


def with_halo(cells, width):
    n = lax.axis_size("col")
    head = lax.slice_in_dim(cells, 0, width, axis=1)
    tail = lax.slice_in_dim(cells, cells.shape[1] - width, cells.shape[1], axis=1)
    below, above = pl.pallas_call(
        functools.partial(_halo_kernel, n),
        out_shape=(jax.ShapeDtypeStruct(head.shape, head.dtype),) * 2,
        in_specs=[pl.BlockSpec(memory_space=pltpu.VMEM)] * 2,
        out_specs=(pl.BlockSpec(memory_space=pltpu.VMEM),) * 2,
        scratch_shapes=[pltpu.SemaphoreType.DMA((2,)), pltpu.SemaphoreType.DMA((2,))],
        compiler_params=pltpu.CompilerParams(collective_id=3, has_side_effects=True),
    )(head, tail)
    return jnp.concatenate([below, cells, above], axis=1)


def split_up(shard, dim, devices):
    before, after = (shard.shape[:dim], shard.shape[dim + 1 :])
    return jnp.moveaxis(shard.reshape(*before, devices, -1, *after), dim, 0)


def sent_and_summed(shard, axis, dim):
    tiles = split_up(shard, dim, lax.axis_size(axis))
    arrived = exchange(tiles, axis, 0)
    return arrived.sum(axis=0)


def joined_along(tiles, dim):
    dims = list(tiles.shape[1:])
    dims[dim] *= tiles.shape[0]
    return jnp.moveaxis(tiles, 0, dim).reshape(dims)


def from_everyone(shard, axis):
    return exchange(shard, axis, 1 if axis == "cuts" else 2, whole=True)


def gather_directly(shard, axis, dim):
    return joined_along(from_everyone(shard, axis), dim)


def taken_together(shard, axis):
    return from_everyone(shard, axis).sum(axis=0)


def packed_total(arrays, axis):
    line, at, done = (jnp.concatenate([a.reshape(-1) for a in arrays]), 0, [])
    running = taken_together(line, axis)
    for a in arrays:
        done.append(running[at : at + a.size].reshape(a.shape))
        at += a.size
    return tuple(done)


def operate(extended):
    channels, depth, cells = extended.shape
    edge = GRID
    interior = extended[:, 1:-1]
    column = jnp.arange(cells, dtype=jnp.int32) % edge
    has_left = (column > 0).astype(jnp.float32)
    has_right = (column < edge - 1).astype(jnp.float32)
    left_part = jnp.pad(interior, ((0, 0), (0, 0), (1, 0)))[:, :, :-1] * has_left
    right_part = jnp.pad(interior, ((0, 0), (0, 0), (0, 1)))[:, :, 1:] * has_right
    upper_part = jnp.pad(interior, ((0, 0), (0, 0), (edge, 0)))[:, :, :-edge]
    lower_part = jnp.pad(interior, ((0, 0), (0, 0), (0, edge)))[:, :, edge:]
    neighbours = extended[:, 2:] + extended[:, :-2]
    neighbours = neighbours + left_part + right_part + upper_part + lower_part
    return interior + strength * (6.0 * interior - neighbours)


def smooth_once(source):
    planes = source.shape[1]
    extended = with_halo(source, ITERS)
    first_plane = lax.axis_index("col") * planes - ITERS
    total_planes = planes * lax.axis_size("col")
    levels = first_plane + jnp.arange(planes + 2 * ITERS, dtype=jnp.int32)
    inside = ((levels >= 0) & (levels < total_planes)).astype(jnp.float32)[None, :, None]
    solution = jnp.zeros_like(source)
    residual = extended
    direction = extended / centre
    ratio = spread / centre
    for iteration in range(ITERS):
        margin = ITERS - iteration
        solution = solution + direction[:, margin : margin + planes]
        window = inside[:, iteration + 1 : iteration + 1 + planes + 2 * (margin - 1)]
        residual = (residual[:, 1:-1] - operate(direction)) * window
        ratio_next = 1.0 / (2.0 * centre / spread - ratio)
        direction = ratio_next * ratio * direction[:, 1:-1] + 2.0 * ratio_next / spread * residual
        ratio = ratio_next
    return solution + direction


def smooth(source):
    return smooth_once(source)


def _eliminate(m_ref, b_ref, o_ref):
    m = m_ref[...]
    b = b_ref[...]
    n = m.shape[0]
    ri = lax.broadcasted_iota(jnp.int32, m.shape, 0)
    ci = lax.broadcasted_iota(jnp.int32, m.shape, 1)
    rb = lax.broadcasted_iota(jnp.int32, b.shape, 0)

    def pick_row(x, rows, p):
        return jnp.sum(jnp.where(rows == p, x, 0.0), axis=0, keepdims=True)

    def pick_col(x, p):
        return jnp.sum(jnp.where(ci[: x.shape[0]] == p, x, 0.0), axis=1, keepdims=True)

    def step(j, carry):
        m, b = carry
        p, q = 2 * j, 2 * j + 1
        c0, c1 = pick_col(m, p), pick_col(m, q)
        r0, r1 = pick_row(m, ri, p), pick_row(m, ri, q)
        s0, s1 = pick_row(b, rb, p), pick_row(b, rb, q)
        a, e = pick_col(r0, p), pick_col(r0, q)
        c, d = pick_col(r1, p), pick_col(r1, q)
        scale = 1.0 / (a * d - e * c)
        n0, n1 = (d * r0 - e * r1) * scale, (a * r1 - c * r0) * scale
        t0, t1 = (d * s0 - e * s1) * scale, (a * s1 - c * s0) * scale
        m = jnp.where(ri == p, n0, jnp.where(ri == q, n1, m - c0 * n0 - c1 * n1))
        b = jnp.where(rb == p, t0, jnp.where(rb == q, t1, b - c0 * t0 - c1 * t1))
        return m, b

    x = lax.fori_loop(0, n // 2, step, (m, b), unroll=True)[1]
    if o_ref.shape == b.shape:
        o_ref[...] = x.astype(o_ref.dtype)
    else:
        o_ref[...] = jnp.sum(jnp.where(ri == ci, x, 0.0), axis=0, keepdims=True)


def spd_solve(m, b, dtype=None):
    shape = (1, b.shape[0]) if b.shape[1] == 1 else b.shape
    return pl.pallas_call(
        _eliminate, out_shape=jax.ShapeDtypeStruct(shape, dtype or b.dtype)
    )(m, b)


def per_device(data, weights, mixing):
    local_scans, ranks, planes, cells = data.shape
    mix_gram = jnp.dot(mixing.T, mixing, precision=highest)
    weight_gram = jnp.dot(weights.T, weights, precision=highest)
    own_weights = lax.dynamic_slice_in_dim(
        weights, lax.axis_index("cuts") * local_scans, local_scans, 0
    )
    scaled = (mixing.T[None, :, :] * own_weights[:, :, None]).transpose(1, 0, 2)
    coefficients = spd_solve(
        mix_gram * weight_gram, scaled.reshape(ranks, local_scans * ranks), jnp.bfloat16
    )
    partial = lax.dot_general(
        coefficients, data.reshape(-1, planes, cells), (((1,), (0,)), ((), ())), preferred_element_type=jnp.float32
    )
    cores = 2
    chips = lax.axis_size("cuts") // cores
    paired = exchange(
        partial.reshape(cores, chips, -1, planes, cells), "cuts", 0, size=cores, summed=True
    )
    portion = exchange(paired, "cuts", 4, size=chips, stride=cores, summed=True)
    smoothed = smooth(portion.reshape(-1, planes, cells))
    half_factor = exchange(smoothed, "cuts", 1, whole=True, size=chips, stride=cores)
    factor = exchange(half_factor, "cuts", 5, whole=True, size=cores, space=pl.ANY)
    factor = factor.reshape(ranks, planes, cells)
    factor_half = factor.astype(jnp.bfloat16)
    factor_gram = lax.dot_general(
        factor, factor, (((1, 2), (1, 2)), ((), ())), precision=lax.Precision.HIGH
    )
    products = lax.dot_general(
        data, factor_half, (((2, 3), (1, 2)), ((), ())), preferred_element_type=jnp.float32
    )
    targets = jnp.sum(mixing[None, :, :] * products, axis=1)
    half = ranks // 2
    row = lax.broadcasted_iota(jnp.int32, (half, half), 0)
    col = lax.broadcasted_iota(jnp.int32, (half, half), 1)
    top, off, low = (factor_gram[:half, :half], factor_gram[:half, half:], factor_gram[half:, half:])
    folded = jnp.where(row >= col, top, low)
    folded, off, low_diag, targets = packed_total(
        (folded, off, jnp.sum(jnp.where(row == col, low, 0.0), axis=1), targets), "col"
    )
    top = jnp.where(row >= col, folded, folded.T)
    low = jnp.where(row < col, folded, jnp.where(row > col, folded.T, low_diag[:, None]))
    factor_gram = jnp.concatenate(
        [jnp.concatenate([top, off], axis=1), jnp.concatenate([off.T, low], axis=1)], axis=0
    )
    updated = spd_solve(mix_gram * factor_gram, targets.T)
    return (factor, updated)


def solution(mesh):
    return jax.shard_map(
        per_device,
        mesh=mesh,
        in_specs=(P("cuts", None, "col", None), P(), P()),
        out_specs=(P(None, "col", None), P("cuts", None)),
        check_vma=False,
    )
```

```python
import functools
import jax
import jax.numpy as jnp
from jax import lax
from jax.sharding import PartitionSpec as P
from jax.experimental import pallas as pl
from jax.experimental.pallas import tpu as pltpu

MESH = pl.DeviceIdType.MESH

GRID = 32
ITERS = 3


strength = 0.5
highest = lax.Precision.HIGHEST
low_edge = 1.0
high_edge = 1.0 + 12.0 * strength
centre = (high_edge + low_edge) / 2.0
spread = (high_edge - low_edge) / 2.0


def extended_2(cells, sides, width):
    for axis, dim in sides:
        count = lax.axis_size(axis)
        ends = count - 1
        head = lax.slice_in_dim(cells, 0, width, axis=dim)
        tail = lax.slice_in_dim(cells, cells.shape[dim] - width, cells.shape[dim], axis=dim)
        cells = jnp.concatenate(
            [
                lax.ppermute(tail, axis, [(i, (i + 1) % count) for i in range(ends)]),
                cells,
                lax.ppermute(head, axis, [((i + 1) % count, i) for i in range(ends)]),
            ],
            axis=dim,
        )
    return cells


def _exchange_kernel(axis, other, size, stride, whole, summed, x_ref, o_ref, *scratch):
    if summed:
        send_sem, recv_sem, own_sem, got = scratch
    else:
        (send_sem, recv_sem, own_sem), got = scratch, o_ref
    me = lax.axis_index(axis)
    fixed = lax.axis_index(other)
    pos = (me // stride) % size
    base = me - pos * stride

    def where(peer_pos):
        peer = base + peer_pos * stride
        return (peer, fixed) if axis == "cuts" else (fixed, peer)

    def part(peer_pos):
        return x_ref if whole else x_ref.at[peer_pos]

    barrier = pltpu.get_barrier_semaphore()
    for d in range(1, size):
        pl.semaphore_signal(
            barrier, inc=1, device_id=where((pos + d) % size), device_id_type=MESH
        )
    pl.semaphore_wait(barrier, size - 1)
    own = pltpu.make_async_copy(part(pos), got.at[pos], own_sem)
    own.start()
    copies = []
    for d in range(1, size):
        peer_pos = (pos + d) % size
        copy = pltpu.make_async_remote_copy(
            src_ref=part(peer_pos),
            dst_ref=got.at[pos],
            send_sem=send_sem.at[peer_pos],
            recv_sem=recv_sem.at[pos],
            device_id=where(peer_pos),
            device_id_type=MESH,
        )
        copy.start()
        copies.append(copy)
    for copy in copies:
        copy.wait_send()
    for d in range(1, size):
        source = (pos + size - d) % size
        pltpu.make_async_remote_copy(
            src_ref=part(source),
            dst_ref=got.at[source],
            send_sem=send_sem.at[source],
            recv_sem=recv_sem.at[source],
            device_id=where(source),
            device_id_type=MESH,
        ).wait_recv()
    own.wait()
    if summed:
        total = got[0]
        for slot in range(1, size):
            total = total + got[slot]
        o_ref[...] = total


def exchange(x, axis, key, whole=False, size=None, stride=1, summed=False, space=None):
    other = "col" if axis == "cuts" else "cuts"
    size = size or lax.axis_size(axis)
    shape = (size, *x.shape) if whole else x.shape
    scratch = [
        pltpu.SemaphoreType.DMA((size,)),
        pltpu.SemaphoreType.DMA((size,)),
        pltpu.SemaphoreType.DMA,
    ]
    if summed:
        scratch.append(pltpu.VMEM(shape, x.dtype))
        shape = shape[1:]
    return pl.pallas_call(
        functools.partial(_exchange_kernel, axis, other, size, stride, whole, summed),
        out_shape=jax.ShapeDtypeStruct(shape, x.dtype),
        in_specs=[pl.BlockSpec(memory_space=pltpu.VMEM)],
        out_specs=pl.BlockSpec(memory_space=space or pltpu.VMEM),
        scratch_shapes=scratch,
        compiler_params=pltpu.CompilerParams(collective_id=key, has_side_effects=True),
    )(x)


def _halo_kernel(n, head_ref, tail_ref, below_ref, above_ref, send_sem, recv_sem):
    me = lax.axis_index("col")
    fixed = lax.axis_index("cuts")
    has_left = (me + n - 1) // n
    has_right = 1 - me // (n - 1)
    left, right = (fixed, me - has_left), (fixed, me + has_right)

    def to_left():
        return pltpu.make_async_remote_copy(
            src_ref=head_ref, dst_ref=above_ref, send_sem=send_sem.at[0],
            recv_sem=recv_sem.at[1], device_id=left, device_id_type=MESH,
        )

    def to_right():
        return pltpu.make_async_remote_copy(
            src_ref=tail_ref, dst_ref=below_ref, send_sem=send_sem.at[1],
            recv_sem=recv_sem.at[0], device_id=right, device_id_type=MESH,
        )

    barrier = pltpu.get_barrier_semaphore()

    @pl.when(me > 0)
    def _():
        pl.semaphore_signal(barrier, inc=1, device_id=left, device_id_type=MESH)

    @pl.when(me < n - 1)
    def _():
        pl.semaphore_signal(barrier, inc=1, device_id=right, device_id_type=MESH)

    pl.semaphore_wait(barrier, has_left + has_right)

    @pl.when(me == 0)
    def _():
        below_ref[...] = jnp.zeros_like(below_ref)

    @pl.when(me == n - 1)
    def _():
        above_ref[...] = jnp.zeros_like(above_ref)

    @pl.when(me > 0)
    def _():
        to_left().start()

    @pl.when(me < n - 1)
    def _():
        to_right().start()

    @pl.when(me > 0)
    def _():
        to_left().wait_send()
        pltpu.make_async_remote_copy(
            src_ref=tail_ref, dst_ref=below_ref, send_sem=send_sem.at[1],
            recv_sem=recv_sem.at[0], device_id=left, device_id_type=MESH,
        ).wait_recv()

    @pl.when(me < n - 1)
    def _():
        to_right().wait_send()
        pltpu.make_async_remote_copy(
            src_ref=head_ref, dst_ref=above_ref, send_sem=send_sem.at[0],
            recv_sem=recv_sem.at[1], device_id=right, device_id_type=MESH,
        ).wait_recv()


def with_halo(cells, width):
    n = lax.axis_size("col")
    head = lax.slice_in_dim(cells, 0, width, axis=1)
    tail = lax.slice_in_dim(cells, cells.shape[1] - width, cells.shape[1], axis=1)
    below, above = pl.pallas_call(
        functools.partial(_halo_kernel, n),
        out_shape=(jax.ShapeDtypeStruct(head.shape, head.dtype),) * 2,
        in_specs=[pl.BlockSpec(memory_space=pltpu.VMEM)] * 2,
        out_specs=(pl.BlockSpec(memory_space=pltpu.VMEM),) * 2,
        scratch_shapes=[pltpu.SemaphoreType.DMA((2,)), pltpu.SemaphoreType.DMA((2,))],
        compiler_params=pltpu.CompilerParams(collective_id=3, has_side_effects=True),
    )(head, tail)
    return jnp.concatenate([below, cells, above], axis=1)


def _scatter_halo_kernel(size, stride, n, width, x_ref, o_ref, below_ref, above_ref,
                         got, head_buf, tail_buf, send_sem, recv_sem, own_sem, hsend, hrecv):
    me = lax.axis_index("cuts")
    cm = lax.axis_index("col")
    pos = (me // stride) % size
    base = me - pos * stride
    has_left = (cm + n - 1) // n
    has_right = 1 - cm // (n - 1)
    left, right = (me, cm - has_left), (me, cm + has_right)

    def where(peer_pos):
        return (base + peer_pos * stride, cm)

    barrier = pltpu.get_barrier_semaphore()
    for d in range(1, size):
        pl.semaphore_signal(
            barrier, inc=1, device_id=where((pos + d) % size), device_id_type=MESH
        )

    @pl.when(cm > 0)
    def _():
        pl.semaphore_signal(barrier, inc=1, device_id=left, device_id_type=MESH)

    @pl.when(cm < n - 1)
    def _():
        pl.semaphore_signal(barrier, inc=1, device_id=right, device_id_type=MESH)

    pl.semaphore_wait(barrier, size - 1 + has_left + has_right)

    @pl.when(cm == 0)
    def _():
        below_ref[...] = jnp.zeros_like(below_ref)

    @pl.when(cm == n - 1)
    def _():
        above_ref[...] = jnp.zeros_like(above_ref)

    own = pltpu.make_async_copy(x_ref.at[pos], got.at[pos], own_sem)
    own.start()
    copies = []
    for d in range(1, size):
        peer_pos = (pos + d) % size
        copy = pltpu.make_async_remote_copy(
            src_ref=x_ref.at[peer_pos], dst_ref=got.at[pos],
            send_sem=send_sem.at[peer_pos], recv_sem=recv_sem.at[pos],
            device_id=where(peer_pos), device_id_type=MESH,
        )
        copy.start()
        copies.append(copy)
    for copy in copies:
        copy.wait_send()
    for d in range(1, size):
        source = (pos + size - d) % size
        pltpu.make_async_remote_copy(
            src_ref=x_ref.at[source], dst_ref=got.at[source],
            send_sem=send_sem.at[source], recv_sem=recv_sem.at[source],
            device_id=where(source), device_id_type=MESH,
        ).wait_recv()
    own.wait()
    total = got[0]
    for slot in range(1, size):
        total = total + got[slot]
    o_ref[...] = total
    planes = total.shape[1]
    head_buf[...] = total[:, :width]
    tail_buf[...] = total[:, planes - width :]

    def to_left():
        return pltpu.make_async_remote_copy(
            src_ref=head_buf, dst_ref=above_ref, send_sem=hsend.at[0],
            recv_sem=hrecv.at[1], device_id=left, device_id_type=MESH,
        )

    def to_right():
        return pltpu.make_async_remote_copy(
            src_ref=tail_buf, dst_ref=below_ref, send_sem=hsend.at[1],
            recv_sem=hrecv.at[0], device_id=right, device_id_type=MESH,
        )

    @pl.when(cm > 0)
    def _():
        to_left().start()

    @pl.when(cm < n - 1)
    def _():
        to_right().start()

    @pl.when(cm > 0)
    def _():
        to_left().wait_send()
        pltpu.make_async_remote_copy(
            src_ref=tail_buf, dst_ref=below_ref, send_sem=hsend.at[1],
            recv_sem=hrecv.at[0], device_id=left, device_id_type=MESH,
        ).wait_recv()

    @pl.when(cm < n - 1)
    def _():
        to_right().wait_send()
        pltpu.make_async_remote_copy(
            src_ref=head_buf, dst_ref=above_ref, send_sem=hsend.at[0],
            recv_sem=hrecv.at[1], device_id=right, device_id_type=MESH,
        ).wait_recv()


def scatter_with_halo(x, size, stride, width):
    n = lax.axis_size("col")
    block = x.shape[1:]
    halo = (block[0], width, *block[2:])
    vmem = pl.BlockSpec(memory_space=pltpu.VMEM)
    portion, below, above = pl.pallas_call(
        functools.partial(_scatter_halo_kernel, size, stride, n, width),
        out_shape=(
            jax.ShapeDtypeStruct(block, x.dtype),
            jax.ShapeDtypeStruct(halo, x.dtype),
            jax.ShapeDtypeStruct(halo, x.dtype),
        ),
        in_specs=[vmem],
        out_specs=(vmem, vmem, vmem),
        scratch_shapes=[
            pltpu.VMEM(x.shape, x.dtype),
            pltpu.VMEM(halo, x.dtype),
            pltpu.VMEM(halo, x.dtype),
            pltpu.SemaphoreType.DMA((size,)),
            pltpu.SemaphoreType.DMA((size,)),
            pltpu.SemaphoreType.DMA,
            pltpu.SemaphoreType.DMA((2,)),
            pltpu.SemaphoreType.DMA((2,)),
        ],
        compiler_params=pltpu.CompilerParams(collective_id=4, has_side_effects=True),
    )(x)
    return portion, jnp.concatenate([below, portion, above], axis=1)


def split_up(shard, dim, devices):
    before, after = (shard.shape[:dim], shard.shape[dim + 1 :])
    return jnp.moveaxis(shard.reshape(*before, devices, -1, *after), dim, 0)


def sent_and_summed(shard, axis, dim):
    tiles = split_up(shard, dim, lax.axis_size(axis))
    arrived = exchange(tiles, axis, 0)
    return arrived.sum(axis=0)


def joined_along(tiles, dim):
    dims = list(tiles.shape[1:])
    dims[dim] *= tiles.shape[0]
    return jnp.moveaxis(tiles, 0, dim).reshape(dims)


def from_everyone(shard, axis):
    return exchange(shard, axis, 1 if axis == "cuts" else 2, whole=True)


def gather_directly(shard, axis, dim):
    return joined_along(from_everyone(shard, axis), dim)


def taken_together(shard, axis):
    return from_everyone(shard, axis).sum(axis=0)


def packed_total(arrays, axis):
    line, at, done = (jnp.concatenate([a.reshape(-1) for a in arrays]), 0, [])
    running = taken_together(line, axis)
    for a in arrays:
        done.append(running[at : at + a.size].reshape(a.shape))
        at += a.size
    return tuple(done)


def operate(extended):
    channels, depth, cells = extended.shape
    edge = GRID
    interior = extended[:, 1:-1]
    column = jnp.arange(cells, dtype=jnp.int32) % edge
    has_left = (column > 0).astype(jnp.float32)
    has_right = (column < edge - 1).astype(jnp.float32)
    left_part = jnp.pad(interior, ((0, 0), (0, 0), (1, 0)))[:, :, :-1] * has_left
    right_part = jnp.pad(interior, ((0, 0), (0, 0), (0, 1)))[:, :, 1:] * has_right
    upper_part = jnp.pad(interior, ((0, 0), (0, 0), (edge, 0)))[:, :, :-edge]
    lower_part = jnp.pad(interior, ((0, 0), (0, 0), (0, edge)))[:, :, edge:]
    neighbours = extended[:, 2:] + extended[:, :-2]
    neighbours = neighbours + left_part + right_part + upper_part + lower_part
    return interior + strength * (6.0 * interior - neighbours)


def smooth_once(source, extended):
    planes = source.shape[1]
    first_plane = lax.axis_index("col") * planes - ITERS
    total_planes = planes * lax.axis_size("col")
    levels = first_plane + jnp.arange(planes + 2 * ITERS, dtype=jnp.int32)
    inside = ((levels >= 0) & (levels < total_planes)).astype(jnp.float32)[None, :, None]
    solution = jnp.zeros_like(source)
    residual = extended
    direction = extended / centre
    ratio = spread / centre
    for iteration in range(ITERS):
        margin = ITERS - iteration
        solution = solution + direction[:, margin : margin + planes]
        window = inside[:, iteration + 1 : iteration + 1 + planes + 2 * (margin - 1)]
        residual = (residual[:, 1:-1] - operate(direction)) * window
        ratio_next = 1.0 / (2.0 * centre / spread - ratio)
        direction = ratio_next * ratio * direction[:, 1:-1] + 2.0 * ratio_next / spread * residual
        ratio = ratio_next
    return solution + direction


def _eliminate(m_ref, b_ref, o_ref):
    m = m_ref[...]
    b = b_ref[...]
    n = m.shape[0]
    ri = lax.broadcasted_iota(jnp.int32, m.shape, 0)
    ci = lax.broadcasted_iota(jnp.int32, m.shape, 1)
    rb = lax.broadcasted_iota(jnp.int32, b.shape, 0)

    def pick_row(x, rows, p):
        return jnp.sum(jnp.where(rows == p, x, 0.0), axis=0, keepdims=True)

    def pick_col(x, p):
        return jnp.sum(jnp.where(ci[: x.shape[0]] == p, x, 0.0), axis=1, keepdims=True)

    def step(j, carry):
        m, b = carry
        p, q = 2 * j, 2 * j + 1
        c0, c1 = pick_col(m, p), pick_col(m, q)
        r0, r1 = pick_row(m, ri, p), pick_row(m, ri, q)
        s0, s1 = pick_row(b, rb, p), pick_row(b, rb, q)
        a, e = pick_col(r0, p), pick_col(r0, q)
        c, d = pick_col(r1, p), pick_col(r1, q)
        scale = 1.0 / (a * d - e * c)
        n0, n1 = (d * r0 - e * r1) * scale, (a * r1 - c * r0) * scale
        t0, t1 = (d * s0 - e * s1) * scale, (a * s1 - c * s0) * scale
        m = jnp.where(ri == p, n0, jnp.where(ri == q, n1, m - c0 * n0 - c1 * n1))
        b = jnp.where(rb == p, t0, jnp.where(rb == q, t1, b - c0 * t0 - c1 * t1))
        return m, b

    x = lax.fori_loop(0, n // 2, step, (m, b), unroll=True)[1]
    if o_ref.shape == b.shape:
        o_ref[...] = x.astype(o_ref.dtype)
    else:
        o_ref[...] = jnp.sum(jnp.where(ri == ci, x, 0.0), axis=0, keepdims=True)


def spd_solve(m, b, dtype=None):
    shape = (1, b.shape[0]) if b.shape[1] == 1 else b.shape
    return pl.pallas_call(
        _eliminate, out_shape=jax.ShapeDtypeStruct(shape, dtype or b.dtype)
    )(m, b)


def per_device(data, weights, mixing):
    local_scans, ranks, planes, cells = data.shape
    mix_gram = jnp.dot(mixing.T, mixing, precision=highest)
    weight_gram = jnp.dot(weights.T, weights, precision=highest)
    own_weights = lax.dynamic_slice_in_dim(
        weights, lax.axis_index("cuts") * local_scans, local_scans, 0
    )
    scaled = (mixing.T[None, :, :] * own_weights[:, :, None]).transpose(1, 0, 2)
    coefficients = spd_solve(
        mix_gram * weight_gram, scaled.reshape(ranks, local_scans * ranks), jnp.bfloat16
    )
    partial = lax.dot_general(
        coefficients, data.reshape(-1, planes, cells), (((1,), (0,)), ((), ())), preferred_element_type=jnp.float32
    )
    cores = 2
    chips = lax.axis_size("cuts") // cores
    paired = exchange(
        partial.reshape(cores, chips, -1, planes, cells), "cuts", 0, size=cores, summed=True
    )
    portion, extended = scatter_with_halo(paired, chips, cores, ITERS)
    smoothed = smooth_once(portion, extended)
    half_factor = exchange(smoothed, "cuts", 1, whole=True, size=chips, stride=cores)
    factor = exchange(half_factor, "cuts", 5, whole=True, size=cores, space=pl.ANY)
    factor = factor.reshape(ranks, planes, cells)
    factor_half = factor.astype(jnp.bfloat16)
    factor_gram = lax.dot_general(
        factor, factor, (((1, 2), (1, 2)), ((), ())), precision=lax.Precision.HIGH
    )
    products = lax.dot_general(
        data, factor_half, (((2, 3), (1, 2)), ((), ())), preferred_element_type=jnp.float32
    )
    targets = jnp.sum(mixing[None, :, :] * products, axis=1)
    half = ranks // 2
    row = lax.broadcasted_iota(jnp.int32, (half, half), 0)
    col = lax.broadcasted_iota(jnp.int32, (half, half), 1)
    top, off, low = (factor_gram[:half, :half], factor_gram[:half, half:], factor_gram[half:, half:])
    folded = jnp.where(row >= col, top, low)
    folded, off, low_diag, targets = packed_total(
        (folded, off, jnp.sum(jnp.where(row == col, low, 0.0), axis=1), targets), "col"
    )
    top = jnp.where(row >= col, folded, folded.T)
    low = jnp.where(row < col, folded, jnp.where(row > col, folded.T, low_diag[:, None]))
    factor_gram = jnp.concatenate(
        [jnp.concatenate([top, off], axis=1), jnp.concatenate([off.T, low], axis=1)], axis=0
    )
    updated = spd_solve(mix_gram * factor_gram, targets.T)
    return (factor, updated)


def solution(mesh):
    return jax.shard_map(
        per_device,
        mesh=mesh,
        in_specs=(P("cuts", None, "col", None), P(), P()),
        out_specs=(P(None, "col", None), P("cuts", None)),
        check_vma=False,
    )
```

```python
import functools
import jax
import jax.numpy as jnp
from jax import lax
from jax.sharding import PartitionSpec as P
from jax.experimental import pallas as pl
from jax.experimental.pallas import tpu as pltpu

MESH = pl.DeviceIdType.MESH

GRID = 32
ITERS = 3


strength = 0.5
highest = lax.Precision.HIGHEST
low_edge = 1.0
high_edge = 1.0 + 12.0 * strength
centre = (high_edge + low_edge) / 2.0
spread = (high_edge - low_edge) / 2.0


def extended_2(cells, sides, width):
    for axis, dim in sides:
        count = lax.axis_size(axis)
        ends = count - 1
        head = lax.slice_in_dim(cells, 0, width, axis=dim)
        tail = lax.slice_in_dim(cells, cells.shape[dim] - width, cells.shape[dim], axis=dim)
        cells = jnp.concatenate(
            [
                lax.ppermute(tail, axis, [(i, (i + 1) % count) for i in range(ends)]),
                cells,
                lax.ppermute(head, axis, [((i + 1) % count, i) for i in range(ends)]),
            ],
            axis=dim,
        )
    return cells


def _exchange_kernel(axis, other, size, stride, whole, summed, x_ref, o_ref, *scratch):
    if summed:
        send_sem, recv_sem, own_sem, got = scratch
    else:
        (send_sem, recv_sem, own_sem), got = scratch, o_ref
    me = lax.axis_index(axis)
    fixed = lax.axis_index(other)
    pos = (me // stride) % size
    base = me - pos * stride

    def where(peer_pos):
        peer = base + peer_pos * stride
        return (peer, fixed) if axis == "cuts" else (fixed, peer)

    def part(peer_pos):
        return x_ref if whole else x_ref.at[peer_pos]

    barrier = pltpu.get_barrier_semaphore()
    for d in range(1, size):
        pl.semaphore_signal(
            barrier, inc=1, device_id=where((pos + d) % size), device_id_type=MESH
        )
    pl.semaphore_wait(barrier, size - 1)
    own = pltpu.make_async_copy(part(pos), got.at[pos], own_sem)
    own.start()
    copies = []
    for d in range(1, size):
        peer_pos = (pos + d) % size
        copy = pltpu.make_async_remote_copy(
            src_ref=part(peer_pos),
            dst_ref=got.at[pos],
            send_sem=send_sem.at[peer_pos],
            recv_sem=recv_sem.at[pos],
            device_id=where(peer_pos),
            device_id_type=MESH,
        )
        copy.start()
        copies.append(copy)
    for copy in copies:
        copy.wait_send()
    for d in range(1, size):
        source = (pos + size - d) % size
        pltpu.make_async_remote_copy(
            src_ref=part(source),
            dst_ref=got.at[source],
            send_sem=send_sem.at[source],
            recv_sem=recv_sem.at[source],
            device_id=where(source),
            device_id_type=MESH,
        ).wait_recv()
    own.wait()
    if summed:
        total = got[0]
        for slot in range(1, size):
            total = total + got[slot]
        o_ref[...] = total


def exchange(x, axis, key, whole=False, size=None, stride=1, summed=False, space=None):
    other = "col" if axis == "cuts" else "cuts"
    size = size or lax.axis_size(axis)
    shape = (size, *x.shape) if whole else x.shape
    scratch = [
        pltpu.SemaphoreType.DMA((size,)),
        pltpu.SemaphoreType.DMA((size,)),
        pltpu.SemaphoreType.DMA,
    ]
    if summed:
        scratch.append(pltpu.VMEM(shape, x.dtype))
        shape = shape[1:]
    return pl.pallas_call(
        functools.partial(_exchange_kernel, axis, other, size, stride, whole, summed),
        out_shape=jax.ShapeDtypeStruct(shape, x.dtype),
        in_specs=[pl.BlockSpec(memory_space=pltpu.VMEM)],
        out_specs=pl.BlockSpec(memory_space=space or pltpu.VMEM),
        scratch_shapes=scratch,
        compiler_params=pltpu.CompilerParams(collective_id=key, has_side_effects=True),
    )(x)


def _halo_kernel(n, head_ref, tail_ref, below_ref, above_ref, send_sem, recv_sem):
    me = lax.axis_index("col")
    fixed = lax.axis_index("cuts")
    has_left = (me + n - 1) // n
    has_right = 1 - me // (n - 1)
    left, right = (fixed, me - has_left), (fixed, me + has_right)

    def to_left():
        return pltpu.make_async_remote_copy(
            src_ref=head_ref, dst_ref=above_ref, send_sem=send_sem.at[0],
            recv_sem=recv_sem.at[1], device_id=left, device_id_type=MESH,
        )

    def to_right():
        return pltpu.make_async_remote_copy(
            src_ref=tail_ref, dst_ref=below_ref, send_sem=send_sem.at[1],
            recv_sem=recv_sem.at[0], device_id=right, device_id_type=MESH,
        )

    barrier = pltpu.get_barrier_semaphore()

    @pl.when(me > 0)
    def _():
        pl.semaphore_signal(barrier, inc=1, device_id=left, device_id_type=MESH)

    @pl.when(me < n - 1)
    def _():
        pl.semaphore_signal(barrier, inc=1, device_id=right, device_id_type=MESH)

    pl.semaphore_wait(barrier, has_left + has_right)

    @pl.when(me == 0)
    def _():
        below_ref[...] = jnp.zeros_like(below_ref)

    @pl.when(me == n - 1)
    def _():
        above_ref[...] = jnp.zeros_like(above_ref)

    @pl.when(me > 0)
    def _():
        to_left().start()

    @pl.when(me < n - 1)
    def _():
        to_right().start()

    @pl.when(me > 0)
    def _():
        to_left().wait_send()
        pltpu.make_async_remote_copy(
            src_ref=tail_ref, dst_ref=below_ref, send_sem=send_sem.at[1],
            recv_sem=recv_sem.at[0], device_id=left, device_id_type=MESH,
        ).wait_recv()

    @pl.when(me < n - 1)
    def _():
        to_right().wait_send()
        pltpu.make_async_remote_copy(
            src_ref=head_ref, dst_ref=above_ref, send_sem=send_sem.at[0],
            recv_sem=recv_sem.at[1], device_id=right, device_id_type=MESH,
        ).wait_recv()


def with_halo(cells, width):
    n = lax.axis_size("col")
    head = lax.slice_in_dim(cells, 0, width, axis=1)
    tail = lax.slice_in_dim(cells, cells.shape[1] - width, cells.shape[1], axis=1)
    below, above = pl.pallas_call(
        functools.partial(_halo_kernel, n),
        out_shape=(jax.ShapeDtypeStruct(head.shape, head.dtype),) * 2,
        in_specs=[pl.BlockSpec(memory_space=pltpu.VMEM)] * 2,
        out_specs=(pl.BlockSpec(memory_space=pltpu.VMEM),) * 2,
        scratch_shapes=[pltpu.SemaphoreType.DMA((2,)), pltpu.SemaphoreType.DMA((2,))],
        compiler_params=pltpu.CompilerParams(collective_id=3, has_side_effects=True),
    )(head, tail)
    return jnp.concatenate([below, cells, above], axis=1)


def _scatter_halo_kernel(size, stride, n, width, x_ref, o_ref, below_ref, above_ref,
                         got, head_buf, tail_buf, send_sem, recv_sem, own_sem, hsend, hrecv,
                         pair_got, pair_buf, pair_sem):
    me = lax.axis_index("cuts")
    cm = lax.axis_index("col")
    pos = (me // stride) % size
    base = me - pos * stride
    core = me % stride
    partner = me + 1 - 2 * core
    has_left = (cm + n - 1) // n
    has_right = 1 - cm // (n - 1)
    left, right = (me, cm - has_left), (me, cm + has_right)

    def where(peer_pos):
        return (base + peer_pos * stride, cm)

    barrier = pltpu.get_barrier_semaphore()
    for d in range(1, size):
        pl.semaphore_signal(
            barrier, inc=1, device_id=where((pos + d) % size), device_id_type=MESH
        )

    @pl.when(cm > 0)
    def _():
        pl.semaphore_signal(barrier, inc=1, device_id=left, device_id_type=MESH)

    @pl.when(cm < n - 1)
    def _():
        pl.semaphore_signal(barrier, inc=1, device_id=right, device_id_type=MESH)

    pl.semaphore_signal(barrier, inc=1, device_id=(partner, cm), device_id_type=MESH)
    pl.semaphore_wait(barrier, size + has_left + has_right)

    pair = pltpu.make_async_remote_copy(
        src_ref=x_ref.at[1 - core], dst_ref=pair_got, send_sem=pair_sem.at[0],
        recv_sem=pair_sem.at[1], device_id=(partner, cm), device_id_type=MESH,
    )
    pair.start()
    pair.wait_send()
    pair.wait_recv()
    pair_buf[...] = x_ref[core] + pair_got[...]

    @pl.when(cm == 0)
    def _():
        below_ref[...] = jnp.zeros_like(below_ref)

    @pl.when(cm == n - 1)
    def _():
        above_ref[...] = jnp.zeros_like(above_ref)

    own = pltpu.make_async_copy(pair_buf.at[pos], got.at[pos], own_sem)
    own.start()
    copies = []
    for d in range(1, size):
        peer_pos = (pos + d) % size
        copy = pltpu.make_async_remote_copy(
            src_ref=pair_buf.at[peer_pos], dst_ref=got.at[pos],
            send_sem=send_sem.at[peer_pos], recv_sem=recv_sem.at[pos],
            device_id=where(peer_pos), device_id_type=MESH,
        )
        copy.start()
        copies.append(copy)
    for copy in copies:
        copy.wait_send()
    for d in range(1, size):
        source = (pos + size - d) % size
        pltpu.make_async_remote_copy(
            src_ref=pair_buf.at[source], dst_ref=got.at[source],
            send_sem=send_sem.at[source], recv_sem=recv_sem.at[source],
            device_id=where(source), device_id_type=MESH,
        ).wait_recv()
    own.wait()
    total = got[0]
    for slot in range(1, size):
        total = total + got[slot]
    o_ref[...] = total
    planes = total.shape[1]
    head_buf[...] = total[:, :width]
    tail_buf[...] = total[:, planes - width :]

    def to_left():
        return pltpu.make_async_remote_copy(
            src_ref=head_buf, dst_ref=above_ref, send_sem=hsend.at[0],
            recv_sem=hrecv.at[1], device_id=left, device_id_type=MESH,
        )

    def to_right():
        return pltpu.make_async_remote_copy(
            src_ref=tail_buf, dst_ref=below_ref, send_sem=hsend.at[1],
            recv_sem=hrecv.at[0], device_id=right, device_id_type=MESH,
        )

    @pl.when(cm > 0)
    def _():
        to_left().start()

    @pl.when(cm < n - 1)
    def _():
        to_right().start()

    @pl.when(cm > 0)
    def _():
        to_left().wait_send()
        pltpu.make_async_remote_copy(
            src_ref=tail_buf, dst_ref=below_ref, send_sem=hsend.at[1],
            recv_sem=hrecv.at[0], device_id=left, device_id_type=MESH,
        ).wait_recv()

    @pl.when(cm < n - 1)
    def _():
        to_right().wait_send()
        pltpu.make_async_remote_copy(
            src_ref=head_buf, dst_ref=above_ref, send_sem=hsend.at[0],
            recv_sem=hrecv.at[1], device_id=right, device_id_type=MESH,
        ).wait_recv()


def scatter_with_halo(x, size, stride, width):
    n = lax.axis_size("col")
    block = x.shape[2:]
    halo = (block[0], width, *block[2:])
    vmem = pl.BlockSpec(memory_space=pltpu.VMEM)
    portion, below, above = pl.pallas_call(
        functools.partial(_scatter_halo_kernel, size, stride, n, width),
        out_shape=(
            jax.ShapeDtypeStruct(block, x.dtype),
            jax.ShapeDtypeStruct(halo, x.dtype),
            jax.ShapeDtypeStruct(halo, x.dtype),
        ),
        in_specs=[vmem],
        out_specs=(vmem, vmem, vmem),
        scratch_shapes=[
            pltpu.VMEM(x.shape[1:], x.dtype),
            pltpu.VMEM(halo, x.dtype),
            pltpu.VMEM(halo, x.dtype),
            pltpu.SemaphoreType.DMA((size,)),
            pltpu.SemaphoreType.DMA((size,)),
            pltpu.SemaphoreType.DMA,
            pltpu.SemaphoreType.DMA((2,)),
            pltpu.SemaphoreType.DMA((2,)),
            pltpu.VMEM(x.shape[1:], x.dtype),
            pltpu.VMEM(x.shape[1:], x.dtype),
            pltpu.SemaphoreType.DMA((2,)),
        ],
        compiler_params=pltpu.CompilerParams(collective_id=4, has_side_effects=True),
    )(x)
    return portion, jnp.concatenate([below, portion, above], axis=1)


def split_up(shard, dim, devices):
    before, after = (shard.shape[:dim], shard.shape[dim + 1 :])
    return jnp.moveaxis(shard.reshape(*before, devices, -1, *after), dim, 0)


def sent_and_summed(shard, axis, dim):
    tiles = split_up(shard, dim, lax.axis_size(axis))
    arrived = exchange(tiles, axis, 0)
    return arrived.sum(axis=0)


def joined_along(tiles, dim):
    dims = list(tiles.shape[1:])
    dims[dim] *= tiles.shape[0]
    return jnp.moveaxis(tiles, 0, dim).reshape(dims)


def from_everyone(shard, axis):
    return exchange(shard, axis, 1 if axis == "cuts" else 2, whole=True)


def gather_directly(shard, axis, dim):
    return joined_along(from_everyone(shard, axis), dim)


def taken_together(shard, axis):
    return from_everyone(shard, axis).sum(axis=0)


def packed_total(arrays, axis):
    line, at, done = (jnp.concatenate([a.reshape(-1) for a in arrays]), 0, [])
    running = taken_together(line, axis)
    for a in arrays:
        done.append(running[at : at + a.size].reshape(a.shape))
        at += a.size
    return tuple(done)


def operate(extended):
    channels, depth, cells = extended.shape
    edge = GRID
    interior = extended[:, 1:-1]
    column = jnp.arange(cells, dtype=jnp.int32) % edge
    has_left = (column > 0).astype(jnp.float32)
    has_right = (column < edge - 1).astype(jnp.float32)
    left_part = jnp.pad(interior, ((0, 0), (0, 0), (1, 0)))[:, :, :-1] * has_left
    right_part = jnp.pad(interior, ((0, 0), (0, 0), (0, 1)))[:, :, 1:] * has_right
    upper_part = jnp.pad(interior, ((0, 0), (0, 0), (edge, 0)))[:, :, :-edge]
    lower_part = jnp.pad(interior, ((0, 0), (0, 0), (0, edge)))[:, :, edge:]
    neighbours = extended[:, 2:] + extended[:, :-2]
    neighbours = neighbours + left_part + right_part + upper_part + lower_part
    return interior + strength * (6.0 * interior - neighbours)


def smooth_once(source, extended):
    planes = source.shape[1]
    first_plane = lax.axis_index("col") * planes - ITERS
    total_planes = planes * lax.axis_size("col")
    levels = first_plane + jnp.arange(planes + 2 * ITERS, dtype=jnp.int32)
    inside = ((levels >= 0) & (levels < total_planes)).astype(jnp.float32)[None, :, None]
    solution = jnp.zeros_like(source)
    residual = extended
    direction = extended / centre
    ratio = spread / centre
    for iteration in range(ITERS):
        margin = ITERS - iteration
        solution = solution + direction[:, margin : margin + planes]
        window = inside[:, iteration + 1 : iteration + 1 + planes + 2 * (margin - 1)]
        residual = (residual[:, 1:-1] - operate(direction)) * window
        ratio_next = 1.0 / (2.0 * centre / spread - ratio)
        direction = ratio_next * ratio * direction[:, 1:-1] + 2.0 * ratio_next / spread * residual
        ratio = ratio_next
    return solution + direction


def _eliminate(m_ref, b_ref, o_ref):
    m = m_ref[...]
    b = b_ref[...]
    n = m.shape[0]
    ri = lax.broadcasted_iota(jnp.int32, m.shape, 0)
    ci = lax.broadcasted_iota(jnp.int32, m.shape, 1)
    rb = lax.broadcasted_iota(jnp.int32, b.shape, 0)

    def pick_row(x, rows, p):
        return jnp.sum(jnp.where(rows == p, x, 0.0), axis=0, keepdims=True)

    def pick_col(x, p):
        return jnp.sum(jnp.where(ci[: x.shape[0]] == p, x, 0.0), axis=1, keepdims=True)

    def step(j, carry):
        m, b = carry
        p, q = 2 * j, 2 * j + 1
        c0, c1 = pick_col(m, p), pick_col(m, q)
        r0, r1 = pick_row(m, ri, p), pick_row(m, ri, q)
        s0, s1 = pick_row(b, rb, p), pick_row(b, rb, q)
        a, e = pick_col(r0, p), pick_col(r0, q)
        c, d = pick_col(r1, p), pick_col(r1, q)
        scale = 1.0 / (a * d - e * c)
        n0, n1 = (d * r0 - e * r1) * scale, (a * r1 - c * r0) * scale
        t0, t1 = (d * s0 - e * s1) * scale, (a * s1 - c * s0) * scale
        m = jnp.where(ri == p, n0, jnp.where(ri == q, n1, m - c0 * n0 - c1 * n1))
        b = jnp.where(rb == p, t0, jnp.where(rb == q, t1, b - c0 * t0 - c1 * t1))
        return m, b

    x = lax.fori_loop(0, n // 2, step, (m, b), unroll=True)[1]
    if o_ref.shape == b.shape:
        o_ref[...] = x.astype(o_ref.dtype)
    else:
        o_ref[...] = jnp.sum(jnp.where(ri == ci, x, 0.0), axis=0, keepdims=True)


def spd_solve(m, b, dtype=None):
    shape = (1, b.shape[0]) if b.shape[1] == 1 else b.shape
    return pl.pallas_call(
        _eliminate, out_shape=jax.ShapeDtypeStruct(shape, dtype or b.dtype)
    )(m, b)


def per_device(data, weights, mixing):
    local_scans, ranks, planes, cells = data.shape
    mix_gram = jnp.dot(mixing.T, mixing, precision=highest)
    weight_gram = jnp.dot(weights.T, weights, precision=highest)
    own_weights = lax.dynamic_slice_in_dim(
        weights, lax.axis_index("cuts") * local_scans, local_scans, 0
    )
    scaled = (mixing.T[None, :, :] * own_weights[:, :, None]).transpose(1, 0, 2)
    coefficients = spd_solve(
        mix_gram * weight_gram, scaled.reshape(ranks, local_scans * ranks), jnp.bfloat16
    )
    partial = lax.dot_general(
        coefficients, data.reshape(-1, planes, cells), (((1,), (0,)), ((), ())), preferred_element_type=jnp.float32
    )
    cores = 2
    chips = lax.axis_size("cuts") // cores
    portion, extended = scatter_with_halo(
        partial.reshape(cores, chips, -1, planes, cells), chips, cores, ITERS
    )
    smoothed = smooth_once(portion, extended)
    half_factor = exchange(smoothed, "cuts", 1, whole=True, size=chips, stride=cores)
    factor = exchange(half_factor, "cuts", 5, whole=True, size=cores, space=pl.ANY)
    factor = factor.reshape(ranks, planes, cells)
    factor_half = factor.astype(jnp.bfloat16)
    factor_gram = lax.dot_general(
        factor, factor, (((1, 2), (1, 2)), ((), ())), precision=lax.Precision.HIGH
    )
    products = lax.dot_general(
        data, factor_half, (((2, 3), (1, 2)), ((), ())), preferred_element_type=jnp.float32
    )
    targets = jnp.sum(mixing[None, :, :] * products, axis=1)
    half = ranks // 2
    row = lax.broadcasted_iota(jnp.int32, (half, half), 0)
    col = lax.broadcasted_iota(jnp.int32, (half, half), 1)
    top, off, low = (factor_gram[:half, :half], factor_gram[:half, half:], factor_gram[half:, half:])
    folded = jnp.where(row >= col, top, low)
    folded, off, low_diag, targets = packed_total(
        (folded, off, jnp.sum(jnp.where(row == col, low, 0.0), axis=1), targets), "col"
    )
    top = jnp.where(row >= col, folded, folded.T)
    low = jnp.where(row < col, folded, jnp.where(row > col, folded.T, low_diag[:, None]))
    factor_gram = jnp.concatenate(
        [jnp.concatenate([top, off], axis=1), jnp.concatenate([off.T, low], axis=1)], axis=0
    )
    updated = spd_solve(mix_gram * factor_gram, targets.T)
    return (factor, updated)


def solution(mesh):
    return jax.shard_map(
        per_device,
        mesh=mesh,
        in_specs=(P("cuts", None, "col", None), P(), P()),
        out_specs=(P(None, "col", None), P("cuts", None)),
        check_vma=False,
    )
```

```python
import functools
import jax
import jax.numpy as jnp
from jax import lax
from jax.sharding import PartitionSpec as P
from jax.experimental import pallas as pl
from jax.experimental.pallas import tpu as pltpu

MESH = pl.DeviceIdType.MESH

GRID = 32
ITERS = 3


strength = 0.5
highest = lax.Precision.HIGHEST
low_edge = 1.0
high_edge = 1.0 + 12.0 * strength
centre = (high_edge + low_edge) / 2.0
spread = (high_edge - low_edge) / 2.0


def extended_2(cells, sides, width):
    for axis, dim in sides:
        count = lax.axis_size(axis)
        ends = count - 1
        head = lax.slice_in_dim(cells, 0, width, axis=dim)
        tail = lax.slice_in_dim(cells, cells.shape[dim] - width, cells.shape[dim], axis=dim)
        cells = jnp.concatenate(
            [
                lax.ppermute(tail, axis, [(i, (i + 1) % count) for i in range(ends)]),
                cells,
                lax.ppermute(head, axis, [((i + 1) % count, i) for i in range(ends)]),
            ],
            axis=dim,
        )
    return cells


def _exchange_kernel(axis, other, size, stride, whole, summed, x_ref, o_ref, *scratch):
    if summed:
        send_sem, recv_sem, own_sem, got = scratch
    else:
        (send_sem, recv_sem, own_sem), got = scratch, o_ref
    me = lax.axis_index(axis)
    fixed = lax.axis_index(other)
    pos = (me // stride) % size
    base = me - pos * stride

    def where(peer_pos):
        peer = base + peer_pos * stride
        return (peer, fixed) if axis == "cuts" else (fixed, peer)

    def part(peer_pos):
        return x_ref if whole else x_ref.at[peer_pos]

    barrier = pltpu.get_barrier_semaphore()
    for d in range(1, size):
        pl.semaphore_signal(
            barrier, inc=1, device_id=where((pos + d) % size), device_id_type=MESH
        )
    pl.semaphore_wait(barrier, size - 1)
    own = pltpu.make_async_copy(part(pos), got.at[pos], own_sem)
    own.start()
    copies = []
    for d in range(1, size):
        peer_pos = (pos + d) % size
        copy = pltpu.make_async_remote_copy(
            src_ref=part(peer_pos),
            dst_ref=got.at[pos],
            send_sem=send_sem.at[peer_pos],
            recv_sem=recv_sem.at[pos],
            device_id=where(peer_pos),
            device_id_type=MESH,
        )
        copy.start()
        copies.append(copy)
    for copy in copies:
        copy.wait_send()
    for d in range(1, size):
        source = (pos + size - d) % size
        pltpu.make_async_remote_copy(
            src_ref=part(source),
            dst_ref=got.at[source],
            send_sem=send_sem.at[source],
            recv_sem=recv_sem.at[source],
            device_id=where(source),
            device_id_type=MESH,
        ).wait_recv()
    own.wait()
    if summed:
        total = got[0]
        for slot in range(1, size):
            total = total + got[slot]
        o_ref[...] = total


def exchange(x, axis, key, whole=False, size=None, stride=1, summed=False, space=None):
    other = "col" if axis == "cuts" else "cuts"
    size = size or lax.axis_size(axis)
    shape = (size, *x.shape) if whole else x.shape
    scratch = [
        pltpu.SemaphoreType.DMA((size,)),
        pltpu.SemaphoreType.DMA((size,)),
        pltpu.SemaphoreType.DMA,
    ]
    if summed:
        scratch.append(pltpu.VMEM(shape, x.dtype))
        shape = shape[1:]
    return pl.pallas_call(
        functools.partial(_exchange_kernel, axis, other, size, stride, whole, summed),
        out_shape=jax.ShapeDtypeStruct(shape, x.dtype),
        in_specs=[pl.BlockSpec(memory_space=pltpu.VMEM)],
        out_specs=pl.BlockSpec(memory_space=space or pltpu.VMEM),
        scratch_shapes=scratch,
        compiler_params=pltpu.CompilerParams(collective_id=key, has_side_effects=True),
    )(x)


def _halo_kernel(n, head_ref, tail_ref, below_ref, above_ref, send_sem, recv_sem):
    me = lax.axis_index("col")
    fixed = lax.axis_index("cuts")
    has_left = (me + n - 1) // n
    has_right = 1 - me // (n - 1)
    left, right = (fixed, me - has_left), (fixed, me + has_right)

    def to_left():
        return pltpu.make_async_remote_copy(
            src_ref=head_ref, dst_ref=above_ref, send_sem=send_sem.at[0],
            recv_sem=recv_sem.at[1], device_id=left, device_id_type=MESH,
        )

    def to_right():
        return pltpu.make_async_remote_copy(
            src_ref=tail_ref, dst_ref=below_ref, send_sem=send_sem.at[1],
            recv_sem=recv_sem.at[0], device_id=right, device_id_type=MESH,
        )

    barrier = pltpu.get_barrier_semaphore()

    @pl.when(me > 0)
    def _():
        pl.semaphore_signal(barrier, inc=1, device_id=left, device_id_type=MESH)

    @pl.when(me < n - 1)
    def _():
        pl.semaphore_signal(barrier, inc=1, device_id=right, device_id_type=MESH)

    pl.semaphore_wait(barrier, has_left + has_right)

    @pl.when(me == 0)
    def _():
        below_ref[...] = jnp.zeros_like(below_ref)

    @pl.when(me == n - 1)
    def _():
        above_ref[...] = jnp.zeros_like(above_ref)

    @pl.when(me > 0)
    def _():
        to_left().start()

    @pl.when(me < n - 1)
    def _():
        to_right().start()

    @pl.when(me > 0)
    def _():
        to_left().wait_send()
        pltpu.make_async_remote_copy(
            src_ref=tail_ref, dst_ref=below_ref, send_sem=send_sem.at[1],
            recv_sem=recv_sem.at[0], device_id=left, device_id_type=MESH,
        ).wait_recv()

    @pl.when(me < n - 1)
    def _():
        to_right().wait_send()
        pltpu.make_async_remote_copy(
            src_ref=head_ref, dst_ref=above_ref, send_sem=send_sem.at[0],
            recv_sem=recv_sem.at[1], device_id=right, device_id_type=MESH,
        ).wait_recv()


def with_halo(cells, width):
    n = lax.axis_size("col")
    head = lax.slice_in_dim(cells, 0, width, axis=1)
    tail = lax.slice_in_dim(cells, cells.shape[1] - width, cells.shape[1], axis=1)
    below, above = pl.pallas_call(
        functools.partial(_halo_kernel, n),
        out_shape=(jax.ShapeDtypeStruct(head.shape, head.dtype),) * 2,
        in_specs=[pl.BlockSpec(memory_space=pltpu.VMEM)] * 2,
        out_specs=(pl.BlockSpec(memory_space=pltpu.VMEM),) * 2,
        scratch_shapes=[pltpu.SemaphoreType.DMA((2,)), pltpu.SemaphoreType.DMA((2,))],
        compiler_params=pltpu.CompilerParams(collective_id=3, has_side_effects=True),
    )(head, tail)
    return jnp.concatenate([below, cells, above], axis=1)


def _scatter_halo_kernel(size, stride, n, width, x_ref, o_ref, below_ref, above_ref,
                         got, head_buf, tail_buf, send_sem, recv_sem, own_sem, hsend, hrecv,
                         pair_got, pair_buf, pair_sem):
    me = lax.axis_index("cuts")
    cm = lax.axis_index("col")
    pos = (me // stride) % size
    base = me - pos * stride
    core = me % stride
    partner = me + 1 - 2 * core
    has_left = (cm + n - 1) // n
    has_right = 1 - cm // (n - 1)
    left, right = (me, cm - has_left), (me, cm + has_right)

    def where(peer_pos):
        return (base + peer_pos * stride, cm)

    barrier = pltpu.get_barrier_semaphore()
    for d in range(1, size):
        pl.semaphore_signal(
            barrier, inc=1, device_id=where((pos + d) % size), device_id_type=MESH
        )

    @pl.when(cm > 0)
    def _():
        pl.semaphore_signal(barrier, inc=1, device_id=left, device_id_type=MESH)

    @pl.when(cm < n - 1)
    def _():
        pl.semaphore_signal(barrier, inc=1, device_id=right, device_id_type=MESH)

    pl.semaphore_signal(barrier, inc=1, device_id=(partner, cm), device_id_type=MESH)
    pl.semaphore_wait(barrier, size + has_left + has_right)

    pair = pltpu.make_async_remote_copy(
        src_ref=x_ref.at[1 - core], dst_ref=pair_got, send_sem=pair_sem.at[0],
        recv_sem=pair_sem.at[1], device_id=(partner, cm), device_id_type=MESH,
    )
    pair.start()
    pair.wait_send()
    pair.wait_recv()
    pair_buf[...] = x_ref[core] + pair_got[...]

    @pl.when(cm == 0)
    def _():
        below_ref[...] = jnp.zeros_like(below_ref)

    @pl.when(cm == n - 1)
    def _():
        above_ref[...] = jnp.zeros_like(above_ref)

    own = pltpu.make_async_copy(pair_buf.at[pos], got.at[pos], own_sem)
    own.start()
    copies = []
    for d in range(1, size):
        peer_pos = (pos + d) % size
        copy = pltpu.make_async_remote_copy(
            src_ref=pair_buf.at[peer_pos], dst_ref=got.at[pos],
            send_sem=send_sem.at[peer_pos], recv_sem=recv_sem.at[pos],
            device_id=where(peer_pos), device_id_type=MESH,
        )
        copy.start()
        copies.append(copy)
    for copy in copies:
        copy.wait_send()
    for d in range(1, size):
        source = (pos + size - d) % size
        pltpu.make_async_remote_copy(
            src_ref=pair_buf.at[source], dst_ref=got.at[source],
            send_sem=send_sem.at[source], recv_sem=recv_sem.at[source],
            device_id=where(source), device_id_type=MESH,
        ).wait_recv()
    own.wait()
    total = got[0]
    for slot in range(1, size):
        total = total + got[slot]
    o_ref[...] = total
    planes = total.shape[1]
    head_buf[...] = total[:, :width]
    tail_buf[...] = total[:, planes - width :]

    def to_left():
        return pltpu.make_async_remote_copy(
            src_ref=head_buf, dst_ref=above_ref, send_sem=hsend.at[0],
            recv_sem=hrecv.at[1], device_id=left, device_id_type=MESH,
        )

    def to_right():
        return pltpu.make_async_remote_copy(
            src_ref=tail_buf, dst_ref=below_ref, send_sem=hsend.at[1],
            recv_sem=hrecv.at[0], device_id=right, device_id_type=MESH,
        )

    @pl.when(cm > 0)
    def _():
        to_left().start()

    @pl.when(cm < n - 1)
    def _():
        to_right().start()

    @pl.when(cm > 0)
    def _():
        to_left().wait_send()
        pltpu.make_async_remote_copy(
            src_ref=tail_buf, dst_ref=below_ref, send_sem=hsend.at[1],
            recv_sem=hrecv.at[0], device_id=left, device_id_type=MESH,
        ).wait_recv()

    @pl.when(cm < n - 1)
    def _():
        to_right().wait_send()
        pltpu.make_async_remote_copy(
            src_ref=head_buf, dst_ref=above_ref, send_sem=hsend.at[0],
            recv_sem=hrecv.at[1], device_id=right, device_id_type=MESH,
        ).wait_recv()


def scatter_with_halo(x, size, stride, width):
    n = lax.axis_size("col")
    block = x.shape[2:]
    halo = (block[0], width, *block[2:])
    vmem = pl.BlockSpec(memory_space=pltpu.VMEM)
    portion, below, above = pl.pallas_call(
        functools.partial(_scatter_halo_kernel, size, stride, n, width),
        out_shape=(
            jax.ShapeDtypeStruct(block, x.dtype),
            jax.ShapeDtypeStruct(halo, x.dtype),
            jax.ShapeDtypeStruct(halo, x.dtype),
        ),
        in_specs=[vmem],
        out_specs=(vmem, vmem, vmem),
        scratch_shapes=[
            pltpu.VMEM(x.shape[1:], x.dtype),
            pltpu.VMEM(halo, x.dtype),
            pltpu.VMEM(halo, x.dtype),
            pltpu.SemaphoreType.DMA((size,)),
            pltpu.SemaphoreType.DMA((size,)),
            pltpu.SemaphoreType.DMA,
            pltpu.SemaphoreType.DMA((2,)),
            pltpu.SemaphoreType.DMA((2,)),
            pltpu.VMEM(x.shape[1:], x.dtype),
            pltpu.VMEM(x.shape[1:], x.dtype),
            pltpu.SemaphoreType.DMA((2,)),
        ],
        compiler_params=pltpu.CompilerParams(collective_id=4, has_side_effects=True),
    )(x)
    return portion, jnp.concatenate([below, portion, above], axis=1)


def _gather_kernel(size, stride, x_ref, o_ref, got, send_sem, recv_sem, own_sem, pair_sem):
    me = lax.axis_index("cuts")
    cm = lax.axis_index("col")
    pos = (me // stride) % size
    base = me - pos * stride
    core = me % stride
    partner = me + 1 - 2 * core

    def where(peer_pos):
        return (base + peer_pos * stride, cm)

    barrier = pltpu.get_barrier_semaphore()
    for d in range(1, size):
        pl.semaphore_signal(
            barrier, inc=1, device_id=where((pos + d) % size), device_id_type=MESH
        )
    pl.semaphore_signal(barrier, inc=1, device_id=(partner, cm), device_id_type=MESH)
    pl.semaphore_wait(barrier, size)
    own = pltpu.make_async_copy(x_ref, got.at[pos], own_sem.at[0])
    own.start()
    copies = []
    for d in range(1, size):
        peer_pos = (pos + d) % size
        copy = pltpu.make_async_remote_copy(
            src_ref=x_ref, dst_ref=got.at[pos],
            send_sem=send_sem.at[peer_pos], recv_sem=recv_sem.at[pos],
            device_id=where(peer_pos), device_id_type=MESH,
        )
        copy.start()
        copies.append(copy)
    for copy in copies:
        copy.wait_send()
    for d in range(1, size):
        source = (pos + size - d) % size
        pltpu.make_async_remote_copy(
            src_ref=x_ref, dst_ref=got.at[source],
            send_sem=send_sem.at[source], recv_sem=recv_sem.at[source],
            device_id=where(source), device_id_type=MESH,
        ).wait_recv()
    own.wait()
    mine = pltpu.make_async_copy(got, o_ref.at[core], own_sem.at[1])
    mine.start()
    pair = pltpu.make_async_remote_copy(
        src_ref=got, dst_ref=o_ref.at[core], send_sem=pair_sem.at[0],
        recv_sem=pair_sem.at[1], device_id=(partner, cm), device_id_type=MESH,
    )
    pair.start()
    pair.wait_send()
    pltpu.make_async_remote_copy(
        src_ref=got, dst_ref=o_ref.at[1 - core], send_sem=pair_sem.at[0],
        recv_sem=pair_sem.at[1], device_id=(partner, cm), device_id_type=MESH,
    ).wait_recv()
    mine.wait()


def gather_in_two(x, size, stride):
    return pl.pallas_call(
        functools.partial(_gather_kernel, size, stride),
        out_shape=jax.ShapeDtypeStruct((stride, size, *x.shape), x.dtype),
        in_specs=[pl.BlockSpec(memory_space=pltpu.VMEM)],
        out_specs=pl.BlockSpec(memory_space=pl.ANY),
        scratch_shapes=[
            pltpu.VMEM((size, *x.shape), x.dtype),
            pltpu.SemaphoreType.DMA((size,)),
            pltpu.SemaphoreType.DMA((size,)),
            pltpu.SemaphoreType.DMA((2,)),
            pltpu.SemaphoreType.DMA((2,)),
        ],
        compiler_params=pltpu.CompilerParams(collective_id=1, has_side_effects=True),
    )(x)


def split_up(shard, dim, devices):
    before, after = (shard.shape[:dim], shard.shape[dim + 1 :])
    return jnp.moveaxis(shard.reshape(*before, devices, -1, *after), dim, 0)


def sent_and_summed(shard, axis, dim):
    tiles = split_up(shard, dim, lax.axis_size(axis))
    arrived = exchange(tiles, axis, 0)
    return arrived.sum(axis=0)


def joined_along(tiles, dim):
    dims = list(tiles.shape[1:])
    dims[dim] *= tiles.shape[0]
    return jnp.moveaxis(tiles, 0, dim).reshape(dims)


def from_everyone(shard, axis):
    return exchange(shard, axis, 1 if axis == "cuts" else 2, whole=True)


def gather_directly(shard, axis, dim):
    return joined_along(from_everyone(shard, axis), dim)


def taken_together(shard, axis):
    return from_everyone(shard, axis).sum(axis=0)


def packed_total(arrays, axis):
    line, at, done = (jnp.concatenate([a.reshape(-1) for a in arrays]), 0, [])
    running = taken_together(line, axis)
    for a in arrays:
        done.append(running[at : at + a.size].reshape(a.shape))
        at += a.size
    return tuple(done)


def operate(extended):
    channels, depth, cells = extended.shape
    edge = GRID
    interior = extended[:, 1:-1]
    column = jnp.arange(cells, dtype=jnp.int32) % edge
    has_left = (column > 0).astype(jnp.float32)
    has_right = (column < edge - 1).astype(jnp.float32)
    left_part = jnp.pad(interior, ((0, 0), (0, 0), (1, 0)))[:, :, :-1] * has_left
    right_part = jnp.pad(interior, ((0, 0), (0, 0), (0, 1)))[:, :, 1:] * has_right
    upper_part = jnp.pad(interior, ((0, 0), (0, 0), (edge, 0)))[:, :, :-edge]
    lower_part = jnp.pad(interior, ((0, 0), (0, 0), (0, edge)))[:, :, edge:]
    neighbours = extended[:, 2:] + extended[:, :-2]
    neighbours = neighbours + left_part + right_part + upper_part + lower_part
    return interior + strength * (6.0 * interior - neighbours)


def smooth_once(source, extended):
    planes = source.shape[1]
    first_plane = lax.axis_index("col") * planes - ITERS
    total_planes = planes * lax.axis_size("col")
    levels = first_plane + jnp.arange(planes + 2 * ITERS, dtype=jnp.int32)
    inside = ((levels >= 0) & (levels < total_planes)).astype(jnp.float32)[None, :, None]
    solution = jnp.zeros_like(source)
    residual = extended
    direction = extended / centre
    ratio = spread / centre
    for iteration in range(ITERS):
        margin = ITERS - iteration
        solution = solution + direction[:, margin : margin + planes]
        window = inside[:, iteration + 1 : iteration + 1 + planes + 2 * (margin - 1)]
        residual = (residual[:, 1:-1] - operate(direction)) * window
        ratio_next = 1.0 / (2.0 * centre / spread - ratio)
        direction = ratio_next * ratio * direction[:, 1:-1] + 2.0 * ratio_next / spread * residual
        ratio = ratio_next
    return solution + direction


def _eliminate(m_ref, b_ref, o_ref):
    m = m_ref[...]
    b = b_ref[...]
    n = m.shape[0]
    ri = lax.broadcasted_iota(jnp.int32, m.shape, 0)
    ci = lax.broadcasted_iota(jnp.int32, m.shape, 1)
    rb = lax.broadcasted_iota(jnp.int32, b.shape, 0)

    def pick_row(x, rows, p):
        return jnp.sum(jnp.where(rows == p, x, 0.0), axis=0, keepdims=True)

    def pick_col(x, p):
        return jnp.sum(jnp.where(ci[: x.shape[0]] == p, x, 0.0), axis=1, keepdims=True)

    def step(j, carry):
        m, b = carry
        p, q = 2 * j, 2 * j + 1
        c0, c1 = pick_col(m, p), pick_col(m, q)
        r0, r1 = pick_row(m, ri, p), pick_row(m, ri, q)
        s0, s1 = pick_row(b, rb, p), pick_row(b, rb, q)
        a, e = pick_col(r0, p), pick_col(r0, q)
        c, d = pick_col(r1, p), pick_col(r1, q)
        scale = 1.0 / (a * d - e * c)
        n0, n1 = (d * r0 - e * r1) * scale, (a * r1 - c * r0) * scale
        t0, t1 = (d * s0 - e * s1) * scale, (a * s1 - c * s0) * scale
        m = jnp.where(ri == p, n0, jnp.where(ri == q, n1, m - c0 * n0 - c1 * n1))
        b = jnp.where(rb == p, t0, jnp.where(rb == q, t1, b - c0 * t0 - c1 * t1))
        return m, b

    x = lax.fori_loop(0, n // 2, step, (m, b), unroll=True)[1]
    if o_ref.shape == b.shape:
        o_ref[...] = x.astype(o_ref.dtype)
    else:
        o_ref[...] = jnp.sum(jnp.where(ri == ci, x, 0.0), axis=0, keepdims=True)


def spd_solve(m, b, dtype=None):
    shape = (1, b.shape[0]) if b.shape[1] == 1 else b.shape
    return pl.pallas_call(
        _eliminate, out_shape=jax.ShapeDtypeStruct(shape, dtype or b.dtype)
    )(m, b)


def per_device(data, weights, mixing):
    local_scans, ranks, planes, cells = data.shape
    mix_gram = jnp.dot(mixing.T, mixing, precision=highest)
    weight_gram = jnp.dot(weights.T, weights, precision=highest)
    own_weights = lax.dynamic_slice_in_dim(
        weights, lax.axis_index("cuts") * local_scans, local_scans, 0
    )
    scaled = (mixing.T[None, :, :] * own_weights[:, :, None]).transpose(1, 0, 2)
    coefficients = spd_solve(
        mix_gram * weight_gram, scaled.reshape(ranks, local_scans * ranks), jnp.bfloat16
    )
    partial = lax.dot_general(
        coefficients, data.reshape(-1, planes, cells), (((1,), (0,)), ((), ())), preferred_element_type=jnp.float32
    )
    cores = 2
    chips = lax.axis_size("cuts") // cores
    portion, extended = scatter_with_halo(
        partial.reshape(cores, chips, -1, planes, cells), chips, cores, ITERS
    )
    smoothed = smooth_once(portion, extended)
    factor = gather_in_two(smoothed, chips, cores)
    factor = factor.reshape(ranks, planes, cells)
    factor_half = factor.astype(jnp.bfloat16)
    factor_gram = lax.dot_general(
        factor, factor, (((1, 2), (1, 2)), ((), ())), precision=lax.Precision.HIGH
    )
    products = lax.dot_general(
        data, factor_half, (((2, 3), (1, 2)), ((), ())), preferred_element_type=jnp.float32
    )
    targets = jnp.sum(mixing[None, :, :] * products, axis=1)
    half = ranks // 2
    row = lax.broadcasted_iota(jnp.int32, (half, half), 0)
    col = lax.broadcasted_iota(jnp.int32, (half, half), 1)
    top, off, low = (factor_gram[:half, :half], factor_gram[:half, half:], factor_gram[half:, half:])
    folded = jnp.where(row >= col, top, low)
    folded, off, low_diag, targets = packed_total(
        (folded, off, jnp.sum(jnp.where(row == col, low, 0.0), axis=1), targets), "col"
    )
    top = jnp.where(row >= col, folded, folded.T)
    low = jnp.where(row < col, folded, jnp.where(row > col, folded.T, low_diag[:, None]))
    factor_gram = jnp.concatenate(
        [jnp.concatenate([top, off], axis=1), jnp.concatenate([off.T, low], axis=1)], axis=0
    )
    updated = spd_solve(mix_gram * factor_gram, targets.T)
    return (factor, updated)


def solution(mesh):
    return jax.shard_map(
        per_device,
        mesh=mesh,
        in_specs=(P("cuts", None, "col", None), P(), P()),
        out_specs=(P(None, "col", None), P("cuts", None)),
        check_vma=False,
    )
```

```python
import functools
import jax
import jax.numpy as jnp
from jax import lax
from jax.sharding import PartitionSpec as P
from jax.experimental import pallas as pl
from jax.experimental.pallas import tpu as pltpu

MESH = pl.DeviceIdType.MESH

GRID = 32
ITERS = 3


strength = 0.5
highest = lax.Precision.HIGHEST
low_edge = 1.0
high_edge = 1.0 + 12.0 * strength
centre = (high_edge + low_edge) / 2.0
spread = (high_edge - low_edge) / 2.0


def extended_2(cells, sides, width):
    for axis, dim in sides:
        count = lax.axis_size(axis)
        ends = count - 1
        head = lax.slice_in_dim(cells, 0, width, axis=dim)
        tail = lax.slice_in_dim(cells, cells.shape[dim] - width, cells.shape[dim], axis=dim)
        cells = jnp.concatenate(
            [
                lax.ppermute(tail, axis, [(i, (i + 1) % count) for i in range(ends)]),
                cells,
                lax.ppermute(head, axis, [((i + 1) % count, i) for i in range(ends)]),
            ],
            axis=dim,
        )
    return cells


def _exchange_kernel(axis, other, size, stride, whole, summed, x_ref, o_ref, *scratch):
    if summed:
        send_sem, recv_sem, own_sem, got = scratch
    else:
        (send_sem, recv_sem, own_sem), got = scratch, o_ref
    me = lax.axis_index(axis)
    fixed = lax.axis_index(other)
    pos = (me // stride) % size
    base = me - pos * stride

    def where(peer_pos):
        peer = base + peer_pos * stride
        return (peer, fixed) if axis == "cuts" else (fixed, peer)

    def part(peer_pos):
        return x_ref if whole else x_ref.at[peer_pos]

    barrier = pltpu.get_barrier_semaphore()
    for d in range(1, size):
        pl.semaphore_signal(
            barrier, inc=1, device_id=where((pos + d) % size), device_id_type=MESH
        )
    pl.semaphore_wait(barrier, size - 1)
    own = pltpu.make_async_copy(part(pos), got.at[pos], own_sem)
    own.start()
    copies = []
    for d in range(1, size):
        peer_pos = (pos + d) % size
        copy = pltpu.make_async_remote_copy(
            src_ref=part(peer_pos),
            dst_ref=got.at[pos],
            send_sem=send_sem.at[peer_pos],
            recv_sem=recv_sem.at[pos],
            device_id=where(peer_pos),
            device_id_type=MESH,
        )
        copy.start()
        copies.append(copy)
    for copy in copies:
        copy.wait_send()
    for d in range(1, size):
        source = (pos + size - d) % size
        pltpu.make_async_remote_copy(
            src_ref=part(source),
            dst_ref=got.at[source],
            send_sem=send_sem.at[source],
            recv_sem=recv_sem.at[source],
            device_id=where(source),
            device_id_type=MESH,
        ).wait_recv()
    own.wait()
    if summed:
        total = got[0]
        for slot in range(1, size):
            total = total + got[slot]
        o_ref[...] = total


def exchange(x, axis, key, whole=False, size=None, stride=1, summed=False, space=None):
    other = "col" if axis == "cuts" else "cuts"
    size = size or lax.axis_size(axis)
    shape = (size, *x.shape) if whole else x.shape
    scratch = [
        pltpu.SemaphoreType.DMA((size,)),
        pltpu.SemaphoreType.DMA((size,)),
        pltpu.SemaphoreType.DMA,
    ]
    if summed:
        scratch.append(pltpu.VMEM(shape, x.dtype))
        shape = shape[1:]
    return pl.pallas_call(
        functools.partial(_exchange_kernel, axis, other, size, stride, whole, summed),
        out_shape=jax.ShapeDtypeStruct(shape, x.dtype),
        in_specs=[pl.BlockSpec(memory_space=pltpu.VMEM)],
        out_specs=pl.BlockSpec(memory_space=space or pltpu.VMEM),
        scratch_shapes=scratch,
        compiler_params=pltpu.CompilerParams(collective_id=key, has_side_effects=True),
    )(x)


def _halo_kernel(n, head_ref, tail_ref, below_ref, above_ref, send_sem, recv_sem):
    me = lax.axis_index("col")
    fixed = lax.axis_index("cuts")
    has_left = (me + n - 1) // n
    has_right = 1 - me // (n - 1)
    left, right = (fixed, me - has_left), (fixed, me + has_right)

    def to_left():
        return pltpu.make_async_remote_copy(
            src_ref=head_ref, dst_ref=above_ref, send_sem=send_sem.at[0],
            recv_sem=recv_sem.at[1], device_id=left, device_id_type=MESH,
        )

    def to_right():
        return pltpu.make_async_remote_copy(
            src_ref=tail_ref, dst_ref=below_ref, send_sem=send_sem.at[1],
            recv_sem=recv_sem.at[0], device_id=right, device_id_type=MESH,
        )

    barrier = pltpu.get_barrier_semaphore()

    @pl.when(me > 0)
    def _():
        pl.semaphore_signal(barrier, inc=1, device_id=left, device_id_type=MESH)

    @pl.when(me < n - 1)
    def _():
        pl.semaphore_signal(barrier, inc=1, device_id=right, device_id_type=MESH)

    pl.semaphore_wait(barrier, has_left + has_right)

    @pl.when(me == 0)
    def _():
        below_ref[...] = jnp.zeros_like(below_ref)

    @pl.when(me == n - 1)
    def _():
        above_ref[...] = jnp.zeros_like(above_ref)

    @pl.when(me > 0)
    def _():
        to_left().start()

    @pl.when(me < n - 1)
    def _():
        to_right().start()

    @pl.when(me > 0)
    def _():
        to_left().wait_send()
        pltpu.make_async_remote_copy(
            src_ref=tail_ref, dst_ref=below_ref, send_sem=send_sem.at[1],
            recv_sem=recv_sem.at[0], device_id=left, device_id_type=MESH,
        ).wait_recv()

    @pl.when(me < n - 1)
    def _():
        to_right().wait_send()
        pltpu.make_async_remote_copy(
            src_ref=head_ref, dst_ref=above_ref, send_sem=send_sem.at[0],
            recv_sem=recv_sem.at[1], device_id=right, device_id_type=MESH,
        ).wait_recv()


def with_halo(cells, width):
    n = lax.axis_size("col")
    head = lax.slice_in_dim(cells, 0, width, axis=1)
    tail = lax.slice_in_dim(cells, cells.shape[1] - width, cells.shape[1], axis=1)
    below, above = pl.pallas_call(
        functools.partial(_halo_kernel, n),
        out_shape=(jax.ShapeDtypeStruct(head.shape, head.dtype),) * 2,
        in_specs=[pl.BlockSpec(memory_space=pltpu.VMEM)] * 2,
        out_specs=(pl.BlockSpec(memory_space=pltpu.VMEM),) * 2,
        scratch_shapes=[pltpu.SemaphoreType.DMA((2,)), pltpu.SemaphoreType.DMA((2,))],
        compiler_params=pltpu.CompilerParams(collective_id=3, has_side_effects=True),
    )(head, tail)
    return jnp.concatenate([below, cells, above], axis=1)


def _scatter_halo_kernel(size, stride, n, width, x_ref, o_ref, below_ref, above_ref,
                         got, head_buf, tail_buf, send_sem, recv_sem, own_sem, hsend, hrecv,
                         pair_got, pair_buf, pair_sem):
    me = lax.axis_index("cuts")
    cm = lax.axis_index("col")
    pos = (me // stride) % size
    base = me - pos * stride
    core = me % stride
    partner = me + 1 - 2 * core
    has_left = (cm + n - 1) // n
    has_right = 1 - cm // (n - 1)
    left, right = (me, cm - has_left), (me, cm + has_right)

    def where(peer_pos):
        return (base + peer_pos * stride, cm)

    barrier = pltpu.get_barrier_semaphore()
    for d in range(1, size):
        pl.semaphore_signal(
            barrier, inc=1, device_id=where((pos + d) % size), device_id_type=MESH
        )

    @pl.when(cm > 0)
    def _():
        pl.semaphore_signal(barrier, inc=1, device_id=left, device_id_type=MESH)

    @pl.when(cm < n - 1)
    def _():
        pl.semaphore_signal(barrier, inc=1, device_id=right, device_id_type=MESH)

    pl.semaphore_signal(barrier, inc=1, device_id=(partner, cm), device_id_type=MESH)
    pl.semaphore_wait(barrier, size + has_left + has_right)

    pair = pltpu.make_async_remote_copy(
        src_ref=x_ref.at[1 - core], dst_ref=pair_got, send_sem=pair_sem.at[0],
        recv_sem=pair_sem.at[1], device_id=(partner, cm), device_id_type=MESH,
    )
    pair.start()
    pair.wait_send()
    pair.wait_recv()
    pair_buf[...] = x_ref[core] + pair_got[...]

    @pl.when(cm == 0)
    def _():
        below_ref[...] = jnp.zeros_like(below_ref)

    @pl.when(cm == n - 1)
    def _():
        above_ref[...] = jnp.zeros_like(above_ref)

    own = pltpu.make_async_copy(pair_buf.at[pos], got.at[pos], own_sem)
    own.start()
    copies = []
    for d in range(1, size):
        peer_pos = (pos + d) % size
        copy = pltpu.make_async_remote_copy(
            src_ref=pair_buf.at[peer_pos], dst_ref=got.at[pos],
            send_sem=send_sem.at[peer_pos], recv_sem=recv_sem.at[pos],
            device_id=where(peer_pos), device_id_type=MESH,
        )
        copy.start()
        copies.append(copy)
    for copy in copies:
        copy.wait_send()
    for d in range(1, size):
        source = (pos + size - d) % size
        pltpu.make_async_remote_copy(
            src_ref=pair_buf.at[source], dst_ref=got.at[source],
            send_sem=send_sem.at[source], recv_sem=recv_sem.at[source],
            device_id=where(source), device_id_type=MESH,
        ).wait_recv()
    own.wait()
    total = got[0]
    for slot in range(1, size):
        total = total + got[slot]
    o_ref[...] = total
    planes = total.shape[1]
    head_buf[...] = total[:, :width]
    tail_buf[...] = total[:, planes - width :]

    def to_left():
        return pltpu.make_async_remote_copy(
            src_ref=head_buf, dst_ref=above_ref, send_sem=hsend.at[0],
            recv_sem=hrecv.at[1], device_id=left, device_id_type=MESH,
        )

    def to_right():
        return pltpu.make_async_remote_copy(
            src_ref=tail_buf, dst_ref=below_ref, send_sem=hsend.at[1],
            recv_sem=hrecv.at[0], device_id=right, device_id_type=MESH,
        )

    @pl.when(cm > 0)
    def _():
        to_left().start()

    @pl.when(cm < n - 1)
    def _():
        to_right().start()

    @pl.when(cm > 0)
    def _():
        to_left().wait_send()
        pltpu.make_async_remote_copy(
            src_ref=tail_buf, dst_ref=below_ref, send_sem=hsend.at[1],
            recv_sem=hrecv.at[0], device_id=left, device_id_type=MESH,
        ).wait_recv()

    @pl.when(cm < n - 1)
    def _():
        to_right().wait_send()
        pltpu.make_async_remote_copy(
            src_ref=head_buf, dst_ref=above_ref, send_sem=hsend.at[0],
            recv_sem=hrecv.at[1], device_id=right, device_id_type=MESH,
        ).wait_recv()


def scatter_with_halo(x, size, stride, width):
    n = lax.axis_size("col")
    block = x.shape[2:]
    halo = (block[0], width, *block[2:])
    vmem = pl.BlockSpec(memory_space=pltpu.VMEM)
    portion, below, above = pl.pallas_call(
        functools.partial(_scatter_halo_kernel, size, stride, n, width),
        out_shape=(
            jax.ShapeDtypeStruct(block, x.dtype),
            jax.ShapeDtypeStruct(halo, x.dtype),
            jax.ShapeDtypeStruct(halo, x.dtype),
        ),
        in_specs=[vmem],
        out_specs=(vmem, vmem, vmem),
        scratch_shapes=[
            pltpu.VMEM(x.shape[1:], x.dtype),
            pltpu.VMEM(halo, x.dtype),
            pltpu.VMEM(halo, x.dtype),
            pltpu.SemaphoreType.DMA((size,)),
            pltpu.SemaphoreType.DMA((size,)),
            pltpu.SemaphoreType.DMA,
            pltpu.SemaphoreType.DMA((2,)),
            pltpu.SemaphoreType.DMA((2,)),
            pltpu.VMEM(x.shape[1:], x.dtype),
            pltpu.VMEM(x.shape[1:], x.dtype),
            pltpu.SemaphoreType.DMA((2,)),
        ],
        compiler_params=pltpu.CompilerParams(collective_id=4, has_side_effects=True),
    )(x)
    return portion, jnp.concatenate([below, portion, above], axis=1)


def _gather_kernel(size, stride, x_ref, o_ref, got, send_sem, recv_sem, own_sem, pair_sem):
    me = lax.axis_index("cuts")
    cm = lax.axis_index("col")
    pos = (me // stride) % size
    base = me - pos * stride
    core = me % stride
    partner = me + 1 - 2 * core

    def where(peer_pos):
        return (base + peer_pos * stride, cm)

    barrier = pltpu.get_barrier_semaphore()
    for d in range(1, size):
        pl.semaphore_signal(
            barrier, inc=1, device_id=where((pos + d) % size), device_id_type=MESH
        )
    pl.semaphore_signal(barrier, inc=1, device_id=(partner, cm), device_id_type=MESH)
    pl.semaphore_wait(barrier, size)
    own = pltpu.make_async_copy(x_ref, got.at[pos], own_sem.at[0])
    own.start()
    copies = []
    for d in range(1, size):
        peer_pos = (pos + d) % size
        copy = pltpu.make_async_remote_copy(
            src_ref=x_ref, dst_ref=got.at[pos],
            send_sem=send_sem.at[peer_pos], recv_sem=recv_sem.at[pos],
            device_id=where(peer_pos), device_id_type=MESH,
        )
        copy.start()
        copies.append(copy)
    for copy in copies:
        copy.wait_send()
    for d in range(1, size):
        source = (pos + size - d) % size
        pltpu.make_async_remote_copy(
            src_ref=x_ref, dst_ref=got.at[source],
            send_sem=send_sem.at[source], recv_sem=recv_sem.at[source],
            device_id=where(source), device_id_type=MESH,
        ).wait_recv()
    own.wait()
    mine = pltpu.make_async_copy(got, o_ref.at[core], own_sem.at[1])
    mine.start()
    pair = pltpu.make_async_remote_copy(
        src_ref=got, dst_ref=o_ref.at[core], send_sem=pair_sem.at[0],
        recv_sem=pair_sem.at[1], device_id=(partner, cm), device_id_type=MESH,
    )
    pair.start()
    pair.wait_send()
    pltpu.make_async_remote_copy(
        src_ref=got, dst_ref=o_ref.at[1 - core], send_sem=pair_sem.at[0],
        recv_sem=pair_sem.at[1], device_id=(partner, cm), device_id_type=MESH,
    ).wait_recv()
    mine.wait()


def gather_in_two(x, size, stride):
    return pl.pallas_call(
        functools.partial(_gather_kernel, size, stride),
        out_shape=jax.ShapeDtypeStruct((stride, size, *x.shape), x.dtype),
        in_specs=[pl.BlockSpec(memory_space=pltpu.VMEM)],
        out_specs=pl.BlockSpec(memory_space=pl.ANY),
        scratch_shapes=[
            pltpu.VMEM((size, *x.shape), x.dtype),
            pltpu.SemaphoreType.DMA((size,)),
            pltpu.SemaphoreType.DMA((size,)),
            pltpu.SemaphoreType.DMA((2,)),
            pltpu.SemaphoreType.DMA((2,)),
        ],
        compiler_params=pltpu.CompilerParams(collective_id=1, has_side_effects=True),
    )(x)


def split_up(shard, dim, devices):
    before, after = (shard.shape[:dim], shard.shape[dim + 1 :])
    return jnp.moveaxis(shard.reshape(*before, devices, -1, *after), dim, 0)


def sent_and_summed(shard, axis, dim):
    tiles = split_up(shard, dim, lax.axis_size(axis))
    arrived = exchange(tiles, axis, 0)
    return arrived.sum(axis=0)


def joined_along(tiles, dim):
    dims = list(tiles.shape[1:])
    dims[dim] *= tiles.shape[0]
    return jnp.moveaxis(tiles, 0, dim).reshape(dims)


def from_everyone(shard, axis):
    return exchange(shard, axis, 1 if axis == "cuts" else 2, whole=True)


def gather_directly(shard, axis, dim):
    return joined_along(from_everyone(shard, axis), dim)


def taken_together(shard, axis):
    return from_everyone(shard, axis).sum(axis=0)


def packed_total(arrays, axis):
    line, at, done = (jnp.concatenate([a.reshape(-1) for a in arrays]), 0, [])
    running = taken_together(line, axis)
    for a in arrays:
        done.append(running[at : at + a.size].reshape(a.shape))
        at += a.size
    return tuple(done)


def operate(extended):
    channels, depth, cells = extended.shape
    edge = GRID
    interior = extended[:, 1:-1]
    column = jnp.arange(cells, dtype=jnp.int32) % edge
    has_left = (column > 0).astype(jnp.float32)
    has_right = (column < edge - 1).astype(jnp.float32)
    left_part = jnp.pad(interior, ((0, 0), (0, 0), (1, 0)))[:, :, :-1] * has_left
    right_part = jnp.pad(interior, ((0, 0), (0, 0), (0, 1)))[:, :, 1:] * has_right
    upper_part = jnp.pad(interior, ((0, 0), (0, 0), (edge, 0)))[:, :, :-edge]
    lower_part = jnp.pad(interior, ((0, 0), (0, 0), (0, edge)))[:, :, edge:]
    neighbours = extended[:, 2:] + extended[:, :-2]
    neighbours = neighbours + left_part + right_part + upper_part + lower_part
    return interior + strength * (6.0 * interior - neighbours)


def smooth_once(source, extended):
    planes = source.shape[1]
    first_plane = lax.axis_index("col") * planes - ITERS
    total_planes = planes * lax.axis_size("col")
    levels = first_plane + jnp.arange(planes + 2 * ITERS, dtype=jnp.int32)
    inside = ((levels >= 0) & (levels < total_planes)).astype(jnp.float32)[None, :, None]
    solution = jnp.zeros_like(source)
    residual = extended
    direction = extended / centre
    ratio = spread / centre
    for iteration in range(ITERS):
        margin = ITERS - iteration
        solution = solution + direction[:, margin : margin + planes]
        window = inside[:, iteration + 1 : iteration + 1 + planes + 2 * (margin - 1)]
        residual = (residual[:, 1:-1] - operate(direction)) * window
        ratio_next = 1.0 / (2.0 * centre / spread - ratio)
        direction = ratio_next * ratio * direction[:, 1:-1] + 2.0 * ratio_next / spread * residual
        ratio = ratio_next
    return solution + direction


def _gauss_jordan(m, b):
    n = m.shape[0]
    ri = lax.broadcasted_iota(jnp.int32, m.shape, 0)
    ci = lax.broadcasted_iota(jnp.int32, m.shape, 1)
    rb = lax.broadcasted_iota(jnp.int32, b.shape, 0)

    def pick_row(x, rows, p):
        return jnp.sum(jnp.where(rows == p, x, 0.0), axis=0, keepdims=True)

    def pick_col(x, p):
        return jnp.sum(jnp.where(ci[: x.shape[0]] == p, x, 0.0), axis=1, keepdims=True)

    def step(j, carry):
        m, b = carry
        p, q = 2 * j, 2 * j + 1
        c0, c1 = pick_col(m, p), pick_col(m, q)
        r0, r1 = pick_row(m, ri, p), pick_row(m, ri, q)
        s0, s1 = pick_row(b, rb, p), pick_row(b, rb, q)
        a, e = pick_col(r0, p), pick_col(r0, q)
        c, d = pick_col(r1, p), pick_col(r1, q)
        scale = 1.0 / (a * d - e * c)
        n0, n1 = (d * r0 - e * r1) * scale, (a * r1 - c * r0) * scale
        t0, t1 = (d * s0 - e * s1) * scale, (a * s1 - c * s0) * scale
        m = jnp.where(ri == p, n0, jnp.where(ri == q, n1, m - c0 * n0 - c1 * n1))
        b = jnp.where(rb == p, t0, jnp.where(rb == q, t1, b - c0 * t0 - c1 * t1))
        return m, b

    return lax.fori_loop(0, n // 2, step, (m, b), unroll=True)[1]


def _eliminate(m_ref, b_ref, o_ref):
    o_ref[...] = _gauss_jordan(m_ref[...], b_ref[...]).astype(o_ref.dtype)


def _final_solve(g_ref, t_ref, o_ref):
    g = g_ref[...]
    n = g.shape[0]
    t = t_ref[...]
    ri = lax.broadcasted_iota(jnp.int32, g.shape, 0)
    ci = lax.broadcasted_iota(jnp.int32, g.shape, 1)
    m = g * t[:n]
    b = jnp.sum(jnp.where(ri == ci, t[n : n + 1], 0.0), axis=1, keepdims=True)
    x = _gauss_jordan(m, b)
    o_ref[...] = jnp.sum(jnp.where(ri == ci, x, 0.0), axis=0, keepdims=True)


def spd_solve(m, b, dtype=None):
    return pl.pallas_call(
        _eliminate, out_shape=jax.ShapeDtypeStruct(b.shape, dtype or b.dtype)
    )(m, b)


def final_solve(mix_gram, total):
    return pl.pallas_call(
        _final_solve, out_shape=jax.ShapeDtypeStruct((1, mix_gram.shape[0]), jnp.float32)
    )(mix_gram, total)


def per_device(data, weights, mixing):
    local_scans, ranks, planes, cells = data.shape
    mix_gram = jnp.dot(mixing.T, mixing, precision=highest)
    weight_gram = jnp.dot(weights.T, weights, precision=highest)
    own_weights = lax.dynamic_slice_in_dim(
        weights, lax.axis_index("cuts") * local_scans, local_scans, 0
    )
    scaled = (mixing.T[None, :, :] * own_weights[:, :, None]).transpose(1, 0, 2)
    coefficients = spd_solve(
        mix_gram * weight_gram, scaled.reshape(ranks, local_scans * ranks), jnp.bfloat16
    )
    partial = lax.dot_general(
        coefficients, data.reshape(-1, planes, cells), (((1,), (0,)), ((), ())), preferred_element_type=jnp.float32
    )
    cores = 2
    chips = lax.axis_size("cuts") // cores
    portion, extended = scatter_with_halo(
        partial.reshape(cores, chips, -1, planes, cells), chips, cores, ITERS
    )
    smoothed = smooth_once(portion, extended)
    factor = gather_in_two(smoothed, chips, cores)
    factor = factor.reshape(ranks, planes, cells)
    factor_half = factor.astype(jnp.bfloat16)
    factor_gram = lax.dot_general(
        factor, factor, (((1, 2), (1, 2)), ((), ())), precision=lax.Precision.HIGH
    )
    products = lax.dot_general(
        data, factor_half, (((2, 3), (1, 2)), ((), ())), preferred_element_type=jnp.float32
    )
    targets = jnp.sum(mixing[None, :, :] * products, axis=1)
    payload = jnp.concatenate([factor_gram, targets], axis=0)
    total = exchange(payload, "col", 2, whole=True, summed=True)
    updated = final_solve(mix_gram, total)
    return (factor, updated)


def solution(mesh):
    return jax.shard_map(
        per_device,
        mesh=mesh,
        in_specs=(P("cuts", None, "col", None), P(), P()),
        out_specs=(P(None, "col", None), P("cuts", None)),
        check_vma=False,
    )
```

```python
import functools
import jax
import jax.numpy as jnp
from jax import lax
from jax.sharding import PartitionSpec as P
from jax.experimental import pallas as pl
from jax.experimental.pallas import tpu as pltpu

MESH = pl.DeviceIdType.MESH

GRID = 32
ITERS = 3


strength = 0.5
highest = lax.Precision.HIGHEST
low_edge = 1.0
high_edge = 1.0 + 12.0 * strength
centre = (high_edge + low_edge) / 2.0
spread = (high_edge - low_edge) / 2.0


def extended_2(cells, sides, width):
    for axis, dim in sides:
        count = lax.axis_size(axis)
        ends = count - 1
        head = lax.slice_in_dim(cells, 0, width, axis=dim)
        tail = lax.slice_in_dim(cells, cells.shape[dim] - width, cells.shape[dim], axis=dim)
        cells = jnp.concatenate(
            [
                lax.ppermute(tail, axis, [(i, (i + 1) % count) for i in range(ends)]),
                cells,
                lax.ppermute(head, axis, [((i + 1) % count, i) for i in range(ends)]),
            ],
            axis=dim,
        )
    return cells


def _exchange_kernel(axis, other, size, stride, whole, summed, x_ref, o_ref, *scratch):
    if summed:
        send_sem, recv_sem, own_sem, got = scratch
    else:
        (send_sem, recv_sem, own_sem), got = scratch, o_ref
    me = lax.axis_index(axis)
    fixed = lax.axis_index(other)
    pos = (me // stride) % size
    base = me - pos * stride

    def where(peer_pos):
        peer = base + peer_pos * stride
        return (peer, fixed) if axis == "cuts" else (fixed, peer)

    def part(peer_pos):
        return x_ref if whole else x_ref.at[peer_pos]

    barrier = pltpu.get_barrier_semaphore()
    for d in range(1, size):
        pl.semaphore_signal(
            barrier, inc=1, device_id=where((pos + d) % size), device_id_type=MESH
        )
    pl.semaphore_wait(barrier, size - 1)
    own = pltpu.make_async_copy(part(pos), got.at[pos], own_sem)
    own.start()
    copies = []
    for d in range(1, size):
        peer_pos = (pos + d) % size
        copy = pltpu.make_async_remote_copy(
            src_ref=part(peer_pos),
            dst_ref=got.at[pos],
            send_sem=send_sem.at[peer_pos],
            recv_sem=recv_sem.at[pos],
            device_id=where(peer_pos),
            device_id_type=MESH,
        )
        copy.start()
        copies.append(copy)
    for copy in copies:
        copy.wait_send()
    for d in range(1, size):
        source = (pos + size - d) % size
        pltpu.make_async_remote_copy(
            src_ref=part(source),
            dst_ref=got.at[source],
            send_sem=send_sem.at[source],
            recv_sem=recv_sem.at[source],
            device_id=where(source),
            device_id_type=MESH,
        ).wait_recv()
    own.wait()
    if summed:
        total = got[0]
        for slot in range(1, size):
            total = total + got[slot]
        o_ref[...] = total


def exchange(x, axis, key, whole=False, size=None, stride=1, summed=False, space=None):
    other = "col" if axis == "cuts" else "cuts"
    size = size or lax.axis_size(axis)
    shape = (size, *x.shape) if whole else x.shape
    scratch = [
        pltpu.SemaphoreType.DMA((size,)),
        pltpu.SemaphoreType.DMA((size,)),
        pltpu.SemaphoreType.DMA,
    ]
    if summed:
        scratch.append(pltpu.VMEM(shape, x.dtype))
        shape = shape[1:]
    return pl.pallas_call(
        functools.partial(_exchange_kernel, axis, other, size, stride, whole, summed),
        out_shape=jax.ShapeDtypeStruct(shape, x.dtype),
        in_specs=[pl.BlockSpec(memory_space=pltpu.VMEM)],
        out_specs=pl.BlockSpec(memory_space=space or pltpu.VMEM),
        scratch_shapes=scratch,
        compiler_params=pltpu.CompilerParams(collective_id=key, has_side_effects=True),
    )(x)


def _halo_kernel(n, head_ref, tail_ref, below_ref, above_ref, send_sem, recv_sem):
    me = lax.axis_index("col")
    fixed = lax.axis_index("cuts")
    has_left = (me + n - 1) // n
    has_right = 1 - me // (n - 1)
    left, right = (fixed, me - has_left), (fixed, me + has_right)

    def to_left():
        return pltpu.make_async_remote_copy(
            src_ref=head_ref, dst_ref=above_ref, send_sem=send_sem.at[0],
            recv_sem=recv_sem.at[1], device_id=left, device_id_type=MESH,
        )

    def to_right():
        return pltpu.make_async_remote_copy(
            src_ref=tail_ref, dst_ref=below_ref, send_sem=send_sem.at[1],
            recv_sem=recv_sem.at[0], device_id=right, device_id_type=MESH,
        )

    barrier = pltpu.get_barrier_semaphore()

    @pl.when(me > 0)
    def _():
        pl.semaphore_signal(barrier, inc=1, device_id=left, device_id_type=MESH)

    @pl.when(me < n - 1)
    def _():
        pl.semaphore_signal(barrier, inc=1, device_id=right, device_id_type=MESH)

    pl.semaphore_wait(barrier, has_left + has_right)

    @pl.when(me == 0)
    def _():
        below_ref[...] = jnp.zeros_like(below_ref)

    @pl.when(me == n - 1)
    def _():
        above_ref[...] = jnp.zeros_like(above_ref)

    @pl.when(me > 0)
    def _():
        to_left().start()

    @pl.when(me < n - 1)
    def _():
        to_right().start()

    @pl.when(me > 0)
    def _():
        to_left().wait_send()
        pltpu.make_async_remote_copy(
            src_ref=tail_ref, dst_ref=below_ref, send_sem=send_sem.at[1],
            recv_sem=recv_sem.at[0], device_id=left, device_id_type=MESH,
        ).wait_recv()

    @pl.when(me < n - 1)
    def _():
        to_right().wait_send()
        pltpu.make_async_remote_copy(
            src_ref=head_ref, dst_ref=above_ref, send_sem=send_sem.at[0],
            recv_sem=recv_sem.at[1], device_id=right, device_id_type=MESH,
        ).wait_recv()


def with_halo(cells, width):
    n = lax.axis_size("col")
    head = lax.slice_in_dim(cells, 0, width, axis=1)
    tail = lax.slice_in_dim(cells, cells.shape[1] - width, cells.shape[1], axis=1)
    below, above = pl.pallas_call(
        functools.partial(_halo_kernel, n),
        out_shape=(jax.ShapeDtypeStruct(head.shape, head.dtype),) * 2,
        in_specs=[pl.BlockSpec(memory_space=pltpu.VMEM)] * 2,
        out_specs=(pl.BlockSpec(memory_space=pltpu.VMEM),) * 2,
        scratch_shapes=[pltpu.SemaphoreType.DMA((2,)), pltpu.SemaphoreType.DMA((2,))],
        compiler_params=pltpu.CompilerParams(collective_id=3, has_side_effects=True),
    )(head, tail)
    return jnp.concatenate([below, cells, above], axis=1)


def _scatter_halo_kernel(size, stride, n, width, x_ref, o_ref, below_ref, above_ref,
                         got, head_buf, tail_buf, send_sem, recv_sem, own_sem, hsend, hrecv,
                         pair_got, pair_buf, pair_sem):
    me = lax.axis_index("cuts")
    cm = lax.axis_index("col")
    pos = (me // stride) % size
    base = me - pos * stride
    core = me % stride
    partner = me + 1 - 2 * core
    has_left = (cm + n - 1) // n
    has_right = 1 - cm // (n - 1)
    left, right = (me, cm - has_left), (me, cm + has_right)

    def where(peer_pos):
        return (base + peer_pos * stride, cm)

    barrier = pltpu.get_barrier_semaphore()
    for d in range(1, size):
        pl.semaphore_signal(
            barrier, inc=1, device_id=where((pos + d) % size), device_id_type=MESH
        )

    @pl.when(cm > 0)
    def _():
        pl.semaphore_signal(barrier, inc=1, device_id=left, device_id_type=MESH)

    @pl.when(cm < n - 1)
    def _():
        pl.semaphore_signal(barrier, inc=1, device_id=right, device_id_type=MESH)

    pl.semaphore_signal(barrier, inc=1, device_id=(partner, cm), device_id_type=MESH)
    pl.semaphore_wait(barrier, size + has_left + has_right)

    pair = pltpu.make_async_remote_copy(
        src_ref=x_ref.at[1 - core], dst_ref=pair_got, send_sem=pair_sem.at[0],
        recv_sem=pair_sem.at[1], device_id=(partner, cm), device_id_type=MESH,
    )
    pair.start()
    pair.wait_send()
    pair.wait_recv()
    pair_buf[...] = x_ref[core] + pair_got[...]

    @pl.when(cm == 0)
    def _():
        below_ref[...] = jnp.zeros_like(below_ref)

    @pl.when(cm == n - 1)
    def _():
        above_ref[...] = jnp.zeros_like(above_ref)

    own = pltpu.make_async_copy(pair_buf.at[pos], got.at[pos], own_sem)
    own.start()
    copies = []
    for d in range(1, size):
        peer_pos = (pos + d) % size
        copy = pltpu.make_async_remote_copy(
            src_ref=pair_buf.at[peer_pos], dst_ref=got.at[pos],
            send_sem=send_sem.at[peer_pos], recv_sem=recv_sem.at[pos],
            device_id=where(peer_pos), device_id_type=MESH,
        )
        copy.start()
        copies.append(copy)
    for copy in copies:
        copy.wait_send()
    for d in range(1, size):
        source = (pos + size - d) % size
        pltpu.make_async_remote_copy(
            src_ref=pair_buf.at[source], dst_ref=got.at[source],
            send_sem=send_sem.at[source], recv_sem=recv_sem.at[source],
            device_id=where(source), device_id_type=MESH,
        ).wait_recv()
    own.wait()
    total = got[0]
    for slot in range(1, size):
        total = total + got[slot]
    o_ref[...] = total
    planes = total.shape[1]
    head_buf[...] = total[:, :width]
    tail_buf[...] = total[:, planes - width :]

    def to_left():
        return pltpu.make_async_remote_copy(
            src_ref=head_buf, dst_ref=above_ref, send_sem=hsend.at[0],
            recv_sem=hrecv.at[1], device_id=left, device_id_type=MESH,
        )

    def to_right():
        return pltpu.make_async_remote_copy(
            src_ref=tail_buf, dst_ref=below_ref, send_sem=hsend.at[1],
            recv_sem=hrecv.at[0], device_id=right, device_id_type=MESH,
        )

    @pl.when(cm > 0)
    def _():
        to_left().start()

    @pl.when(cm < n - 1)
    def _():
        to_right().start()

    @pl.when(cm > 0)
    def _():
        to_left().wait_send()
        pltpu.make_async_remote_copy(
            src_ref=tail_buf, dst_ref=below_ref, send_sem=hsend.at[1],
            recv_sem=hrecv.at[0], device_id=left, device_id_type=MESH,
        ).wait_recv()

    @pl.when(cm < n - 1)
    def _():
        to_right().wait_send()
        pltpu.make_async_remote_copy(
            src_ref=head_buf, dst_ref=above_ref, send_sem=hsend.at[0],
            recv_sem=hrecv.at[1], device_id=right, device_id_type=MESH,
        ).wait_recv()


def scatter_with_halo(x, size, stride, width):
    n = lax.axis_size("col")
    block = x.shape[2:]
    halo = (block[0], width, *block[2:])
    vmem = pl.BlockSpec(memory_space=pltpu.VMEM)
    portion, below, above = pl.pallas_call(
        functools.partial(_scatter_halo_kernel, size, stride, n, width),
        out_shape=(
            jax.ShapeDtypeStruct(block, x.dtype),
            jax.ShapeDtypeStruct(halo, x.dtype),
            jax.ShapeDtypeStruct(halo, x.dtype),
        ),
        in_specs=[vmem],
        out_specs=(vmem, vmem, vmem),
        scratch_shapes=[
            pltpu.VMEM(x.shape[1:], x.dtype),
            pltpu.VMEM(halo, x.dtype),
            pltpu.VMEM(halo, x.dtype),
            pltpu.SemaphoreType.DMA((size,)),
            pltpu.SemaphoreType.DMA((size,)),
            pltpu.SemaphoreType.DMA,
            pltpu.SemaphoreType.DMA((2,)),
            pltpu.SemaphoreType.DMA((2,)),
            pltpu.VMEM(x.shape[1:], x.dtype),
            pltpu.VMEM(x.shape[1:], x.dtype),
            pltpu.SemaphoreType.DMA((2,)),
        ],
        compiler_params=pltpu.CompilerParams(collective_id=4, has_side_effects=True),
    )(x)
    return portion, jnp.concatenate([below, portion, above], axis=1)


def _gather_kernel(size, stride, x_ref, o_ref, got, send_sem, recv_sem, own_sem, pair_sem):
    me = lax.axis_index("cuts")
    cm = lax.axis_index("col")
    pos = (me // stride) % size
    base = me - pos * stride
    core = me % stride
    partner = me + 1 - 2 * core

    def where(peer_pos):
        return (base + peer_pos * stride, cm)

    barrier = pltpu.get_barrier_semaphore()
    for d in range(1, size):
        pl.semaphore_signal(
            barrier, inc=1, device_id=where((pos + d) % size), device_id_type=MESH
        )
    pl.semaphore_signal(barrier, inc=1, device_id=(partner, cm), device_id_type=MESH)
    pl.semaphore_wait(barrier, size)
    own = pltpu.make_async_copy(x_ref, got.at[pos], own_sem.at[0])
    own.start()
    copies = []
    for d in range(1, size):
        peer_pos = (pos + d) % size
        copy = pltpu.make_async_remote_copy(
            src_ref=x_ref, dst_ref=got.at[pos],
            send_sem=send_sem.at[peer_pos], recv_sem=recv_sem.at[pos],
            device_id=where(peer_pos), device_id_type=MESH,
        )
        copy.start()
        copies.append(copy)
    for copy in copies:
        copy.wait_send()
    for d in range(1, size):
        source = (pos + size - d) % size
        pltpu.make_async_remote_copy(
            src_ref=x_ref, dst_ref=got.at[source],
            send_sem=send_sem.at[source], recv_sem=recv_sem.at[source],
            device_id=where(source), device_id_type=MESH,
        ).wait_recv()
    own.wait()
    mine = pltpu.make_async_copy(got, o_ref.at[core], own_sem.at[1])
    mine.start()
    pair = pltpu.make_async_remote_copy(
        src_ref=got, dst_ref=o_ref.at[core], send_sem=pair_sem.at[0],
        recv_sem=pair_sem.at[1], device_id=(partner, cm), device_id_type=MESH,
    )
    pair.start()
    pair.wait_send()
    pltpu.make_async_remote_copy(
        src_ref=got, dst_ref=o_ref.at[1 - core], send_sem=pair_sem.at[0],
        recv_sem=pair_sem.at[1], device_id=(partner, cm), device_id_type=MESH,
    ).wait_recv()
    mine.wait()


def gather_in_two(x, size, stride):
    return pl.pallas_call(
        functools.partial(_gather_kernel, size, stride),
        out_shape=jax.ShapeDtypeStruct((stride, size, *x.shape), x.dtype),
        in_specs=[pl.BlockSpec(memory_space=pltpu.VMEM)],
        out_specs=pl.BlockSpec(memory_space=pl.ANY),
        scratch_shapes=[
            pltpu.VMEM((size, *x.shape), x.dtype),
            pltpu.SemaphoreType.DMA((size,)),
            pltpu.SemaphoreType.DMA((size,)),
            pltpu.SemaphoreType.DMA((2,)),
            pltpu.SemaphoreType.DMA((2,)),
        ],
        compiler_params=pltpu.CompilerParams(collective_id=1, has_side_effects=True),
    )(x)


def split_up(shard, dim, devices):
    before, after = (shard.shape[:dim], shard.shape[dim + 1 :])
    return jnp.moveaxis(shard.reshape(*before, devices, -1, *after), dim, 0)


def sent_and_summed(shard, axis, dim):
    tiles = split_up(shard, dim, lax.axis_size(axis))
    arrived = exchange(tiles, axis, 0)
    return arrived.sum(axis=0)


def joined_along(tiles, dim):
    dims = list(tiles.shape[1:])
    dims[dim] *= tiles.shape[0]
    return jnp.moveaxis(tiles, 0, dim).reshape(dims)


def from_everyone(shard, axis):
    return exchange(shard, axis, 1 if axis == "cuts" else 2, whole=True)


def gather_directly(shard, axis, dim):
    return joined_along(from_everyone(shard, axis), dim)


def taken_together(shard, axis):
    return from_everyone(shard, axis).sum(axis=0)


def packed_total(arrays, axis):
    line, at, done = (jnp.concatenate([a.reshape(-1) for a in arrays]), 0, [])
    lanes = 128
    rows = -(-line.size // lanes)
    block = jnp.pad(line, (0, rows * lanes - line.size)).reshape(rows, lanes)
    running = taken_together(block, axis).reshape(-1)
    for a in arrays:
        done.append(running[at : at + a.size].reshape(a.shape))
        at += a.size
    return tuple(done)


def operate(extended):
    channels, depth, cells = extended.shape
    edge = GRID
    interior = extended[:, 1:-1]
    column = jnp.arange(cells, dtype=jnp.int32) % edge
    has_left = (column > 0).astype(jnp.float32)
    has_right = (column < edge - 1).astype(jnp.float32)
    left_part = jnp.pad(interior, ((0, 0), (0, 0), (1, 0)))[:, :, :-1] * has_left
    right_part = jnp.pad(interior, ((0, 0), (0, 0), (0, 1)))[:, :, 1:] * has_right
    upper_part = jnp.pad(interior, ((0, 0), (0, 0), (edge, 0)))[:, :, :-edge]
    lower_part = jnp.pad(interior, ((0, 0), (0, 0), (0, edge)))[:, :, edge:]
    neighbours = extended[:, 2:] + extended[:, :-2]
    neighbours = neighbours + left_part + right_part + upper_part + lower_part
    return interior + strength * (6.0 * interior - neighbours)


def smooth_once(source, extended):
    planes = source.shape[1]
    first_plane = lax.axis_index("col") * planes - ITERS
    total_planes = planes * lax.axis_size("col")
    levels = first_plane + jnp.arange(planes + 2 * ITERS, dtype=jnp.int32)
    inside = ((levels >= 0) & (levels < total_planes)).astype(jnp.float32)[None, :, None]
    solution = jnp.zeros_like(source)
    residual = extended
    direction = extended / centre
    ratio = spread / centre
    for iteration in range(ITERS):
        margin = ITERS - iteration
        solution = solution + direction[:, margin : margin + planes]
        window = inside[:, iteration + 1 : iteration + 1 + planes + 2 * (margin - 1)]
        residual = (residual[:, 1:-1] - operate(direction)) * window
        ratio_next = 1.0 / (2.0 * centre / spread - ratio)
        direction = ratio_next * ratio * direction[:, 1:-1] + 2.0 * ratio_next / spread * residual
        ratio = ratio_next
    return solution + direction


def _eliminate(m_ref, b_ref, o_ref):
    m = m_ref[...]
    b = b_ref[...]
    n = m.shape[0]
    ri = lax.broadcasted_iota(jnp.int32, m.shape, 0)
    ci = lax.broadcasted_iota(jnp.int32, m.shape, 1)
    rb = lax.broadcasted_iota(jnp.int32, b.shape, 0)

    def pick_row(x, rows, p):
        return jnp.sum(jnp.where(rows == p, x, 0.0), axis=0, keepdims=True)

    def pick_col(x, p):
        return jnp.sum(jnp.where(ci[: x.shape[0]] == p, x, 0.0), axis=1, keepdims=True)

    def step(j, carry):
        m, b = carry
        p, q = 2 * j, 2 * j + 1
        c0, c1 = pick_col(m, p), pick_col(m, q)
        r0, r1 = pick_row(m, ri, p), pick_row(m, ri, q)
        s0, s1 = pick_row(b, rb, p), pick_row(b, rb, q)
        a, e = pick_col(r0, p), pick_col(r0, q)
        c, d = pick_col(r1, p), pick_col(r1, q)
        scale = 1.0 / (a * d - e * c)
        n0, n1 = (d * r0 - e * r1) * scale, (a * r1 - c * r0) * scale
        t0, t1 = (d * s0 - e * s1) * scale, (a * s1 - c * s0) * scale
        m = jnp.where(ri == p, n0, jnp.where(ri == q, n1, m - c0 * n0 - c1 * n1))
        b = jnp.where(rb == p, t0, jnp.where(rb == q, t1, b - c0 * t0 - c1 * t1))
        return m, b

    x = lax.fori_loop(0, n // 2, step, (m, b), unroll=True)[1]
    if o_ref.shape == b.shape:
        o_ref[...] = x.astype(o_ref.dtype)
    else:
        o_ref[...] = jnp.sum(jnp.where(ri == ci, x, 0.0), axis=0, keepdims=True)


def spd_solve(m, b, dtype=None):
    shape = (1, b.shape[0]) if b.shape[1] == 1 else b.shape
    return pl.pallas_call(
        _eliminate, out_shape=jax.ShapeDtypeStruct(shape, dtype or b.dtype)
    )(m, b)


def per_device(data, weights, mixing):
    local_scans, ranks, planes, cells = data.shape
    mix_gram = jnp.dot(mixing.T, mixing, precision=highest)
    weight_gram = jnp.dot(weights.T, weights, precision=highest)
    own_weights = lax.dynamic_slice_in_dim(
        weights, lax.axis_index("cuts") * local_scans, local_scans, 0
    )
    scaled = (mixing.T[None, :, :] * own_weights[:, :, None]).transpose(1, 0, 2)
    coefficients = spd_solve(
        mix_gram * weight_gram, scaled.reshape(ranks, local_scans * ranks), jnp.bfloat16
    )
    partial = lax.dot_general(
        coefficients, data.reshape(-1, planes, cells), (((1,), (0,)), ((), ())), preferred_element_type=jnp.float32
    )
    cores = 2
    chips = lax.axis_size("cuts") // cores
    portion, extended = scatter_with_halo(
        partial.reshape(cores, chips, -1, planes, cells), chips, cores, ITERS
    )
    smoothed = smooth_once(portion, extended)
    factor = gather_in_two(smoothed, chips, cores)
    factor = factor.reshape(ranks, planes, cells)
    factor_half = factor.astype(jnp.bfloat16)
    factor_gram = lax.dot_general(
        factor, factor, (((1, 2), (1, 2)), ((), ())), precision=lax.Precision.HIGH
    )
    products = lax.dot_general(
        data, factor_half, (((2, 3), (1, 2)), ((), ())), preferred_element_type=jnp.float32
    )
    targets = jnp.sum(mixing[None, :, :] * products, axis=1)
    half = ranks // 2
    row = lax.broadcasted_iota(jnp.int32, (half, half), 0)
    col = lax.broadcasted_iota(jnp.int32, (half, half), 1)
    top, off, low = (factor_gram[:half, :half], factor_gram[:half, half:], factor_gram[half:, half:])
    folded = jnp.where(row >= col, top, low)
    folded, off, low_diag, targets = packed_total(
        (folded, off, jnp.sum(jnp.where(row == col, low, 0.0), axis=1), targets), "col"
    )
    top = jnp.where(row >= col, folded, folded.T)
    low = jnp.where(row < col, folded, jnp.where(row > col, folded.T, low_diag[:, None]))
    factor_gram = jnp.concatenate(
        [jnp.concatenate([top, off], axis=1), jnp.concatenate([off.T, low], axis=1)], axis=0
    )
    updated = spd_solve(mix_gram * factor_gram, targets.T)
    return (factor, updated)


def solution(mesh):
    return jax.shard_map(
        per_device,
        mesh=mesh,
        in_specs=(P("cuts", None, "col", None), P(), P()),
        out_specs=(P(None, "col", None), P("cuts", None)),
        check_vma=False,
    )
```

```python
import functools
import jax
import jax.numpy as jnp
from jax import lax
from jax.sharding import PartitionSpec as P
from jax.experimental import pallas as pl
from jax.experimental.pallas import tpu as pltpu

MESH = pl.DeviceIdType.MESH

GRID = 32
ITERS = 3


strength = 0.5
highest = lax.Precision.HIGHEST
low_edge = 1.0
high_edge = 1.0 + 12.0 * strength
centre = (high_edge + low_edge) / 2.0
spread = (high_edge - low_edge) / 2.0


def extended_2(cells, sides, width):
    for axis, dim in sides:
        count = lax.axis_size(axis)
        ends = count - 1
        head = lax.slice_in_dim(cells, 0, width, axis=dim)
        tail = lax.slice_in_dim(cells, cells.shape[dim] - width, cells.shape[dim], axis=dim)
        cells = jnp.concatenate(
            [
                lax.ppermute(tail, axis, [(i, (i + 1) % count) for i in range(ends)]),
                cells,
                lax.ppermute(head, axis, [((i + 1) % count, i) for i in range(ends)]),
            ],
            axis=dim,
        )
    return cells


def _exchange_kernel(axis, other, size, stride, whole, summed, x_ref, o_ref, *scratch):
    if summed:
        send_sem, recv_sem, own_sem, got = scratch
    else:
        (send_sem, recv_sem, own_sem), got = scratch, o_ref
    me = lax.axis_index(axis)
    fixed = lax.axis_index(other)
    pos = (me // stride) % size
    base = me - pos * stride

    def where(peer_pos):
        peer = base + peer_pos * stride
        return (peer, fixed) if axis == "cuts" else (fixed, peer)

    def part(peer_pos):
        return x_ref if whole else x_ref.at[peer_pos]

    barrier = pltpu.get_barrier_semaphore()
    for d in range(1, size):
        pl.semaphore_signal(
            barrier, inc=1, device_id=where((pos + d) % size), device_id_type=MESH
        )
    pl.semaphore_wait(barrier, size - 1)
    own = pltpu.make_async_copy(part(pos), got.at[pos], own_sem)
    own.start()
    copies = []
    for d in range(1, size):
        peer_pos = (pos + d) % size
        copy = pltpu.make_async_remote_copy(
            src_ref=part(peer_pos),
            dst_ref=got.at[pos],
            send_sem=send_sem.at[peer_pos],
            recv_sem=recv_sem.at[pos],
            device_id=where(peer_pos),
            device_id_type=MESH,
        )
        copy.start()
        copies.append(copy)
    for copy in copies:
        copy.wait_send()
    for d in range(1, size):
        source = (pos + size - d) % size
        pltpu.make_async_remote_copy(
            src_ref=part(source),
            dst_ref=got.at[source],
            send_sem=send_sem.at[source],
            recv_sem=recv_sem.at[source],
            device_id=where(source),
            device_id_type=MESH,
        ).wait_recv()
    own.wait()
    if summed:
        total = got[0]
        for slot in range(1, size):
            total = total + got[slot]
        o_ref[...] = total


def exchange(x, axis, key, whole=False, size=None, stride=1, summed=False, space=None):
    other = "col" if axis == "cuts" else "cuts"
    size = size or lax.axis_size(axis)
    shape = (size, *x.shape) if whole else x.shape
    scratch = [
        pltpu.SemaphoreType.DMA((size,)),
        pltpu.SemaphoreType.DMA((size,)),
        pltpu.SemaphoreType.DMA,
    ]
    if summed:
        scratch.append(pltpu.VMEM(shape, x.dtype))
        shape = shape[1:]
    return pl.pallas_call(
        functools.partial(_exchange_kernel, axis, other, size, stride, whole, summed),
        out_shape=jax.ShapeDtypeStruct(shape, x.dtype),
        in_specs=[pl.BlockSpec(memory_space=pltpu.VMEM)],
        out_specs=pl.BlockSpec(memory_space=space or pltpu.VMEM),
        scratch_shapes=scratch,
        compiler_params=pltpu.CompilerParams(collective_id=key, has_side_effects=True),
    )(x)


def _halo_kernel(n, head_ref, tail_ref, below_ref, above_ref, send_sem, recv_sem):
    me = lax.axis_index("col")
    fixed = lax.axis_index("cuts")
    has_left = (me + n - 1) // n
    has_right = 1 - me // (n - 1)
    left, right = (fixed, me - has_left), (fixed, me + has_right)

    def to_left():
        return pltpu.make_async_remote_copy(
            src_ref=head_ref, dst_ref=above_ref, send_sem=send_sem.at[0],
            recv_sem=recv_sem.at[1], device_id=left, device_id_type=MESH,
        )

    def to_right():
        return pltpu.make_async_remote_copy(
            src_ref=tail_ref, dst_ref=below_ref, send_sem=send_sem.at[1],
            recv_sem=recv_sem.at[0], device_id=right, device_id_type=MESH,
        )

    barrier = pltpu.get_barrier_semaphore()

    @pl.when(me > 0)
    def _():
        pl.semaphore_signal(barrier, inc=1, device_id=left, device_id_type=MESH)

    @pl.when(me < n - 1)
    def _():
        pl.semaphore_signal(barrier, inc=1, device_id=right, device_id_type=MESH)

    pl.semaphore_wait(barrier, has_left + has_right)

    @pl.when(me == 0)
    def _():
        below_ref[...] = jnp.zeros_like(below_ref)

    @pl.when(me == n - 1)
    def _():
        above_ref[...] = jnp.zeros_like(above_ref)

    @pl.when(me > 0)
    def _():
        to_left().start()

    @pl.when(me < n - 1)
    def _():
        to_right().start()

    @pl.when(me > 0)
    def _():
        to_left().wait_send()
        pltpu.make_async_remote_copy(
            src_ref=tail_ref, dst_ref=below_ref, send_sem=send_sem.at[1],
            recv_sem=recv_sem.at[0], device_id=left, device_id_type=MESH,
        ).wait_recv()

    @pl.when(me < n - 1)
    def _():
        to_right().wait_send()
        pltpu.make_async_remote_copy(
            src_ref=head_ref, dst_ref=above_ref, send_sem=send_sem.at[0],
            recv_sem=recv_sem.at[1], device_id=right, device_id_type=MESH,
        ).wait_recv()


def with_halo(cells, width):
    n = lax.axis_size("col")
    head = lax.slice_in_dim(cells, 0, width, axis=1)
    tail = lax.slice_in_dim(cells, cells.shape[1] - width, cells.shape[1], axis=1)
    below, above = pl.pallas_call(
        functools.partial(_halo_kernel, n),
        out_shape=(jax.ShapeDtypeStruct(head.shape, head.dtype),) * 2,
        in_specs=[pl.BlockSpec(memory_space=pltpu.VMEM)] * 2,
        out_specs=(pl.BlockSpec(memory_space=pltpu.VMEM),) * 2,
        scratch_shapes=[pltpu.SemaphoreType.DMA((2,)), pltpu.SemaphoreType.DMA((2,))],
        compiler_params=pltpu.CompilerParams(collective_id=3, has_side_effects=True),
    )(head, tail)
    return jnp.concatenate([below, cells, above], axis=1)


def _scatter_halo_kernel(size, stride, n, width, x_ref, o_ref, below_ref, above_ref,
                         got, head_buf, tail_buf, send_sem, recv_sem, own_sem, hsend, hrecv,
                         pair_got, pair_buf, pair_sem):
    me = lax.axis_index("cuts")
    cm = lax.axis_index("col")
    pos = (me // stride) % size
    base = me - pos * stride
    core = me % stride
    partner = me + 1 - 2 * core
    has_left = (cm + n - 1) // n
    has_right = 1 - cm // (n - 1)
    left, right = (me, cm - has_left), (me, cm + has_right)

    def where(peer_pos):
        return (base + peer_pos * stride, cm)

    barrier = pltpu.get_barrier_semaphore()
    for d in range(1, size):
        pl.semaphore_signal(
            barrier, inc=1, device_id=where((pos + d) % size), device_id_type=MESH
        )

    @pl.when(cm > 0)
    def _():
        pl.semaphore_signal(barrier, inc=1, device_id=left, device_id_type=MESH)

    @pl.when(cm < n - 1)
    def _():
        pl.semaphore_signal(barrier, inc=1, device_id=right, device_id_type=MESH)

    pl.semaphore_signal(barrier, inc=1, device_id=(partner, cm), device_id_type=MESH)
    pl.semaphore_wait(barrier, size + has_left + has_right)

    pair = pltpu.make_async_remote_copy(
        src_ref=x_ref.at[1 - core], dst_ref=pair_got, send_sem=pair_sem.at[0],
        recv_sem=pair_sem.at[1], device_id=(partner, cm), device_id_type=MESH,
    )
    pair.start()
    pair.wait_send()
    pair.wait_recv()
    pair_buf[...] = x_ref[core] + pair_got[...]

    @pl.when(cm == 0)
    def _():
        below_ref[...] = jnp.zeros_like(below_ref)

    @pl.when(cm == n - 1)
    def _():
        above_ref[...] = jnp.zeros_like(above_ref)

    own = pltpu.make_async_copy(pair_buf.at[pos], got.at[pos], own_sem)
    own.start()
    copies = []
    for d in range(1, size):
        peer_pos = (pos + d) % size
        copy = pltpu.make_async_remote_copy(
            src_ref=pair_buf.at[peer_pos], dst_ref=got.at[pos],
            send_sem=send_sem.at[peer_pos], recv_sem=recv_sem.at[pos],
            device_id=where(peer_pos), device_id_type=MESH,
        )
        copy.start()
        copies.append(copy)
    for copy in copies:
        copy.wait_send()
    for d in range(1, size):
        source = (pos + size - d) % size
        pltpu.make_async_remote_copy(
            src_ref=pair_buf.at[source], dst_ref=got.at[source],
            send_sem=send_sem.at[source], recv_sem=recv_sem.at[source],
            device_id=where(source), device_id_type=MESH,
        ).wait_recv()
    own.wait()
    total = got[0]
    for slot in range(1, size):
        total = total + got[slot]
    o_ref[...] = total
    planes = total.shape[1]
    head_buf[...] = total[:, :width]
    tail_buf[...] = total[:, planes - width :]

    def to_left():
        return pltpu.make_async_remote_copy(
            src_ref=head_buf, dst_ref=above_ref, send_sem=hsend.at[0],
            recv_sem=hrecv.at[1], device_id=left, device_id_type=MESH,
        )

    def to_right():
        return pltpu.make_async_remote_copy(
            src_ref=tail_buf, dst_ref=below_ref, send_sem=hsend.at[1],
            recv_sem=hrecv.at[0], device_id=right, device_id_type=MESH,
        )

    @pl.when(cm > 0)
    def _():
        to_left().start()

    @pl.when(cm < n - 1)
    def _():
        to_right().start()

    @pl.when(cm > 0)
    def _():
        to_left().wait_send()
        pltpu.make_async_remote_copy(
            src_ref=tail_buf, dst_ref=below_ref, send_sem=hsend.at[1],
            recv_sem=hrecv.at[0], device_id=left, device_id_type=MESH,
        ).wait_recv()

    @pl.when(cm < n - 1)
    def _():
        to_right().wait_send()
        pltpu.make_async_remote_copy(
            src_ref=head_buf, dst_ref=above_ref, send_sem=hsend.at[0],
            recv_sem=hrecv.at[1], device_id=right, device_id_type=MESH,
        ).wait_recv()


def scatter_with_halo(x, size, stride, width):
    n = lax.axis_size("col")
    block = x.shape[2:]
    halo = (block[0], width, *block[2:])
    vmem = pl.BlockSpec(memory_space=pltpu.VMEM)
    portion, below, above = pl.pallas_call(
        functools.partial(_scatter_halo_kernel, size, stride, n, width),
        out_shape=(
            jax.ShapeDtypeStruct(block, x.dtype),
            jax.ShapeDtypeStruct(halo, x.dtype),
            jax.ShapeDtypeStruct(halo, x.dtype),
        ),
        in_specs=[vmem],
        out_specs=(vmem, vmem, vmem),
        scratch_shapes=[
            pltpu.VMEM(x.shape[1:], x.dtype),
            pltpu.VMEM(halo, x.dtype),
            pltpu.VMEM(halo, x.dtype),
            pltpu.SemaphoreType.DMA((size,)),
            pltpu.SemaphoreType.DMA((size,)),
            pltpu.SemaphoreType.DMA,
            pltpu.SemaphoreType.DMA((2,)),
            pltpu.SemaphoreType.DMA((2,)),
            pltpu.VMEM(x.shape[1:], x.dtype),
            pltpu.VMEM(x.shape[1:], x.dtype),
            pltpu.SemaphoreType.DMA((2,)),
        ],
        compiler_params=pltpu.CompilerParams(collective_id=4, has_side_effects=True),
    )(x)
    return portion, jnp.concatenate([below, portion, above], axis=1)


def _gather_kernel(size, stride, x_ref, o_ref, got, send_sem, recv_sem, own_sem, pair_sem):
    me = lax.axis_index("cuts")
    cm = lax.axis_index("col")
    pos = (me // stride) % size
    base = me - pos * stride
    core = me % stride
    partner = me + 1 - 2 * core

    def where(peer_pos):
        return (base + peer_pos * stride, cm)

    barrier = pltpu.get_barrier_semaphore()
    for d in range(1, size):
        pl.semaphore_signal(
            barrier, inc=1, device_id=where((pos + d) % size), device_id_type=MESH
        )
    pl.semaphore_signal(barrier, inc=1, device_id=(partner, cm), device_id_type=MESH)
    pl.semaphore_wait(barrier, size)
    own = pltpu.make_async_copy(x_ref, got.at[pos], own_sem.at[0])
    own.start()
    copies = []
    for d in range(1, size):
        peer_pos = (pos + d) % size
        copy = pltpu.make_async_remote_copy(
            src_ref=x_ref, dst_ref=got.at[pos],
            send_sem=send_sem.at[peer_pos], recv_sem=recv_sem.at[pos],
            device_id=where(peer_pos), device_id_type=MESH,
        )
        copy.start()
        copies.append(copy)
    for copy in copies:
        copy.wait_send()
    for d in range(1, size):
        source = (pos + size - d) % size
        pltpu.make_async_remote_copy(
            src_ref=x_ref, dst_ref=got.at[source],
            send_sem=send_sem.at[source], recv_sem=recv_sem.at[source],
            device_id=where(source), device_id_type=MESH,
        ).wait_recv()
    own.wait()
    mine = pltpu.make_async_copy(got, o_ref.at[core], own_sem.at[1])
    mine.start()
    pair = pltpu.make_async_remote_copy(
        src_ref=got, dst_ref=o_ref.at[core], send_sem=pair_sem.at[0],
        recv_sem=pair_sem.at[1], device_id=(partner, cm), device_id_type=MESH,
    )
    pair.start()
    pair.wait_send()
    pltpu.make_async_remote_copy(
        src_ref=got, dst_ref=o_ref.at[1 - core], send_sem=pair_sem.at[0],
        recv_sem=pair_sem.at[1], device_id=(partner, cm), device_id_type=MESH,
    ).wait_recv()
    mine.wait()


def gather_in_two(x, size, stride):
    return pl.pallas_call(
        functools.partial(_gather_kernel, size, stride),
        out_shape=jax.ShapeDtypeStruct((stride, size, *x.shape), x.dtype),
        in_specs=[pl.BlockSpec(memory_space=pltpu.VMEM)],
        out_specs=pl.BlockSpec(memory_space=pl.ANY),
        scratch_shapes=[
            pltpu.VMEM((size, *x.shape), x.dtype),
            pltpu.SemaphoreType.DMA((size,)),
            pltpu.SemaphoreType.DMA((size,)),
            pltpu.SemaphoreType.DMA((2,)),
            pltpu.SemaphoreType.DMA((2,)),
        ],
        compiler_params=pltpu.CompilerParams(collective_id=1, has_side_effects=True),
    )(x)


def _split_sum_kernel(n, rows, x_ref, o_ref, other_ref, got, half_buf, send_sem, recv_sem,
                      own_sem, pair_sem):
    me = lax.axis_index("col")
    cuts = lax.axis_index("cuts")
    partner = cuts + 1 - 2 * (cuts % 2)

    def where(peer):
        return (cuts, peer)

    barrier = pltpu.get_barrier_semaphore()
    for d in range(1, n):
        pl.semaphore_signal(barrier, inc=1, device_id=where((me + d) % n), device_id_type=MESH)
    pl.semaphore_signal(barrier, inc=1, device_id=(partner, me), device_id_type=MESH)
    pl.semaphore_wait(barrier, n)
    own = pltpu.make_async_copy(x_ref, got.at[me], own_sem)
    own.start()
    copies = []
    for d in range(1, n):
        peer = (me + d) % n
        copy = pltpu.make_async_remote_copy(
            src_ref=x_ref, dst_ref=got.at[me], send_sem=send_sem.at[peer],
            recv_sem=recv_sem.at[me], device_id=where(peer), device_id_type=MESH,
        )
        copy.start()
        copies.append(copy)
    for copy in copies:
        copy.wait_send()
    for d in range(1, n):
        source = (me + n - d) % n
        pltpu.make_async_remote_copy(
            src_ref=x_ref, dst_ref=got.at[source], send_sem=send_sem.at[source],
            recv_sem=recv_sem.at[source], device_id=where(source), device_id_type=MESH,
        ).wait_recv()
    own.wait()
    total = got[0]
    for slot in range(1, n):
        total = total + got[slot]
    o_ref[...] = total
    half_buf[...] = total[:rows]
    pair = pltpu.make_async_remote_copy(
        src_ref=half_buf, dst_ref=other_ref, send_sem=pair_sem.at[0],
        recv_sem=pair_sem.at[1], device_id=(partner, me), device_id_type=MESH,
    )
    pair.start()
    pair.wait_send()
    pair.wait_recv()


def split_total(line, targets):
    n = lax.axis_size("col")
    lanes = 128
    rows = -(-line.size // (2 * lanes))
    core = lax.axis_index("cuts") % 2
    halves = jnp.pad(line, (0, 2 * rows * lanes - line.size)).reshape(2, rows, lanes)
    tail = jnp.pad(targets.reshape(-1), (0, lanes - targets.size)).reshape(1, lanes)
    block = jnp.concatenate([lax.dynamic_index_in_dim(halves, core, 0, False), tail], axis=0)
    vmem = pl.BlockSpec(memory_space=pltpu.VMEM)
    total, other = pl.pallas_call(
        functools.partial(_split_sum_kernel, n, rows),
        out_shape=(
            jax.ShapeDtypeStruct(block.shape, block.dtype),
            jax.ShapeDtypeStruct((rows, lanes), block.dtype),
        ),
        in_specs=[vmem],
        out_specs=(vmem, vmem),
        scratch_shapes=[
            pltpu.VMEM((n, *block.shape), block.dtype),
            pltpu.VMEM((rows, lanes), block.dtype),
            pltpu.SemaphoreType.DMA((n,)),
            pltpu.SemaphoreType.DMA((n,)),
            pltpu.SemaphoreType.DMA,
            pltpu.SemaphoreType.DMA((2,)),
        ],
        compiler_params=pltpu.CompilerParams(collective_id=2, has_side_effects=True),
    )(block)
    mine = total[:rows]
    first = jnp.where(core == 0, mine, other)
    second = jnp.where(core == 0, other, mine)
    whole = jnp.concatenate([first, second], axis=0).reshape(-1)[: line.size]
    return whole, total[rows, : targets.size].reshape(targets.shape)


def split_up(shard, dim, devices):
    before, after = (shard.shape[:dim], shard.shape[dim + 1 :])
    return jnp.moveaxis(shard.reshape(*before, devices, -1, *after), dim, 0)


def sent_and_summed(shard, axis, dim):
    tiles = split_up(shard, dim, lax.axis_size(axis))
    arrived = exchange(tiles, axis, 0)
    return arrived.sum(axis=0)


def joined_along(tiles, dim):
    dims = list(tiles.shape[1:])
    dims[dim] *= tiles.shape[0]
    return jnp.moveaxis(tiles, 0, dim).reshape(dims)


def from_everyone(shard, axis):
    return exchange(shard, axis, 1 if axis == "cuts" else 2, whole=True)


def gather_directly(shard, axis, dim):
    return joined_along(from_everyone(shard, axis), dim)


def taken_together(shard, axis):
    return from_everyone(shard, axis).sum(axis=0)


def packed_total(arrays, axis):
    line, at, done = (jnp.concatenate([a.reshape(-1) for a in arrays]), 0, [])
    lanes = 128
    rows = -(-line.size // lanes)
    block = jnp.pad(line, (0, rows * lanes - line.size)).reshape(rows, lanes)
    running = taken_together(block, axis).reshape(-1)
    for a in arrays:
        done.append(running[at : at + a.size].reshape(a.shape))
        at += a.size
    return tuple(done)


def operate(extended):
    channels, depth, cells = extended.shape
    edge = GRID
    interior = extended[:, 1:-1]
    column = jnp.arange(cells, dtype=jnp.int32) % edge
    has_left = (column > 0).astype(jnp.float32)
    has_right = (column < edge - 1).astype(jnp.float32)
    left_part = jnp.pad(interior, ((0, 0), (0, 0), (1, 0)))[:, :, :-1] * has_left
    right_part = jnp.pad(interior, ((0, 0), (0, 0), (0, 1)))[:, :, 1:] * has_right
    upper_part = jnp.pad(interior, ((0, 0), (0, 0), (edge, 0)))[:, :, :-edge]
    lower_part = jnp.pad(interior, ((0, 0), (0, 0), (0, edge)))[:, :, edge:]
    neighbours = extended[:, 2:] + extended[:, :-2]
    neighbours = neighbours + left_part + right_part + upper_part + lower_part
    return interior + strength * (6.0 * interior - neighbours)


def smooth_once(source, extended):
    planes = source.shape[1]
    first_plane = lax.axis_index("col") * planes - ITERS
    total_planes = planes * lax.axis_size("col")
    levels = first_plane + jnp.arange(planes + 2 * ITERS, dtype=jnp.int32)
    inside = ((levels >= 0) & (levels < total_planes)).astype(jnp.float32)[None, :, None]
    solution = jnp.zeros_like(source)
    residual = extended
    direction = extended / centre
    ratio = spread / centre
    for iteration in range(ITERS):
        margin = ITERS - iteration
        solution = solution + direction[:, margin : margin + planes]
        window = inside[:, iteration + 1 : iteration + 1 + planes + 2 * (margin - 1)]
        residual = (residual[:, 1:-1] - operate(direction)) * window
        ratio_next = 1.0 / (2.0 * centre / spread - ratio)
        direction = ratio_next * ratio * direction[:, 1:-1] + 2.0 * ratio_next / spread * residual
        ratio = ratio_next
    return solution + direction


def _eliminate(m_ref, b_ref, o_ref):
    m = m_ref[...]
    b = b_ref[...]
    n = m.shape[0]
    ri = lax.broadcasted_iota(jnp.int32, m.shape, 0)
    ci = lax.broadcasted_iota(jnp.int32, m.shape, 1)
    rb = lax.broadcasted_iota(jnp.int32, b.shape, 0)

    def pick_row(x, rows, p):
        return jnp.sum(jnp.where(rows == p, x, 0.0), axis=0, keepdims=True)

    def pick_col(x, p):
        return jnp.sum(jnp.where(ci[: x.shape[0]] == p, x, 0.0), axis=1, keepdims=True)

    def step(j, carry):
        m, b = carry
        p, q = 2 * j, 2 * j + 1
        c0, c1 = pick_col(m, p), pick_col(m, q)
        r0, r1 = pick_row(m, ri, p), pick_row(m, ri, q)
        s0, s1 = pick_row(b, rb, p), pick_row(b, rb, q)
        a, e = pick_col(r0, p), pick_col(r0, q)
        c, d = pick_col(r1, p), pick_col(r1, q)
        scale = 1.0 / (a * d - e * c)
        n0, n1 = (d * r0 - e * r1) * scale, (a * r1 - c * r0) * scale
        t0, t1 = (d * s0 - e * s1) * scale, (a * s1 - c * s0) * scale
        m = jnp.where(ri == p, n0, jnp.where(ri == q, n1, m - c0 * n0 - c1 * n1))
        b = jnp.where(rb == p, t0, jnp.where(rb == q, t1, b - c0 * t0 - c1 * t1))
        return m, b

    x = lax.fori_loop(0, n // 2, step, (m, b), unroll=True)[1]
    if o_ref.shape == b.shape:
        o_ref[...] = x.astype(o_ref.dtype)
    else:
        o_ref[...] = jnp.sum(jnp.where(ri == ci, x, 0.0), axis=0, keepdims=True)


def spd_solve(m, b, dtype=None):
    shape = (1, b.shape[0]) if b.shape[1] == 1 else b.shape
    return pl.pallas_call(
        _eliminate, out_shape=jax.ShapeDtypeStruct(shape, dtype or b.dtype)
    )(m, b)


def per_device(data, weights, mixing):
    local_scans, ranks, planes, cells = data.shape
    mix_gram = jnp.dot(mixing.T, mixing, precision=highest)
    weight_gram = jnp.dot(weights.T, weights, precision=highest)
    own_weights = lax.dynamic_slice_in_dim(
        weights, lax.axis_index("cuts") * local_scans, local_scans, 0
    )
    scaled = (mixing.T[None, :, :] * own_weights[:, :, None]).transpose(1, 0, 2)
    coefficients = spd_solve(
        mix_gram * weight_gram, scaled.reshape(ranks, local_scans * ranks), jnp.bfloat16
    )
    partial = lax.dot_general(
        coefficients, data.reshape(-1, planes, cells), (((1,), (0,)), ((), ())), preferred_element_type=jnp.float32
    )
    cores = 2
    chips = lax.axis_size("cuts") // cores
    portion, extended = scatter_with_halo(
        partial.reshape(cores, chips, -1, planes, cells), chips, cores, ITERS
    )
    smoothed = smooth_once(portion, extended)
    factor = gather_in_two(smoothed, chips, cores)
    factor = factor.reshape(ranks, planes, cells)
    factor_half = factor.astype(jnp.bfloat16)
    factor_gram = lax.dot_general(
        factor, factor, (((1, 2), (1, 2)), ((), ())), precision=lax.Precision.HIGH
    )
    products = lax.dot_general(
        data, factor_half, (((2, 3), (1, 2)), ((), ())), preferred_element_type=jnp.float32
    )
    targets = jnp.sum(mixing[None, :, :] * products, axis=1)
    half = ranks // 2
    row = lax.broadcasted_iota(jnp.int32, (half, half), 0)
    col = lax.broadcasted_iota(jnp.int32, (half, half), 1)
    top, off, low = (factor_gram[:half, :half], factor_gram[:half, half:], factor_gram[half:, half:])
    folded = jnp.where(row >= col, top, low)
    low_diag = jnp.sum(jnp.where(row == col, low, 0.0), axis=1)
    line, targets = split_total(
        jnp.concatenate([folded.reshape(-1), off.reshape(-1), low_diag]), targets
    )
    folded = line[: half * half].reshape(half, half)
    off = line[half * half : 2 * half * half].reshape(half, half)
    low_diag = line[2 * half * half :]
    top = jnp.where(row >= col, folded, folded.T)
    low = jnp.where(row < col, folded, jnp.where(row > col, folded.T, low_diag[:, None]))
    factor_gram = jnp.concatenate(
        [jnp.concatenate([top, off], axis=1), jnp.concatenate([off.T, low], axis=1)], axis=0
    )
    updated = spd_solve(mix_gram * factor_gram, targets.T)
    return (factor, updated)


def solution(mesh):
    return jax.shard_map(
        per_device,
        mesh=mesh,
        in_specs=(P("cuts", None, "col", None), P(), P()),
        out_specs=(P(None, "col", None), P("cuts", None)),
        check_vma=False,
    )
```

```python
import functools
import jax
import jax.numpy as jnp
from jax import lax
from jax.sharding import PartitionSpec as P
from jax.experimental import pallas as pl
from jax.experimental.pallas import tpu as pltpu

MESH = pl.DeviceIdType.MESH

GRID = 32
ITERS = 3


strength = 0.5
highest = lax.Precision.HIGHEST
low_edge = 1.0
high_edge = 1.0 + 12.0 * strength
centre = (high_edge + low_edge) / 2.0
spread = (high_edge - low_edge) / 2.0


def extended_2(cells, sides, width):
    for axis, dim in sides:
        count = lax.axis_size(axis)
        ends = count - 1
        head = lax.slice_in_dim(cells, 0, width, axis=dim)
        tail = lax.slice_in_dim(cells, cells.shape[dim] - width, cells.shape[dim], axis=dim)
        cells = jnp.concatenate(
            [
                lax.ppermute(tail, axis, [(i, (i + 1) % count) for i in range(ends)]),
                cells,
                lax.ppermute(head, axis, [((i + 1) % count, i) for i in range(ends)]),
            ],
            axis=dim,
        )
    return cells


def _exchange_kernel(axis, other, size, stride, whole, summed, x_ref, o_ref, *scratch):
    if summed:
        send_sem, recv_sem, own_sem, got = scratch
    else:
        (send_sem, recv_sem, own_sem), got = scratch, o_ref
    me = lax.axis_index(axis)
    fixed = lax.axis_index(other)
    pos = (me // stride) % size
    base = me - pos * stride

    def where(peer_pos):
        peer = base + peer_pos * stride
        return (peer, fixed) if axis == "cuts" else (fixed, peer)

    def part(peer_pos):
        return x_ref if whole else x_ref.at[peer_pos]

    if axis == "col" and size == 16:
        hops = lambda z, x: 2 * min(z, 4 - z) + min(x, 4 - x)
        order = sorted(((z, x) for z in range(4) for x in range(4) if z or x),
                       key=lambda o: -hops(*o))
        peers = [((pos // 4 + z) % 4) * 4 + (pos % 4 + x) % 4 for z, x in order]
    else:
        peers = [(pos + d) % size for d in range(1, size)]
    barrier = pltpu.get_barrier_semaphore()
    for peer_pos in peers:
        pl.semaphore_signal(barrier, inc=1, device_id=where(peer_pos), device_id_type=MESH)
    pl.semaphore_wait(barrier, size - 1)
    own = pltpu.make_async_copy(part(pos), got.at[pos], own_sem)
    own.start()
    copies = []
    for peer_pos in peers:
        copy = pltpu.make_async_remote_copy(
            src_ref=part(peer_pos),
            dst_ref=got.at[pos],
            send_sem=send_sem.at[peer_pos],
            recv_sem=recv_sem.at[pos],
            device_id=where(peer_pos),
            device_id_type=MESH,
        )
        copy.start()
        copies.append(copy)
    for copy in copies:
        copy.wait_send()
    for d in range(1, size):
        source = (pos + size - d) % size
        pltpu.make_async_remote_copy(
            src_ref=part(source),
            dst_ref=got.at[source],
            send_sem=send_sem.at[source],
            recv_sem=recv_sem.at[source],
            device_id=where(source),
            device_id_type=MESH,
        ).wait_recv()
    own.wait()
    if summed:
        total = got[0]
        for slot in range(1, size):
            total = total + got[slot]
        o_ref[...] = total


def exchange(x, axis, key, whole=False, size=None, stride=1, summed=False, space=None):
    other = "col" if axis == "cuts" else "cuts"
    size = size or lax.axis_size(axis)
    shape = (size, *x.shape) if whole else x.shape
    scratch = [
        pltpu.SemaphoreType.DMA((size,)),
        pltpu.SemaphoreType.DMA((size,)),
        pltpu.SemaphoreType.DMA,
    ]
    if summed:
        scratch.append(pltpu.VMEM(shape, x.dtype))
        shape = shape[1:]
    return pl.pallas_call(
        functools.partial(_exchange_kernel, axis, other, size, stride, whole, summed),
        out_shape=jax.ShapeDtypeStruct(shape, x.dtype),
        in_specs=[pl.BlockSpec(memory_space=pltpu.VMEM)],
        out_specs=pl.BlockSpec(memory_space=space or pltpu.VMEM),
        scratch_shapes=scratch,
        compiler_params=pltpu.CompilerParams(collective_id=key, has_side_effects=True),
    )(x)


def _halo_kernel(n, head_ref, tail_ref, below_ref, above_ref, send_sem, recv_sem):
    me = lax.axis_index("col")
    fixed = lax.axis_index("cuts")
    has_left = (me + n - 1) // n
    has_right = 1 - me // (n - 1)
    left, right = (fixed, me - has_left), (fixed, me + has_right)

    def to_left():
        return pltpu.make_async_remote_copy(
            src_ref=head_ref, dst_ref=above_ref, send_sem=send_sem.at[0],
            recv_sem=recv_sem.at[1], device_id=left, device_id_type=MESH,
        )

    def to_right():
        return pltpu.make_async_remote_copy(
            src_ref=tail_ref, dst_ref=below_ref, send_sem=send_sem.at[1],
            recv_sem=recv_sem.at[0], device_id=right, device_id_type=MESH,
        )

    barrier = pltpu.get_barrier_semaphore()

    @pl.when(me > 0)
    def _():
        pl.semaphore_signal(barrier, inc=1, device_id=left, device_id_type=MESH)

    @pl.when(me < n - 1)
    def _():
        pl.semaphore_signal(barrier, inc=1, device_id=right, device_id_type=MESH)

    pl.semaphore_wait(barrier, has_left + has_right)

    @pl.when(me == 0)
    def _():
        below_ref[...] = jnp.zeros_like(below_ref)

    @pl.when(me == n - 1)
    def _():
        above_ref[...] = jnp.zeros_like(above_ref)

    @pl.when(me > 0)
    def _():
        to_left().start()

    @pl.when(me < n - 1)
    def _():
        to_right().start()

    @pl.when(me > 0)
    def _():
        to_left().wait_send()
        pltpu.make_async_remote_copy(
            src_ref=tail_ref, dst_ref=below_ref, send_sem=send_sem.at[1],
            recv_sem=recv_sem.at[0], device_id=left, device_id_type=MESH,
        ).wait_recv()

    @pl.when(me < n - 1)
    def _():
        to_right().wait_send()
        pltpu.make_async_remote_copy(
            src_ref=head_ref, dst_ref=above_ref, send_sem=send_sem.at[0],
            recv_sem=recv_sem.at[1], device_id=right, device_id_type=MESH,
        ).wait_recv()


def with_halo(cells, width):
    n = lax.axis_size("col")
    head = lax.slice_in_dim(cells, 0, width, axis=1)
    tail = lax.slice_in_dim(cells, cells.shape[1] - width, cells.shape[1], axis=1)
    below, above = pl.pallas_call(
        functools.partial(_halo_kernel, n),
        out_shape=(jax.ShapeDtypeStruct(head.shape, head.dtype),) * 2,
        in_specs=[pl.BlockSpec(memory_space=pltpu.VMEM)] * 2,
        out_specs=(pl.BlockSpec(memory_space=pltpu.VMEM),) * 2,
        scratch_shapes=[pltpu.SemaphoreType.DMA((2,)), pltpu.SemaphoreType.DMA((2,))],
        compiler_params=pltpu.CompilerParams(collective_id=3, has_side_effects=True),
    )(head, tail)
    return jnp.concatenate([below, cells, above], axis=1)


def _scatter_halo_kernel(size, stride, n, width, x_ref, o_ref, below_ref, above_ref,
                         got, head_buf, tail_buf, send_sem, recv_sem, own_sem, hsend, hrecv,
                         pair_got, pair_buf, pair_sem):
    me = lax.axis_index("cuts")
    cm = lax.axis_index("col")
    pos = (me // stride) % size
    base = me - pos * stride
    core = me % stride
    partner = me + 1 - 2 * core
    has_left = (cm + n - 1) // n
    has_right = 1 - cm // (n - 1)
    left, right = (me, cm - has_left), (me, cm + has_right)

    def where(peer_pos):
        return (base + peer_pos * stride, cm)

    barrier = pltpu.get_barrier_semaphore()
    for d in range(1, size):
        pl.semaphore_signal(
            barrier, inc=1, device_id=where((pos + d) % size), device_id_type=MESH
        )

    @pl.when(cm > 0)
    def _():
        pl.semaphore_signal(barrier, inc=1, device_id=left, device_id_type=MESH)

    @pl.when(cm < n - 1)
    def _():
        pl.semaphore_signal(barrier, inc=1, device_id=right, device_id_type=MESH)

    pl.semaphore_signal(barrier, inc=1, device_id=(partner, cm), device_id_type=MESH)
    pl.semaphore_wait(barrier, size + has_left + has_right)

    pair = pltpu.make_async_remote_copy(
        src_ref=x_ref.at[1 - core], dst_ref=pair_got, send_sem=pair_sem.at[0],
        recv_sem=pair_sem.at[1], device_id=(partner, cm), device_id_type=MESH,
    )
    pair.start()
    pair.wait_send()
    pair.wait_recv()
    pair_buf[...] = x_ref[core] + pair_got[...]

    @pl.when(cm == 0)
    def _():
        below_ref[...] = jnp.zeros_like(below_ref)

    @pl.when(cm == n - 1)
    def _():
        above_ref[...] = jnp.zeros_like(above_ref)

    own = pltpu.make_async_copy(pair_buf.at[pos], got.at[pos], own_sem)
    own.start()
    copies = []
    for d in range(1, size):
        peer_pos = (pos + d) % size
        copy = pltpu.make_async_remote_copy(
            src_ref=pair_buf.at[peer_pos], dst_ref=got.at[pos],
            send_sem=send_sem.at[peer_pos], recv_sem=recv_sem.at[pos],
            device_id=where(peer_pos), device_id_type=MESH,
        )
        copy.start()
        copies.append(copy)
    for copy in copies:
        copy.wait_send()
    for d in range(1, size):
        source = (pos + size - d) % size
        pltpu.make_async_remote_copy(
            src_ref=pair_buf.at[source], dst_ref=got.at[source],
            send_sem=send_sem.at[source], recv_sem=recv_sem.at[source],
            device_id=where(source), device_id_type=MESH,
        ).wait_recv()
    own.wait()
    total = got[0]
    for slot in range(1, size):
        total = total + got[slot]
    o_ref[...] = total
    planes = total.shape[1]
    head_buf[...] = total[:, :width]
    tail_buf[...] = total[:, planes - width :]

    def to_left():
        return pltpu.make_async_remote_copy(
            src_ref=head_buf, dst_ref=above_ref, send_sem=hsend.at[0],
            recv_sem=hrecv.at[1], device_id=left, device_id_type=MESH,
        )

    def to_right():
        return pltpu.make_async_remote_copy(
            src_ref=tail_buf, dst_ref=below_ref, send_sem=hsend.at[1],
            recv_sem=hrecv.at[0], device_id=right, device_id_type=MESH,
        )

    @pl.when(cm > 0)
    def _():
        to_left().start()

    @pl.when(cm < n - 1)
    def _():
        to_right().start()

    @pl.when(cm > 0)
    def _():
        to_left().wait_send()
        pltpu.make_async_remote_copy(
            src_ref=tail_buf, dst_ref=below_ref, send_sem=hsend.at[1],
            recv_sem=hrecv.at[0], device_id=left, device_id_type=MESH,
        ).wait_recv()

    @pl.when(cm < n - 1)
    def _():
        to_right().wait_send()
        pltpu.make_async_remote_copy(
            src_ref=head_buf, dst_ref=above_ref, send_sem=hsend.at[0],
            recv_sem=hrecv.at[1], device_id=right, device_id_type=MESH,
        ).wait_recv()


def scatter_with_halo(x, size, stride, width):
    n = lax.axis_size("col")
    block = x.shape[2:]
    halo = (block[0], width, *block[2:])
    vmem = pl.BlockSpec(memory_space=pltpu.VMEM)
    portion, below, above = pl.pallas_call(
        functools.partial(_scatter_halo_kernel, size, stride, n, width),
        out_shape=(
            jax.ShapeDtypeStruct(block, x.dtype),
            jax.ShapeDtypeStruct(halo, x.dtype),
            jax.ShapeDtypeStruct(halo, x.dtype),
        ),
        in_specs=[vmem],
        out_specs=(vmem, vmem, vmem),
        scratch_shapes=[
            pltpu.VMEM(x.shape[1:], x.dtype),
            pltpu.VMEM(halo, x.dtype),
            pltpu.VMEM(halo, x.dtype),
            pltpu.SemaphoreType.DMA((size,)),
            pltpu.SemaphoreType.DMA((size,)),
            pltpu.SemaphoreType.DMA,
            pltpu.SemaphoreType.DMA((2,)),
            pltpu.SemaphoreType.DMA((2,)),
            pltpu.VMEM(x.shape[1:], x.dtype),
            pltpu.VMEM(x.shape[1:], x.dtype),
            pltpu.SemaphoreType.DMA((2,)),
        ],
        compiler_params=pltpu.CompilerParams(collective_id=4, has_side_effects=True),
    )(x)
    return portion, jnp.concatenate([below, portion, above], axis=1)


def _gather_kernel(size, stride, x_ref, o_ref, got, send_sem, recv_sem, own_sem, pair_sem):
    me = lax.axis_index("cuts")
    cm = lax.axis_index("col")
    pos = (me // stride) % size
    base = me - pos * stride
    core = me % stride
    partner = me + 1 - 2 * core

    def where(peer_pos):
        return (base + peer_pos * stride, cm)

    barrier = pltpu.get_barrier_semaphore()
    for d in range(1, size):
        pl.semaphore_signal(
            barrier, inc=1, device_id=where((pos + d) % size), device_id_type=MESH
        )
    pl.semaphore_signal(barrier, inc=1, device_id=(partner, cm), device_id_type=MESH)
    pl.semaphore_wait(barrier, size)
    own = pltpu.make_async_copy(x_ref, got.at[pos], own_sem.at[0])
    own.start()
    copies = []
    for d in range(1, size):
        peer_pos = (pos + d) % size
        copy = pltpu.make_async_remote_copy(
            src_ref=x_ref, dst_ref=got.at[pos],
            send_sem=send_sem.at[peer_pos], recv_sem=recv_sem.at[pos],
            device_id=where(peer_pos), device_id_type=MESH,
        )
        copy.start()
        copies.append(copy)
    for copy in copies:
        copy.wait_send()
    for d in range(1, size):
        source = (pos + size - d) % size
        pltpu.make_async_remote_copy(
            src_ref=x_ref, dst_ref=got.at[source],
            send_sem=send_sem.at[source], recv_sem=recv_sem.at[source],
            device_id=where(source), device_id_type=MESH,
        ).wait_recv()
    own.wait()
    mine = pltpu.make_async_copy(got, o_ref.at[core], own_sem.at[1])
    mine.start()
    pair = pltpu.make_async_remote_copy(
        src_ref=got, dst_ref=o_ref.at[core], send_sem=pair_sem.at[0],
        recv_sem=pair_sem.at[1], device_id=(partner, cm), device_id_type=MESH,
    )
    pair.start()
    pair.wait_send()
    pltpu.make_async_remote_copy(
        src_ref=got, dst_ref=o_ref.at[1 - core], send_sem=pair_sem.at[0],
        recv_sem=pair_sem.at[1], device_id=(partner, cm), device_id_type=MESH,
    ).wait_recv()
    mine.wait()


def gather_in_two(x, size, stride):
    return pl.pallas_call(
        functools.partial(_gather_kernel, size, stride),
        out_shape=jax.ShapeDtypeStruct((stride, size, *x.shape), x.dtype),
        in_specs=[pl.BlockSpec(memory_space=pltpu.VMEM)],
        out_specs=pl.BlockSpec(memory_space=pl.ANY),
        scratch_shapes=[
            pltpu.VMEM((size, *x.shape), x.dtype),
            pltpu.SemaphoreType.DMA((size,)),
            pltpu.SemaphoreType.DMA((size,)),
            pltpu.SemaphoreType.DMA((2,)),
            pltpu.SemaphoreType.DMA((2,)),
        ],
        compiler_params=pltpu.CompilerParams(collective_id=1, has_side_effects=True),
    )(x)


def split_up(shard, dim, devices):
    before, after = (shard.shape[:dim], shard.shape[dim + 1 :])
    return jnp.moveaxis(shard.reshape(*before, devices, -1, *after), dim, 0)


def sent_and_summed(shard, axis, dim):
    tiles = split_up(shard, dim, lax.axis_size(axis))
    arrived = exchange(tiles, axis, 0)
    return arrived.sum(axis=0)


def joined_along(tiles, dim):
    dims = list(tiles.shape[1:])
    dims[dim] *= tiles.shape[0]
    return jnp.moveaxis(tiles, 0, dim).reshape(dims)


def from_everyone(shard, axis):
    return exchange(shard, axis, 1 if axis == "cuts" else 2, whole=True)


def gather_directly(shard, axis, dim):
    return joined_along(from_everyone(shard, axis), dim)


def taken_together(shard, axis):
    return from_everyone(shard, axis).sum(axis=0)


def packed_total(arrays, axis):
    line, at, done = (jnp.concatenate([a.reshape(-1) for a in arrays]), 0, [])
    lanes = 128
    rows = -(-line.size // lanes)
    block = jnp.pad(line, (0, rows * lanes - line.size)).reshape(rows, lanes)
    running = taken_together(block, axis).reshape(-1)
    for a in arrays:
        done.append(running[at : at + a.size].reshape(a.shape))
        at += a.size
    return tuple(done)


def operate(extended):
    channels, depth, cells = extended.shape
    edge = GRID
    interior = extended[:, 1:-1]
    column = jnp.arange(cells, dtype=jnp.int32) % edge
    has_left = (column > 0).astype(jnp.float32)
    has_right = (column < edge - 1).astype(jnp.float32)
    left_part = jnp.pad(interior, ((0, 0), (0, 0), (1, 0)))[:, :, :-1] * has_left
    right_part = jnp.pad(interior, ((0, 0), (0, 0), (0, 1)))[:, :, 1:] * has_right
    upper_part = jnp.pad(interior, ((0, 0), (0, 0), (edge, 0)))[:, :, :-edge]
    lower_part = jnp.pad(interior, ((0, 0), (0, 0), (0, edge)))[:, :, edge:]
    neighbours = extended[:, 2:] + extended[:, :-2]
    neighbours = neighbours + left_part + right_part + upper_part + lower_part
    return interior + strength * (6.0 * interior - neighbours)


def smooth_once(source, extended):
    planes = source.shape[1]
    first_plane = lax.axis_index("col") * planes - ITERS
    total_planes = planes * lax.axis_size("col")
    levels = first_plane + jnp.arange(planes + 2 * ITERS, dtype=jnp.int32)
    inside = ((levels >= 0) & (levels < total_planes)).astype(jnp.float32)[None, :, None]
    solution = jnp.zeros_like(source)
    residual = extended
    direction = extended / centre
    ratio = spread / centre
    for iteration in range(ITERS):
        margin = ITERS - iteration
        solution = solution + direction[:, margin : margin + planes]
        window = inside[:, iteration + 1 : iteration + 1 + planes + 2 * (margin - 1)]
        residual = (residual[:, 1:-1] - operate(direction)) * window
        ratio_next = 1.0 / (2.0 * centre / spread - ratio)
        direction = ratio_next * ratio * direction[:, 1:-1] + 2.0 * ratio_next / spread * residual
        ratio = ratio_next
    return solution + direction


def _eliminate(m_ref, b_ref, o_ref):
    m = m_ref[...]
    b = b_ref[...]
    n = m.shape[0]
    ri = lax.broadcasted_iota(jnp.int32, m.shape, 0)
    ci = lax.broadcasted_iota(jnp.int32, m.shape, 1)
    rb = lax.broadcasted_iota(jnp.int32, b.shape, 0)

    def pick_row(x, rows, p):
        return jnp.sum(jnp.where(rows == p, x, 0.0), axis=0, keepdims=True)

    def pick_col(x, p):
        return jnp.sum(jnp.where(ci[: x.shape[0]] == p, x, 0.0), axis=1, keepdims=True)

    def step(j, carry):
        m, b = carry
        p, q = 2 * j, 2 * j + 1
        c0, c1 = pick_col(m, p), pick_col(m, q)
        r0, r1 = pick_row(m, ri, p), pick_row(m, ri, q)
        s0, s1 = pick_row(b, rb, p), pick_row(b, rb, q)
        a, e = pick_col(r0, p), pick_col(r0, q)
        c, d = pick_col(r1, p), pick_col(r1, q)
        scale = 1.0 / (a * d - e * c)
        n0, n1 = (d * r0 - e * r1) * scale, (a * r1 - c * r0) * scale
        t0, t1 = (d * s0 - e * s1) * scale, (a * s1 - c * s0) * scale
        m = jnp.where(ri == p, n0, jnp.where(ri == q, n1, m - c0 * n0 - c1 * n1))
        b = jnp.where(rb == p, t0, jnp.where(rb == q, t1, b - c0 * t0 - c1 * t1))
        return m, b

    x = lax.fori_loop(0, n // 2, step, (m, b), unroll=True)[1]
    if o_ref.shape == b.shape:
        o_ref[...] = x.astype(o_ref.dtype)
    else:
        o_ref[...] = jnp.sum(jnp.where(ri == ci, x, 0.0), axis=0, keepdims=True)


def spd_solve(m, b, dtype=None):
    shape = (1, b.shape[0]) if b.shape[1] == 1 else b.shape
    return pl.pallas_call(
        _eliminate, out_shape=jax.ShapeDtypeStruct(shape, dtype or b.dtype)
    )(m, b)


def per_device(data, weights, mixing):
    local_scans, ranks, planes, cells = data.shape
    mix_gram = jnp.dot(mixing.T, mixing, precision=highest)
    weight_gram = jnp.dot(weights.T, weights, precision=highest)
    own_weights = lax.dynamic_slice_in_dim(
        weights, lax.axis_index("cuts") * local_scans, local_scans, 0
    )
    scaled = (mixing.T[None, :, :] * own_weights[:, :, None]).transpose(1, 0, 2)
    coefficients = spd_solve(
        mix_gram * weight_gram, scaled.reshape(ranks, local_scans * ranks), jnp.bfloat16
    )
    partial = lax.dot_general(
        coefficients, data.reshape(-1, planes, cells), (((1,), (0,)), ((), ())), preferred_element_type=jnp.float32
    )
    cores = 2
    chips = lax.axis_size("cuts") // cores
    portion, extended = scatter_with_halo(
        partial.reshape(cores, chips, -1, planes, cells), chips, cores, ITERS
    )
    smoothed = smooth_once(portion, extended)
    factor = gather_in_two(smoothed, chips, cores)
    factor = factor.reshape(ranks, planes, cells)
    factor_half = factor.astype(jnp.bfloat16)
    factor_gram = lax.dot_general(
        factor, factor, (((1, 2), (1, 2)), ((), ())), precision=lax.Precision.HIGH
    )
    products = lax.dot_general(
        data, factor_half, (((2, 3), (1, 2)), ((), ())), preferred_element_type=jnp.float32
    )
    targets = jnp.sum(mixing[None, :, :] * products, axis=1)
    half = ranks // 2
    row = lax.broadcasted_iota(jnp.int32, (half, half), 0)
    col = lax.broadcasted_iota(jnp.int32, (half, half), 1)
    top, off, low = (factor_gram[:half, :half], factor_gram[:half, half:], factor_gram[half:, half:])
    folded = jnp.where(row >= col, top, low)
    folded, off, low_diag, targets = packed_total(
        (folded, off, jnp.sum(jnp.where(row == col, low, 0.0), axis=1), targets), "col"
    )
    top = jnp.where(row >= col, folded, folded.T)
    low = jnp.where(row < col, folded, jnp.where(row > col, folded.T, low_diag[:, None]))
    factor_gram = jnp.concatenate(
        [jnp.concatenate([top, off], axis=1), jnp.concatenate([off.T, low], axis=1)], axis=0
    )
    updated = spd_solve(mix_gram * factor_gram, targets.T)
    return (factor, updated)


def solution(mesh):
    return jax.shard_map(
        per_device,
        mesh=mesh,
        in_specs=(P("cuts", None, "col", None), P(), P()),
        out_specs=(P(None, "col", None), P("cuts", None)),
        check_vma=False,
    )
```

```python
import functools
import jax
import jax.numpy as jnp
from jax import lax
from jax.sharding import PartitionSpec as P
from jax.experimental import pallas as pl
from jax.experimental.pallas import tpu as pltpu

MESH = pl.DeviceIdType.MESH

GRID = 32
ITERS = 3


strength = 0.5
highest = lax.Precision.HIGHEST
low_edge = 1.0
high_edge = 1.0 + 12.0 * strength
centre = (high_edge + low_edge) / 2.0
spread = (high_edge - low_edge) / 2.0


def extended_2(cells, sides, width):
    for axis, dim in sides:
        count = lax.axis_size(axis)
        ends = count - 1
        head = lax.slice_in_dim(cells, 0, width, axis=dim)
        tail = lax.slice_in_dim(cells, cells.shape[dim] - width, cells.shape[dim], axis=dim)
        cells = jnp.concatenate(
            [
                lax.ppermute(tail, axis, [(i, (i + 1) % count) for i in range(ends)]),
                cells,
                lax.ppermute(head, axis, [((i + 1) % count, i) for i in range(ends)]),
            ],
            axis=dim,
        )
    return cells


def _exchange_kernel(axis, other, size, stride, whole, summed, x_ref, o_ref, *scratch):
    if summed:
        send_sem, recv_sem, own_sem, got = scratch
    else:
        (send_sem, recv_sem, own_sem), got = scratch, o_ref
    me = lax.axis_index(axis)
    fixed = lax.axis_index(other)
    pos = (me // stride) % size
    base = me - pos * stride

    def where(peer_pos):
        peer = base + peer_pos * stride
        return (peer, fixed) if axis == "cuts" else (fixed, peer)

    def part(peer_pos):
        return x_ref if whole else x_ref.at[peer_pos]

    barrier = pltpu.get_barrier_semaphore()
    for d in range(1, size):
        pl.semaphore_signal(
            barrier, inc=1, device_id=where((pos + d) % size), device_id_type=MESH
        )
    pl.semaphore_wait(barrier, size - 1)
    own = pltpu.make_async_copy(part(pos), got.at[pos], own_sem)
    own.start()
    copies = []
    for d in range(1, size):
        peer_pos = (pos + d) % size
        copy = pltpu.make_async_remote_copy(
            src_ref=part(peer_pos),
            dst_ref=got.at[pos],
            send_sem=send_sem.at[peer_pos],
            recv_sem=recv_sem.at[pos],
            device_id=where(peer_pos),
            device_id_type=MESH,
        )
        copy.start()
        copies.append(copy)
    for copy in copies:
        copy.wait_send()
    for d in range(1, size):
        source = (pos + size - d) % size
        pltpu.make_async_remote_copy(
            src_ref=part(source),
            dst_ref=got.at[source],
            send_sem=send_sem.at[source],
            recv_sem=recv_sem.at[source],
            device_id=where(source),
            device_id_type=MESH,
        ).wait_recv()
    own.wait()
    if summed:
        total = got[0]
        for slot in range(1, size):
            total = total + got[slot]
        o_ref[...] = total


def exchange(x, axis, key, whole=False, size=None, stride=1, summed=False, space=None):
    other = "col" if axis == "cuts" else "cuts"
    size = size or lax.axis_size(axis)
    shape = (size, *x.shape) if whole else x.shape
    scratch = [
        pltpu.SemaphoreType.DMA((size,)),
        pltpu.SemaphoreType.DMA((size,)),
        pltpu.SemaphoreType.DMA,
    ]
    if summed:
        scratch.append(pltpu.VMEM(shape, x.dtype))
        shape = shape[1:]
    return pl.pallas_call(
        functools.partial(_exchange_kernel, axis, other, size, stride, whole, summed),
        out_shape=jax.ShapeDtypeStruct(shape, x.dtype),
        in_specs=[pl.BlockSpec(memory_space=pltpu.VMEM)],
        out_specs=pl.BlockSpec(memory_space=space or pltpu.VMEM),
        scratch_shapes=scratch,
        compiler_params=pltpu.CompilerParams(collective_id=key, has_side_effects=True),
    )(x)


def _halo_kernel(n, head_ref, tail_ref, below_ref, above_ref, send_sem, recv_sem):
    me = lax.axis_index("col")
    fixed = lax.axis_index("cuts")
    has_left = (me + n - 1) // n
    has_right = 1 - me // (n - 1)
    left, right = (fixed, me - has_left), (fixed, me + has_right)

    def to_left():
        return pltpu.make_async_remote_copy(
            src_ref=head_ref, dst_ref=above_ref, send_sem=send_sem.at[0],
            recv_sem=recv_sem.at[1], device_id=left, device_id_type=MESH,
        )

    def to_right():
        return pltpu.make_async_remote_copy(
            src_ref=tail_ref, dst_ref=below_ref, send_sem=send_sem.at[1],
            recv_sem=recv_sem.at[0], device_id=right, device_id_type=MESH,
        )

    barrier = pltpu.get_barrier_semaphore()

    @pl.when(me > 0)
    def _():
        pl.semaphore_signal(barrier, inc=1, device_id=left, device_id_type=MESH)

    @pl.when(me < n - 1)
    def _():
        pl.semaphore_signal(barrier, inc=1, device_id=right, device_id_type=MESH)

    pl.semaphore_wait(barrier, has_left + has_right)

    @pl.when(me == 0)
    def _():
        below_ref[...] = jnp.zeros_like(below_ref)

    @pl.when(me == n - 1)
    def _():
        above_ref[...] = jnp.zeros_like(above_ref)

    @pl.when(me > 0)
    def _():
        to_left().start()

    @pl.when(me < n - 1)
    def _():
        to_right().start()

    @pl.when(me > 0)
    def _():
        to_left().wait_send()
        pltpu.make_async_remote_copy(
            src_ref=tail_ref, dst_ref=below_ref, send_sem=send_sem.at[1],
            recv_sem=recv_sem.at[0], device_id=left, device_id_type=MESH,
        ).wait_recv()

    @pl.when(me < n - 1)
    def _():
        to_right().wait_send()
        pltpu.make_async_remote_copy(
            src_ref=head_ref, dst_ref=above_ref, send_sem=send_sem.at[0],
            recv_sem=recv_sem.at[1], device_id=right, device_id_type=MESH,
        ).wait_recv()


def with_halo(cells, width):
    n = lax.axis_size("col")
    head = lax.slice_in_dim(cells, 0, width, axis=1)
    tail = lax.slice_in_dim(cells, cells.shape[1] - width, cells.shape[1], axis=1)
    below, above = pl.pallas_call(
        functools.partial(_halo_kernel, n),
        out_shape=(jax.ShapeDtypeStruct(head.shape, head.dtype),) * 2,
        in_specs=[pl.BlockSpec(memory_space=pltpu.VMEM)] * 2,
        out_specs=(pl.BlockSpec(memory_space=pltpu.VMEM),) * 2,
        scratch_shapes=[pltpu.SemaphoreType.DMA((2,)), pltpu.SemaphoreType.DMA((2,))],
        compiler_params=pltpu.CompilerParams(collective_id=3, has_side_effects=True),
    )(head, tail)
    return jnp.concatenate([below, cells, above], axis=1)


def _scatter_halo_kernel(size, stride, n, width, x_ref, o_ref, below_ref, above_ref,
                         got, head_buf, tail_buf, send_sem, recv_sem, own_sem, hsend, hrecv,
                         pair_got, pair_buf, pair_sem):
    me = lax.axis_index("cuts")
    cm = lax.axis_index("col")
    pos = (me // stride) % size
    base = me - pos * stride
    core = me % stride
    partner = me + 1 - 2 * core
    has_left = (cm + n - 1) // n
    has_right = 1 - cm // (n - 1)
    left, right = (me, cm - has_left), (me, cm + has_right)

    def where(peer_pos):
        return (base + peer_pos * stride, cm)

    barrier = pltpu.get_barrier_semaphore()
    for d in range(1, size):
        pl.semaphore_signal(
            barrier, inc=1, device_id=where((pos + d) % size), device_id_type=MESH
        )

    @pl.when(cm > 0)
    def _():
        pl.semaphore_signal(barrier, inc=1, device_id=left, device_id_type=MESH)

    @pl.when(cm < n - 1)
    def _():
        pl.semaphore_signal(barrier, inc=1, device_id=right, device_id_type=MESH)

    pl.semaphore_signal(barrier, inc=1, device_id=(partner, cm), device_id_type=MESH)
    pl.semaphore_wait(barrier, size + has_left + has_right)

    pair = pltpu.make_async_remote_copy(
        src_ref=x_ref.at[1 - core], dst_ref=pair_got, send_sem=pair_sem.at[0],
        recv_sem=pair_sem.at[1], device_id=(partner, cm), device_id_type=MESH,
    )
    pair.start()
    pair.wait_send()
    pair.wait_recv()
    pair_buf[...] = x_ref[core] + pair_got[...]

    @pl.when(cm == 0)
    def _():
        below_ref[...] = jnp.zeros_like(below_ref)

    @pl.when(cm == n - 1)
    def _():
        above_ref[...] = jnp.zeros_like(above_ref)

    own = pltpu.make_async_copy(pair_buf.at[pos], got.at[pos], own_sem)
    own.start()
    copies = []
    for d in range(1, size):
        peer_pos = (pos + d) % size
        copy = pltpu.make_async_remote_copy(
            src_ref=pair_buf.at[peer_pos], dst_ref=got.at[pos],
            send_sem=send_sem.at[peer_pos], recv_sem=recv_sem.at[pos],
            device_id=where(peer_pos), device_id_type=MESH,
        )
        copy.start()
        copies.append(copy)
    for copy in copies:
        copy.wait_send()
    for d in range(1, size):
        source = (pos + size - d) % size
        pltpu.make_async_remote_copy(
            src_ref=pair_buf.at[source], dst_ref=got.at[source],
            send_sem=send_sem.at[source], recv_sem=recv_sem.at[source],
            device_id=where(source), device_id_type=MESH,
        ).wait_recv()
    own.wait()
    total = got[0]
    for slot in range(1, size):
        total = total + got[slot]
    o_ref[...] = total
    planes = total.shape[1]
    head_buf[...] = total[:, :width]
    tail_buf[...] = total[:, planes - width :]

    def to_left():
        return pltpu.make_async_remote_copy(
            src_ref=head_buf, dst_ref=above_ref, send_sem=hsend.at[0],
            recv_sem=hrecv.at[1], device_id=left, device_id_type=MESH,
        )

    def to_right():
        return pltpu.make_async_remote_copy(
            src_ref=tail_buf, dst_ref=below_ref, send_sem=hsend.at[1],
            recv_sem=hrecv.at[0], device_id=right, device_id_type=MESH,
        )

    @pl.when(cm > 0)
    def _():
        to_left().start()

    @pl.when(cm < n - 1)
    def _():
        to_right().start()

    @pl.when(cm > 0)
    def _():
        to_left().wait_send()
        pltpu.make_async_remote_copy(
            src_ref=tail_buf, dst_ref=below_ref, send_sem=hsend.at[1],
            recv_sem=hrecv.at[0], device_id=left, device_id_type=MESH,
        ).wait_recv()

    @pl.when(cm < n - 1)
    def _():
        to_right().wait_send()
        pltpu.make_async_remote_copy(
            src_ref=head_buf, dst_ref=above_ref, send_sem=hsend.at[0],
            recv_sem=hrecv.at[1], device_id=right, device_id_type=MESH,
        ).wait_recv()


def scatter_with_halo(x, size, stride, width):
    n = lax.axis_size("col")
    block = x.shape[2:]
    halo = (block[0], width, *block[2:])
    vmem = pl.BlockSpec(memory_space=pltpu.VMEM)
    portion, below, above = pl.pallas_call(
        functools.partial(_scatter_halo_kernel, size, stride, n, width),
        out_shape=(
            jax.ShapeDtypeStruct(block, x.dtype),
            jax.ShapeDtypeStruct(halo, x.dtype),
            jax.ShapeDtypeStruct(halo, x.dtype),
        ),
        in_specs=[vmem],
        out_specs=(vmem, vmem, vmem),
        scratch_shapes=[
            pltpu.VMEM(x.shape[1:], x.dtype),
            pltpu.VMEM(halo, x.dtype),
            pltpu.VMEM(halo, x.dtype),
            pltpu.SemaphoreType.DMA((size,)),
            pltpu.SemaphoreType.DMA((size,)),
            pltpu.SemaphoreType.DMA,
            pltpu.SemaphoreType.DMA((2,)),
            pltpu.SemaphoreType.DMA((2,)),
            pltpu.VMEM(x.shape[1:], x.dtype),
            pltpu.VMEM(x.shape[1:], x.dtype),
            pltpu.SemaphoreType.DMA((2,)),
        ],
        compiler_params=pltpu.CompilerParams(collective_id=4, has_side_effects=True),
    )(x)
    return portion, jnp.concatenate([below, portion, above], axis=1)


def _gather_kernel(size, stride, x_ref, o_ref, got, send_sem, recv_sem, own_sem, pair_sem):
    me = lax.axis_index("cuts")
    cm = lax.axis_index("col")
    pos = (me // stride) % size
    base = me - pos * stride
    core = me % stride
    partner = me + 1 - 2 * core

    def where(peer_pos):
        return (base + peer_pos * stride, cm)

    barrier = pltpu.get_barrier_semaphore()
    for d in range(1, size):
        pl.semaphore_signal(
            barrier, inc=1, device_id=where((pos + d) % size), device_id_type=MESH
        )
    pl.semaphore_signal(barrier, inc=1, device_id=(partner, cm), device_id_type=MESH)
    pl.semaphore_wait(barrier, size)
    own = pltpu.make_async_copy(x_ref, got.at[pos], own_sem.at[0])
    own.start()
    copies = []
    for d in range(1, size):
        peer_pos = (pos + d) % size
        copy = pltpu.make_async_remote_copy(
            src_ref=x_ref, dst_ref=got.at[pos],
            send_sem=send_sem.at[peer_pos], recv_sem=recv_sem.at[pos],
            device_id=where(peer_pos), device_id_type=MESH,
        )
        copy.start()
        copies.append(copy)
    for copy in copies:
        copy.wait_send()
    for d in range(1, size):
        source = (pos + size - d) % size
        pltpu.make_async_remote_copy(
            src_ref=x_ref, dst_ref=got.at[source],
            send_sem=send_sem.at[source], recv_sem=recv_sem.at[source],
            device_id=where(source), device_id_type=MESH,
        ).wait_recv()
    own.wait()
    mine = pltpu.make_async_copy(got, o_ref.at[core], own_sem.at[1])
    mine.start()
    pair = pltpu.make_async_remote_copy(
        src_ref=got, dst_ref=o_ref.at[core], send_sem=pair_sem.at[0],
        recv_sem=pair_sem.at[1], device_id=(partner, cm), device_id_type=MESH,
    )
    pair.start()
    pair.wait_send()
    pltpu.make_async_remote_copy(
        src_ref=got, dst_ref=o_ref.at[1 - core], send_sem=pair_sem.at[0],
        recv_sem=pair_sem.at[1], device_id=(partner, cm), device_id_type=MESH,
    ).wait_recv()
    mine.wait()


def gather_in_two(x, size, stride):
    return pl.pallas_call(
        functools.partial(_gather_kernel, size, stride),
        out_shape=jax.ShapeDtypeStruct((stride, size, *x.shape), x.dtype),
        in_specs=[pl.BlockSpec(memory_space=pltpu.VMEM)],
        out_specs=pl.BlockSpec(memory_space=pl.ANY),
        scratch_shapes=[
            pltpu.VMEM((size, *x.shape), x.dtype),
            pltpu.SemaphoreType.DMA((size,)),
            pltpu.SemaphoreType.DMA((size,)),
            pltpu.SemaphoreType.DMA((2,)),
            pltpu.SemaphoreType.DMA((2,)),
        ],
        compiler_params=pltpu.CompilerParams(collective_id=1, has_side_effects=True),
    )(x)


def split_up(shard, dim, devices):
    before, after = (shard.shape[:dim], shard.shape[dim + 1 :])
    return jnp.moveaxis(shard.reshape(*before, devices, -1, *after), dim, 0)


def sent_and_summed(shard, axis, dim):
    tiles = split_up(shard, dim, lax.axis_size(axis))
    arrived = exchange(tiles, axis, 0)
    return arrived.sum(axis=0)


def joined_along(tiles, dim):
    dims = list(tiles.shape[1:])
    dims[dim] *= tiles.shape[0]
    return jnp.moveaxis(tiles, 0, dim).reshape(dims)


def from_everyone(shard, axis):
    return exchange(shard, axis, 1 if axis == "cuts" else 2, whole=True)


def gather_directly(shard, axis, dim):
    return joined_along(from_everyone(shard, axis), dim)


def taken_together(shard, axis):
    return from_everyone(shard, axis).sum(axis=0)


def packed_total(arrays, axis):
    line, at, done = (jnp.concatenate([a.reshape(-1) for a in arrays]), 0, [])
    lanes = 128
    rows = -(-line.size // lanes)
    block = jnp.pad(line, (0, rows * lanes - line.size)).reshape(rows, lanes)
    running = taken_together(block, axis).reshape(-1)
    for a in arrays:
        done.append(running[at : at + a.size].reshape(a.shape))
        at += a.size
    return tuple(done)


def operate(extended):
    channels, depth, cells = extended.shape
    edge = GRID
    interior = extended[:, 1:-1]
    column = jnp.arange(cells, dtype=jnp.int32) % edge
    has_left = (column > 0).astype(jnp.float32)
    has_right = (column < edge - 1).astype(jnp.float32)
    left_part = jnp.pad(interior, ((0, 0), (0, 0), (1, 0)))[:, :, :-1] * has_left
    right_part = jnp.pad(interior, ((0, 0), (0, 0), (0, 1)))[:, :, 1:] * has_right
    upper_part = jnp.pad(interior, ((0, 0), (0, 0), (edge, 0)))[:, :, :-edge]
    lower_part = jnp.pad(interior, ((0, 0), (0, 0), (0, edge)))[:, :, edge:]
    neighbours = extended[:, 2:] + extended[:, :-2]
    neighbours = neighbours + left_part + right_part + upper_part + lower_part
    return interior + strength * (6.0 * interior - neighbours)


def smooth_once(source, extended):
    planes = source.shape[1]
    first_plane = lax.axis_index("col") * planes - ITERS
    total_planes = planes * lax.axis_size("col")
    levels = first_plane + jnp.arange(planes + 2 * ITERS, dtype=jnp.int32)
    inside = ((levels >= 0) & (levels < total_planes)).astype(jnp.float32)[None, :, None]
    solution = jnp.zeros_like(source)
    residual = extended
    direction = extended / centre
    ratio = spread / centre
    for iteration in range(ITERS):
        margin = ITERS - iteration
        solution = solution + direction[:, margin : margin + planes]
        window = inside[:, iteration + 1 : iteration + 1 + planes + 2 * (margin - 1)]
        residual = (residual[:, 1:-1] - operate(direction)) * window
        ratio_next = 1.0 / (2.0 * centre / spread - ratio)
        direction = ratio_next * ratio * direction[:, 1:-1] + 2.0 * ratio_next / spread * residual
        ratio = ratio_next
    return solution + direction


def _eliminate(m_ref, b_ref, o_ref):
    m = m_ref[...]
    b = b_ref[...]
    n = m.shape[0]
    ri = lax.broadcasted_iota(jnp.int32, m.shape, 0)
    ci = lax.broadcasted_iota(jnp.int32, m.shape, 1)
    rb = lax.broadcasted_iota(jnp.int32, b.shape, 0)

    def pick_row(x, rows, p):
        return jnp.sum(jnp.where(rows == p, x, 0.0), axis=0, keepdims=True)

    def pick_col(x, p):
        return jnp.sum(jnp.where(ci[: x.shape[0]] == p, x, 0.0), axis=1, keepdims=True)

    def step(j, carry):
        m, b = carry
        p, q = 2 * j, 2 * j + 1
        c0, c1 = pick_col(m, p), pick_col(m, q)
        r0, r1 = pick_row(m, ri, p), pick_row(m, ri, q)
        s0, s1 = pick_row(b, rb, p), pick_row(b, rb, q)
        a, e = pick_col(r0, p), pick_col(r0, q)
        c, d = pick_col(r1, p), pick_col(r1, q)
        scale = 1.0 / (a * d - e * c)
        n0, n1 = (d * r0 - e * r1) * scale, (a * r1 - c * r0) * scale
        t0, t1 = (d * s0 - e * s1) * scale, (a * s1 - c * s0) * scale
        m = jnp.where(ri == p, n0, jnp.where(ri == q, n1, m - c0 * n0 - c1 * n1))
        b = jnp.where(rb == p, t0, jnp.where(rb == q, t1, b - c0 * t0 - c1 * t1))
        return m, b

    x = lax.fori_loop(0, n // 2, step, (m, b), unroll=True)[1]
    if o_ref.shape == b.shape:
        o_ref[...] = x.astype(o_ref.dtype)
    else:
        o_ref[...] = jnp.sum(jnp.where(ri == ci, x, 0.0), axis=0, keepdims=True)


def spd_solve(m, b, dtype=None):
    shape = (1, b.shape[0]) if b.shape[1] == 1 else b.shape
    return pl.pallas_call(
        _eliminate, out_shape=jax.ShapeDtypeStruct(shape, dtype or b.dtype)
    )(m, b)


def per_device(data, weights, mixing):
    local_scans, ranks, planes, cells = data.shape
    mix_gram = jnp.dot(mixing.T, mixing, precision=lax.Precision.HIGH)
    weight_gram = jnp.dot(weights.T, weights, precision=lax.Precision.HIGH)
    own_weights = lax.dynamic_slice_in_dim(
        weights, lax.axis_index("cuts") * local_scans, local_scans, 0
    )
    scaled = (mixing.T[None, :, :] * own_weights[:, :, None]).transpose(1, 0, 2)
    coefficients = spd_solve(
        mix_gram * weight_gram, scaled.reshape(ranks, local_scans * ranks), jnp.bfloat16
    )
    partial = lax.dot_general(
        coefficients, data.reshape(-1, planes, cells), (((1,), (0,)), ((), ())), preferred_element_type=jnp.float32
    )
    cores = 2
    chips = lax.axis_size("cuts") // cores
    portion, extended = scatter_with_halo(
        partial.reshape(cores, chips, -1, planes, cells), chips, cores, ITERS
    )
    smoothed = smooth_once(portion, extended)
    factor = gather_in_two(smoothed, chips, cores)
    factor = factor.reshape(ranks, planes, cells)
    factor_half = factor.astype(jnp.bfloat16)
    factor_gram = lax.dot_general(
        factor, factor, (((1, 2), (1, 2)), ((), ())), precision=lax.Precision.HIGH
    )
    products = lax.dot_general(
        data, factor_half, (((2, 3), (1, 2)), ((), ())), preferred_element_type=jnp.float32
    )
    targets = jnp.sum(mixing[None, :, :] * products, axis=1)
    half = ranks // 2
    row = lax.broadcasted_iota(jnp.int32, (half, half), 0)
    col = lax.broadcasted_iota(jnp.int32, (half, half), 1)
    top, off, low = (factor_gram[:half, :half], factor_gram[:half, half:], factor_gram[half:, half:])
    folded = jnp.where(row >= col, top, low)
    folded, off, low_diag, targets = packed_total(
        (folded, off, jnp.sum(jnp.where(row == col, low, 0.0), axis=1), targets), "col"
    )
    top = jnp.where(row >= col, folded, folded.T)
    low = jnp.where(row < col, folded, jnp.where(row > col, folded.T, low_diag[:, None]))
    factor_gram = jnp.concatenate(
        [jnp.concatenate([top, off], axis=1), jnp.concatenate([off.T, low], axis=1)], axis=0
    )
    updated = spd_solve(mix_gram * factor_gram, targets.T)
    return (factor, updated)


def solution(mesh):
    return jax.shard_map(
        per_device,
        mesh=mesh,
        in_specs=(P("cuts", None, "col", None), P(), P()),
        out_specs=(P(None, "col", None), P("cuts", None)),
        check_vma=False,
    )
```

```python
import functools
import jax
import jax.numpy as jnp
from jax import lax
from jax.sharding import PartitionSpec as P
from jax.experimental import pallas as pl
from jax.experimental.pallas import tpu as pltpu

MESH = pl.DeviceIdType.MESH

GRID = 32
ITERS = 3


strength = 0.5
highest = lax.Precision.HIGHEST
low_edge = 1.0
high_edge = 1.0 + 12.0 * strength
centre = (high_edge + low_edge) / 2.0
spread = (high_edge - low_edge) / 2.0


def extended_2(cells, sides, width):
    for axis, dim in sides:
        count = lax.axis_size(axis)
        ends = count - 1
        head = lax.slice_in_dim(cells, 0, width, axis=dim)
        tail = lax.slice_in_dim(cells, cells.shape[dim] - width, cells.shape[dim], axis=dim)
        cells = jnp.concatenate(
            [
                lax.ppermute(tail, axis, [(i, (i + 1) % count) for i in range(ends)]),
                cells,
                lax.ppermute(head, axis, [((i + 1) % count, i) for i in range(ends)]),
            ],
            axis=dim,
        )
    return cells


def _exchange_kernel(axis, other, size, stride, whole, summed, x_ref, o_ref, *scratch):
    if summed:
        send_sem, recv_sem, own_sem, got = scratch
    else:
        (send_sem, recv_sem, own_sem), got = scratch, o_ref
    me = lax.axis_index(axis)
    fixed = lax.axis_index(other)
    pos = (me // stride) % size
    base = me - pos * stride

    def where(peer_pos):
        peer = base + peer_pos * stride
        return (peer, fixed) if axis == "cuts" else (fixed, peer)

    def part(peer_pos):
        return x_ref if whole else x_ref.at[peer_pos]

    barrier = pltpu.get_barrier_semaphore()
    for d in range(1, size):
        pl.semaphore_signal(
            barrier, inc=1, device_id=where((pos + d) % size), device_id_type=MESH
        )
    pl.semaphore_wait(barrier, size - 1)
    own = pltpu.make_async_copy(part(pos), got.at[pos], own_sem)
    own.start()
    copies = []
    for d in range(1, size):
        peer_pos = (pos + d) % size
        copy = pltpu.make_async_remote_copy(
            src_ref=part(peer_pos),
            dst_ref=got.at[pos],
            send_sem=send_sem.at[peer_pos],
            recv_sem=recv_sem.at[pos],
            device_id=where(peer_pos),
            device_id_type=MESH,
        )
        copy.start()
        copies.append(copy)
    for copy in copies:
        copy.wait_send()
    for d in range(1, size):
        source = (pos + size - d) % size
        pltpu.make_async_remote_copy(
            src_ref=part(source),
            dst_ref=got.at[source],
            send_sem=send_sem.at[source],
            recv_sem=recv_sem.at[source],
            device_id=where(source),
            device_id_type=MESH,
        ).wait_recv()
    own.wait()
    if summed:
        total = got[0]
        for slot in range(1, size):
            total = total + got[slot]
        o_ref[...] = total


def exchange(x, axis, key, whole=False, size=None, stride=1, summed=False, space=None):
    other = "col" if axis == "cuts" else "cuts"
    size = size or lax.axis_size(axis)
    shape = (size, *x.shape) if whole else x.shape
    scratch = [
        pltpu.SemaphoreType.DMA((size,)),
        pltpu.SemaphoreType.DMA((size,)),
        pltpu.SemaphoreType.DMA,
    ]
    if summed:
        scratch.append(pltpu.VMEM(shape, x.dtype))
        shape = shape[1:]
    return pl.pallas_call(
        functools.partial(_exchange_kernel, axis, other, size, stride, whole, summed),
        out_shape=jax.ShapeDtypeStruct(shape, x.dtype),
        in_specs=[pl.BlockSpec(memory_space=pltpu.VMEM)],
        out_specs=pl.BlockSpec(memory_space=space or pltpu.VMEM),
        scratch_shapes=scratch,
        compiler_params=pltpu.CompilerParams(collective_id=key, has_side_effects=True),
    )(x)


def _halo_kernel(n, head_ref, tail_ref, below_ref, above_ref, send_sem, recv_sem):
    me = lax.axis_index("col")
    fixed = lax.axis_index("cuts")
    has_left = (me + n - 1) // n
    has_right = 1 - me // (n - 1)
    left, right = (fixed, me - has_left), (fixed, me + has_right)

    def to_left():
        return pltpu.make_async_remote_copy(
            src_ref=head_ref, dst_ref=above_ref, send_sem=send_sem.at[0],
            recv_sem=recv_sem.at[1], device_id=left, device_id_type=MESH,
        )

    def to_right():
        return pltpu.make_async_remote_copy(
            src_ref=tail_ref, dst_ref=below_ref, send_sem=send_sem.at[1],
            recv_sem=recv_sem.at[0], device_id=right, device_id_type=MESH,
        )

    barrier = pltpu.get_barrier_semaphore()

    @pl.when(me > 0)
    def _():
        pl.semaphore_signal(barrier, inc=1, device_id=left, device_id_type=MESH)

    @pl.when(me < n - 1)
    def _():
        pl.semaphore_signal(barrier, inc=1, device_id=right, device_id_type=MESH)

    pl.semaphore_wait(barrier, has_left + has_right)

    @pl.when(me == 0)
    def _():
        below_ref[...] = jnp.zeros_like(below_ref)

    @pl.when(me == n - 1)
    def _():
        above_ref[...] = jnp.zeros_like(above_ref)

    @pl.when(me > 0)
    def _():
        to_left().start()

    @pl.when(me < n - 1)
    def _():
        to_right().start()

    @pl.when(me > 0)
    def _():
        to_left().wait_send()
        pltpu.make_async_remote_copy(
            src_ref=tail_ref, dst_ref=below_ref, send_sem=send_sem.at[1],
            recv_sem=recv_sem.at[0], device_id=left, device_id_type=MESH,
        ).wait_recv()

    @pl.when(me < n - 1)
    def _():
        to_right().wait_send()
        pltpu.make_async_remote_copy(
            src_ref=head_ref, dst_ref=above_ref, send_sem=send_sem.at[0],
            recv_sem=recv_sem.at[1], device_id=right, device_id_type=MESH,
        ).wait_recv()


def with_halo(cells, width):
    n = lax.axis_size("col")
    head = lax.slice_in_dim(cells, 0, width, axis=1)
    tail = lax.slice_in_dim(cells, cells.shape[1] - width, cells.shape[1], axis=1)
    below, above = pl.pallas_call(
        functools.partial(_halo_kernel, n),
        out_shape=(jax.ShapeDtypeStruct(head.shape, head.dtype),) * 2,
        in_specs=[pl.BlockSpec(memory_space=pltpu.VMEM)] * 2,
        out_specs=(pl.BlockSpec(memory_space=pltpu.VMEM),) * 2,
        scratch_shapes=[pltpu.SemaphoreType.DMA((2,)), pltpu.SemaphoreType.DMA((2,))],
        compiler_params=pltpu.CompilerParams(collective_id=3, has_side_effects=True),
    )(head, tail)
    return jnp.concatenate([below, cells, above], axis=1)


def _scatter_halo_kernel(size, stride, n, width, x_ref, o_ref, below_ref, above_ref,
                         got, head_buf, tail_buf, send_sem, recv_sem, own_sem, hsend, hrecv,
                         pair_got, pair_buf, pair_sem):
    me = lax.axis_index("cuts")
    cm = lax.axis_index("col")
    pos = (me // stride) % size
    base = me - pos * stride
    core = me % stride
    partner = me + 1 - 2 * core
    has_left = (cm + n - 1) // n
    has_right = 1 - cm // (n - 1)
    left, right = (me, cm - has_left), (me, cm + has_right)

    def where(peer_pos):
        return (base + peer_pos * stride, cm)

    barrier = pltpu.get_barrier_semaphore()
    for d in range(1, size):
        pl.semaphore_signal(
            barrier, inc=1, device_id=where((pos + d) % size), device_id_type=MESH
        )

    @pl.when(cm > 0)
    def _():
        pl.semaphore_signal(barrier, inc=1, device_id=left, device_id_type=MESH)

    @pl.when(cm < n - 1)
    def _():
        pl.semaphore_signal(barrier, inc=1, device_id=right, device_id_type=MESH)

    pl.semaphore_signal(barrier, inc=1, device_id=(partner, cm), device_id_type=MESH)
    pl.semaphore_wait(barrier, size + has_left + has_right)

    pair = pltpu.make_async_remote_copy(
        src_ref=x_ref.at[1 - core], dst_ref=pair_got, send_sem=pair_sem.at[0],
        recv_sem=pair_sem.at[1], device_id=(partner, cm), device_id_type=MESH,
    )
    pair.start()
    pair.wait_send()
    pair.wait_recv()
    pair_buf[...] = x_ref[core] + pair_got[...]

    @pl.when(cm == 0)
    def _():
        below_ref[...] = jnp.zeros_like(below_ref)

    @pl.when(cm == n - 1)
    def _():
        above_ref[...] = jnp.zeros_like(above_ref)

    own = pltpu.make_async_copy(pair_buf.at[pos], got.at[pos], own_sem)
    own.start()
    copies = []
    for d in range(1, size):
        peer_pos = (pos + d) % size
        copy = pltpu.make_async_remote_copy(
            src_ref=pair_buf.at[peer_pos], dst_ref=got.at[pos],
            send_sem=send_sem.at[peer_pos], recv_sem=recv_sem.at[pos],
            device_id=where(peer_pos), device_id_type=MESH,
        )
        copy.start()
        copies.append(copy)
    for copy in copies:
        copy.wait_send()
    for d in range(1, size):
        source = (pos + size - d) % size
        pltpu.make_async_remote_copy(
            src_ref=pair_buf.at[source], dst_ref=got.at[source],
            send_sem=send_sem.at[source], recv_sem=recv_sem.at[source],
            device_id=where(source), device_id_type=MESH,
        ).wait_recv()
    own.wait()
    total = got[0]
    for slot in range(1, size):
        total = total + got[slot]
    o_ref[...] = total
    planes = total.shape[1]
    head_buf[...] = total[:, :width]
    tail_buf[...] = total[:, planes - width :]

    def to_left():
        return pltpu.make_async_remote_copy(
            src_ref=head_buf, dst_ref=above_ref, send_sem=hsend.at[0],
            recv_sem=hrecv.at[1], device_id=left, device_id_type=MESH,
        )

    def to_right():
        return pltpu.make_async_remote_copy(
            src_ref=tail_buf, dst_ref=below_ref, send_sem=hsend.at[1],
            recv_sem=hrecv.at[0], device_id=right, device_id_type=MESH,
        )

    @pl.when(cm > 0)
    def _():
        to_left().start()

    @pl.when(cm < n - 1)
    def _():
        to_right().start()

    @pl.when(cm > 0)
    def _():
        to_left().wait_send()
        pltpu.make_async_remote_copy(
            src_ref=tail_buf, dst_ref=below_ref, send_sem=hsend.at[1],
            recv_sem=hrecv.at[0], device_id=left, device_id_type=MESH,
        ).wait_recv()

    @pl.when(cm < n - 1)
    def _():
        to_right().wait_send()
        pltpu.make_async_remote_copy(
            src_ref=head_buf, dst_ref=above_ref, send_sem=hsend.at[0],
            recv_sem=hrecv.at[1], device_id=right, device_id_type=MESH,
        ).wait_recv()


def scatter_with_halo(x, size, stride, width):
    n = lax.axis_size("col")
    block = x.shape[2:]
    halo = (block[0], width, *block[2:])
    vmem = pl.BlockSpec(memory_space=pltpu.VMEM)
    portion, below, above = pl.pallas_call(
        functools.partial(_scatter_halo_kernel, size, stride, n, width),
        out_shape=(
            jax.ShapeDtypeStruct(block, x.dtype),
            jax.ShapeDtypeStruct(halo, x.dtype),
            jax.ShapeDtypeStruct(halo, x.dtype),
        ),
        in_specs=[vmem],
        out_specs=(vmem, vmem, vmem),
        scratch_shapes=[
            pltpu.VMEM(x.shape[1:], x.dtype),
            pltpu.VMEM(halo, x.dtype),
            pltpu.VMEM(halo, x.dtype),
            pltpu.SemaphoreType.DMA((size,)),
            pltpu.SemaphoreType.DMA((size,)),
            pltpu.SemaphoreType.DMA,
            pltpu.SemaphoreType.DMA((2,)),
            pltpu.SemaphoreType.DMA((2,)),
            pltpu.VMEM(x.shape[1:], x.dtype),
            pltpu.VMEM(x.shape[1:], x.dtype),
            pltpu.SemaphoreType.DMA((2,)),
        ],
        compiler_params=pltpu.CompilerParams(collective_id=4, has_side_effects=True),
    )(x)
    return portion, jnp.concatenate([below, portion, above], axis=1)


def _gather_kernel(size, stride, x_ref, o_ref, got, send_sem, recv_sem, own_sem, pair_sem):
    me = lax.axis_index("cuts")
    cm = lax.axis_index("col")
    pos = (me // stride) % size
    base = me - pos * stride
    core = me % stride
    partner = me + 1 - 2 * core

    def where(peer_pos):
        return (base + peer_pos * stride, cm)

    barrier = pltpu.get_barrier_semaphore()
    for d in range(1, size):
        pl.semaphore_signal(
            barrier, inc=1, device_id=where((pos + d) % size), device_id_type=MESH
        )
    pl.semaphore_signal(barrier, inc=1, device_id=(partner, cm), device_id_type=MESH)
    pl.semaphore_wait(barrier, size)
    own = pltpu.make_async_copy(x_ref, got.at[pos], own_sem.at[0])
    own.start()
    copies = []
    for d in range(1, size):
        peer_pos = (pos + d) % size
        copy = pltpu.make_async_remote_copy(
            src_ref=x_ref, dst_ref=got.at[pos],
            send_sem=send_sem.at[peer_pos], recv_sem=recv_sem.at[pos],
            device_id=where(peer_pos), device_id_type=MESH,
        )
        copy.start()
        copies.append(copy)
    for copy in copies:
        copy.wait_send()
    for d in range(1, size):
        source = (pos + size - d) % size
        pltpu.make_async_remote_copy(
            src_ref=x_ref, dst_ref=got.at[source],
            send_sem=send_sem.at[source], recv_sem=recv_sem.at[source],
            device_id=where(source), device_id_type=MESH,
        ).wait_recv()
    own.wait()
    mine = pltpu.make_async_copy(got, o_ref.at[core], own_sem.at[1])
    mine.start()
    pair = pltpu.make_async_remote_copy(
        src_ref=got, dst_ref=o_ref.at[core], send_sem=pair_sem.at[0],
        recv_sem=pair_sem.at[1], device_id=(partner, cm), device_id_type=MESH,
    )
    pair.start()
    pair.wait_send()
    pltpu.make_async_remote_copy(
        src_ref=got, dst_ref=o_ref.at[1 - core], send_sem=pair_sem.at[0],
        recv_sem=pair_sem.at[1], device_id=(partner, cm), device_id_type=MESH,
    ).wait_recv()
    mine.wait()


def gather_in_two(x, size, stride):
    return pl.pallas_call(
        functools.partial(_gather_kernel, size, stride),
        out_shape=jax.ShapeDtypeStruct((stride, size, *x.shape), x.dtype),
        in_specs=[pl.BlockSpec(memory_space=pltpu.VMEM)],
        out_specs=pl.BlockSpec(memory_space=pl.ANY),
        scratch_shapes=[
            pltpu.VMEM((size, *x.shape), x.dtype),
            pltpu.SemaphoreType.DMA((size,)),
            pltpu.SemaphoreType.DMA((size,)),
            pltpu.SemaphoreType.DMA((2,)),
            pltpu.SemaphoreType.DMA((2,)),
        ],
        compiler_params=pltpu.CompilerParams(collective_id=1, has_side_effects=True),
    )(x)


def split_up(shard, dim, devices):
    before, after = (shard.shape[:dim], shard.shape[dim + 1 :])
    return jnp.moveaxis(shard.reshape(*before, devices, -1, *after), dim, 0)


def sent_and_summed(shard, axis, dim):
    tiles = split_up(shard, dim, lax.axis_size(axis))
    arrived = exchange(tiles, axis, 0)
    return arrived.sum(axis=0)


def joined_along(tiles, dim):
    dims = list(tiles.shape[1:])
    dims[dim] *= tiles.shape[0]
    return jnp.moveaxis(tiles, 0, dim).reshape(dims)


def from_everyone(shard, axis):
    return exchange(shard, axis, 1 if axis == "cuts" else 2, whole=True)


def gather_directly(shard, axis, dim):
    return joined_along(from_everyone(shard, axis), dim)


def taken_together(shard, axis):
    return from_everyone(shard, axis).sum(axis=0)


def packed_total(arrays, axis):
    line, at, done = (jnp.concatenate([a.reshape(-1) for a in arrays]), 0, [])
    lanes = 128
    rows = -(-line.size // lanes)
    block = jnp.pad(line, (0, rows * lanes - line.size)).reshape(rows, lanes)
    running = taken_together(block, axis).reshape(-1)
    for a in arrays:
        done.append(running[at : at + a.size].reshape(a.shape))
        at += a.size
    return tuple(done)


def operate(extended):
    channels, depth, cells = extended.shape
    edge = GRID
    interior = extended[:, 1:-1]
    column = jnp.arange(cells, dtype=jnp.int32) % edge
    has_left = (column > 0).astype(jnp.float32)
    has_right = (column < edge - 1).astype(jnp.float32)
    left_part = jnp.pad(interior, ((0, 0), (0, 0), (1, 0)))[:, :, :-1] * has_left
    right_part = jnp.pad(interior, ((0, 0), (0, 0), (0, 1)))[:, :, 1:] * has_right
    upper_part = jnp.pad(interior, ((0, 0), (0, 0), (edge, 0)))[:, :, :-edge]
    lower_part = jnp.pad(interior, ((0, 0), (0, 0), (0, edge)))[:, :, edge:]
    neighbours = extended[:, 2:] + extended[:, :-2]
    neighbours = neighbours + left_part + right_part + upper_part + lower_part
    return interior + strength * (6.0 * interior - neighbours)


def smooth_once(source, extended):
    planes = source.shape[1]
    first_plane = lax.axis_index("col") * planes - ITERS
    total_planes = planes * lax.axis_size("col")
    levels = first_plane + jnp.arange(planes + 2 * ITERS, dtype=jnp.int32)
    inside = ((levels >= 0) & (levels < total_planes)).astype(jnp.float32)[None, :, None]
    solution = jnp.zeros_like(source)
    residual = extended
    direction = extended / centre
    ratio = spread / centre
    for iteration in range(ITERS):
        margin = ITERS - iteration
        solution = solution + direction[:, margin : margin + planes]
        window = inside[:, iteration + 1 : iteration + 1 + planes + 2 * (margin - 1)]
        residual = (residual[:, 1:-1] - operate(direction)) * window
        ratio_next = 1.0 / (2.0 * centre / spread - ratio)
        direction = ratio_next * ratio * direction[:, 1:-1] + 2.0 * ratio_next / spread * residual
        ratio = ratio_next
    return solution + direction


def _eliminate(m_ref, b_ref, o_ref):
    m = m_ref[...]
    b = b_ref[...]
    n = m.shape[0]
    ri = lax.broadcasted_iota(jnp.int32, m.shape, 0)
    ci = lax.broadcasted_iota(jnp.int32, m.shape, 1)
    if b.shape[0] == 1:
        b = jnp.sum(jnp.where(ri == ci, b, 0.0), axis=1, keepdims=True)
    rb = lax.broadcasted_iota(jnp.int32, b.shape, 0)

    def pick_row(x, rows, p):
        return jnp.sum(jnp.where(rows == p, x, 0.0), axis=0, keepdims=True)

    def pick_col(x, p):
        return jnp.sum(jnp.where(ci[: x.shape[0]] == p, x, 0.0), axis=1, keepdims=True)

    def step(j, carry):
        m, b = carry
        p, q = 2 * j, 2 * j + 1
        c0, c1 = pick_col(m, p), pick_col(m, q)
        r0, r1 = pick_row(m, ri, p), pick_row(m, ri, q)
        s0, s1 = pick_row(b, rb, p), pick_row(b, rb, q)
        a, e = pick_col(r0, p), pick_col(r0, q)
        c, d = pick_col(r1, p), pick_col(r1, q)
        scale = 1.0 / (a * d - e * c)
        n0, n1 = (d * r0 - e * r1) * scale, (a * r1 - c * r0) * scale
        t0, t1 = (d * s0 - e * s1) * scale, (a * s1 - c * s0) * scale
        m = jnp.where(ri == p, n0, jnp.where(ri == q, n1, m - c0 * n0 - c1 * n1))
        b = jnp.where(rb == p, t0, jnp.where(rb == q, t1, b - c0 * t0 - c1 * t1))
        return m, b

    x = lax.fori_loop(0, n // 2, step, (m, b), unroll=True)[1]
    if o_ref.shape == b.shape:
        o_ref[...] = x.astype(o_ref.dtype)
    else:
        o_ref[...] = jnp.sum(jnp.where(ri == ci, x, 0.0), axis=0, keepdims=True)


def spd_solve(m, b, dtype=None):
    shape = b.shape if b.shape[0] == 1 else b.shape
    return pl.pallas_call(
        _eliminate, out_shape=jax.ShapeDtypeStruct(shape, dtype or b.dtype)
    )(m, b)


def per_device(data, weights, mixing):
    local_scans, ranks, planes, cells = data.shape
    mix_gram = jnp.dot(mixing.T, mixing, precision=highest)
    weight_gram = jnp.dot(weights.T, weights, precision=highest)
    own_weights = lax.dynamic_slice_in_dim(
        weights, lax.axis_index("cuts") * local_scans, local_scans, 0
    )
    scaled = (mixing.T[None, :, :] * own_weights[:, :, None]).transpose(1, 0, 2)
    coefficients = spd_solve(
        mix_gram * weight_gram, scaled.reshape(ranks, local_scans * ranks), jnp.bfloat16
    )
    partial = lax.dot_general(
        coefficients, data.reshape(-1, planes, cells), (((1,), (0,)), ((), ())), preferred_element_type=jnp.float32
    )
    cores = 2
    chips = lax.axis_size("cuts") // cores
    portion, extended = scatter_with_halo(
        partial.reshape(cores, chips, -1, planes, cells), chips, cores, ITERS
    )
    smoothed = smooth_once(portion, extended)
    factor = gather_in_two(smoothed, chips, cores)
    factor = factor.reshape(ranks, planes, cells)
    factor_half = factor.astype(jnp.bfloat16)
    factor_gram = lax.dot_general(
        factor, factor, (((1, 2), (1, 2)), ((), ())), precision=lax.Precision.HIGH
    )
    products = lax.dot_general(
        data, factor_half, (((2, 3), (1, 2)), ((), ())), preferred_element_type=jnp.float32
    )
    targets = jnp.sum(mixing[None, :, :] * products, axis=1)
    half = ranks // 2
    row = lax.broadcasted_iota(jnp.int32, (half, half), 0)
    col = lax.broadcasted_iota(jnp.int32, (half, half), 1)
    top, off, low = (factor_gram[:half, :half], factor_gram[:half, half:], factor_gram[half:, half:])
    folded = jnp.where(row >= col, top, low)
    folded, off, low_diag, targets = packed_total(
        (folded, off, jnp.sum(jnp.where(row == col, low, 0.0), axis=1), targets), "col"
    )
    top = jnp.where(row >= col, folded, folded.T)
    low = jnp.where(row < col, folded, jnp.where(row > col, folded.T, low_diag[:, None]))
    factor_gram = jnp.concatenate(
        [jnp.concatenate([top, off], axis=1), jnp.concatenate([off.T, low], axis=1)], axis=0
    )
    updated = spd_solve(mix_gram * factor_gram, targets)
    return (factor, updated)


def solution(mesh):
    return jax.shard_map(
        per_device,
        mesh=mesh,
        in_specs=(P("cuts", None, "col", None), P(), P()),
        out_specs=(P(None, "col", None), P("cuts", None)),
        check_vma=False,
    )
```
